256 devices in a mesh: group: 16 (over z_lo, x), expert: 16 (over y, z_hi, core).
Axes of the slice: x: 4, y: 4, z: 8 (z_hi: 2, z_lo: 4; z = z_hi * 4 + z_lo), core: 2. Of those that a mesh axis runs over, the one named last changes fastest.
Arguments:
- query_nope: bfloat16 [2048, 16, 128], P('group', 'expert'), may hold values from -6 to 6
- query_rope: bfloat16 [2048, 16, 64], P('group', 'expert'), may hold values from -8 to 8
- absorb_weight: bfloat16 [16, 128, 512], P('expert'), may hold values from -0.5 to 0.5
- value_weight: bfloat16 [16, 512, 128], P('expert'), may hold values from -1 to 1
- output_weight: bfloat16 [2048, 2048], P('expert'), may hold values from -0.25 to 0.25
- cache_latent: bfloat16 [32, 1024, 512], P('group'), may hold values from -6 to 6
- cache_rope: bfloat16 [32, 1024, 64], P('group'), may hold values from -8 to 8
- node_length: int32 [32], P('group'), may hold values from 128 to 1024, as said below
- new_latent: bfloat16 [2048, 512], P('group'), may hold values from -6 to 6
- new_rope: bfloat16 [2048, 64], P('group'), may hold values from -8 to 8
- parent_node: int32 [32], replicated, may hold values from 0 to 31, as said below
- leaf_node: int32 [256], replicated, may hold values from 0 to 31, as said below
- residual: bfloat16 [2048, 2048], P(('group', 'expert')), may hold values from -6 to 6
- norm_gain: bfloat16 [2048], replicated, may hold values from 0.5 to 1.5
- router_weight: bfloat16 [2048, 64], replicated, may hold values from -0.25 to 0.25
- routes: int32 [2048, 6], P(('group', 'expert')), may hold values from 0 to 63, all different within a row; in each aligned block of 8 rows (0 to 7, 8 to 15, ...) at most 2 rows name the same one
- expert_gate: bfloat16 [256, 2048, 352], P(('group', 'expert')), may hold values from -0.125 to 0.125
- expert_up: bfloat16 [256, 2048, 352], P(('group', 'expert')), may hold values from -0.125 to 0.125
- expert_down: bfloat16 [256, 352, 2048], P(('group', 'expert')), may hold values from -0.15625 to 0.15625
- shared_gate: bfloat16 [2048, 2816], P(None, 'group'), may hold values from -0.125 to 0.125
- shared_up: bfloat16 [2048, 2816], P(None, 'group'), may hold values from -0.125 to 0.125
- shared_down: bfloat16 [2816, 2048], P('group'), may hold values from -0.109375 to 0.109375
Outputs:
- layer_out: bfloat16 [2048, 2048], P(('group', 'expert'))
The draws below stay inside these ranges and needn't reach their ends.
Inputs may be any that keep to these rules, and one draw needn't show every extreme that they name: `parent_node`: a root is its own parent; every other node's parent is one level nearer the root in a tree of three levels. leaf_node[r], its parent and that node's parent are three different nodes, the path from a leaf to a root. `node_length`: some node holds all 1024 slots. `routes`: the 6 experts of a token differ; in the 8 rows of one device no expert is named more than 2 times.
All inputs are finite; a program needn't handle non-finite values.
Results may differ from the reference program's by a relative error of at most 0.022.
Values may be sent and summed in bfloat16 or wider, within the bound.
A program may use at most 128 MiB of HBM per device.

```python
import math
import jax
import jax.numpy as jnp
import numpy as np
from jax import lax

D = 2048
H = 16
NOPE = 128
ROPE = 64
LAT = 512
VDIM = 128
EXPERTS = 64
MOE_FF = 1408
TOPK = 6
SHARED_FF = 2816
QT = 8
FF_BLOCKS = 4
LVL = 1024
NODES = 32
REQUESTS = 256
TOKENS = 2048
TOK_DEV = 8
FF_BLK = 352
CAP = 2
N_GROUP = 16
N_EXPERT = 16


def tree_tables(key):
    key_list = jax.random.split(jax.random.fold_in(key, 7), 4)
    ordering = jax.random.permutation(key_list[0], NODES).astype(jnp.int32)
    root_count = NODES // 8
    middles = NODES // 4
    leaves = NODES - root_count - middles
    own_ids = jnp.arange(NODES, dtype=jnp.int32)
    rank_of = jnp.zeros((NODES,), jnp.int32).at[ordering].set(own_ids)
    mid_parent = ordering[jax.random.randint(key_list[1], (NODES,), 0, root_count)]
    leaf_parent = ordering[root_count + jax.random.randint(key_list[2], (NODES,), 0, middles)]
    parents = jnp.where(rank_of < root_count, own_ids, jnp.where(rank_of < root_count + middles, mid_parent, leaf_parent))
    leaf_ids = ordering[root_count + middles + jax.random.randint(key_list[3], (REQUESTS,), 0, leaves)]
    return (parents.astype(jnp.int32), leaf_ids.astype(jnp.int32))


def draw_parent_node(key, part):
    return tree_tables(key)[0]


def draw_leaf_node(key, part):
    return tree_tables(key)[1]


def draw_node_length(key, part):
    key_list = jax.random.split(jax.random.fold_in(key, 51), 2)
    lengths = jax.random.randint(key_list[0], (NODES,), LVL // 8, LVL + 1)
    longest = jax.random.randint(key_list[1], (), 0, NODES)
    return jnp.where(jnp.arange(NODES, dtype=jnp.int32) == longest, LVL, lengths).astype(jnp.int32)


def draw_query_rope(key, part):
    jitter = jax.random.normal(jax.random.fold_in(key, 21), (TOKENS, H, ROPE), jnp.float32)
    drawn = jitter
    return jnp.clip(drawn, -8.0, 8.0).astype(jnp.bfloat16)


def draw_cache_rope(key, part):
    jitter = jax.random.normal(jax.random.fold_in(key, 31), (NODES, LVL, ROPE), jnp.float32)
    drawn = jitter
    return jnp.clip(drawn, -8.0, 8.0).astype(jnp.bfloat16)


def draw_new_rope(key, part):
    jitter = jax.random.normal(jax.random.fold_in(key, 41), (TOKENS, ROPE), jnp.float32)
    drawn = jitter
    return jnp.clip(drawn, -8.0, 8.0).astype(jnp.bfloat16)


def shard_levels(own_key, extent, cuts, smallest, high):
    factor_of = 1.0
    for position, parts in cuts:
        draws = jax.random.uniform(jax.random.fold_in(jax.random.fold_in(own_key, 6), position), (parts,), jnp.float32, smallest / len(cuts), high / len(cuts))
        factor_of = factor_of * jnp.repeat(jnp.exp(draws), extent[position] // parts).reshape((-1,) + (1,) * (len(extent) - 1 - position))
    return factor_of


def assign_block(rng, own, number, rows, number_of, top, limit, skew):
    sequence = jax.random.permutation(rng, number_of)
    crowded, usual = shares(number_of, rows * top, limit, skew, True), shares(number_of, rows * top, limit, skew, False)
    places = jnp.arange(number_of)

    def named(sizes, rotation):
        used = int((sizes > 0).sum())
        fixed = max(1, used // 4)
        moved = fixed + (places - fixed + rotation * (used - fixed)) % max(1, number_of - fixed)
        return jnp.zeros((number_of,), jnp.int32).at[sequence[jnp.where(places < fixed, places, moved)]].set(jnp.asarray(sizes, jnp.int32))

    sizes = jnp.where(number % 4 == 0, named(crowded, number // 4), named(usual, number - number // 4 - 1))
    mixed = jax.random.permutation(jax.random.fold_in(own, 3), number_of)
    giver, taker = mixed[0:number_of // 2 * 2:2], mixed[1:number_of // 2 * 2:2]
    room = jnp.minimum(sizes[giver] - 1, limit - sizes[taker]) // 2
    room = jnp.where((giver == sequence[0]) | (taker == sequence[0]) | (sizes[taker] == 0), 0, jnp.maximum(room, 0))
    moved = jax.random.randint(jax.random.fold_in(own, 4), (number_of // 2,), 0, 1 << 20) % (room + 1)
    sizes = sizes.at[giver].add(-moved).at[taker].add(moved)
    items = jnp.searchsorted(jnp.cumsum(sizes), jnp.arange(rows * top), side="right").astype(jnp.int32)
    listing = items.reshape(top, rows).T
    listing = listing[jax.random.permutation(jax.random.fold_in(own, 1), rows)]
    rotation = jax.random.randint(jax.random.fold_in(own, 2), (rows, 1), 0, top)
    return jnp.take_along_axis(listing, (jnp.arange(top)[None, :] + rotation) % top, axis=1)


def shares(number_of, total, most, skew, full):
    weights = [(1 << 20) // math.isqrt(grade ** skew) + 1 for grade in range(1, number_of + 1)]
    largest = most if full else min(most, max(-(-total // number_of), total * weights[0] // sum(weights)))
    least = 1 if total - largest >= number_of - 1 else 0
    counts, rest = [largest] + [least] * (number_of - 1), total - largest - least * (number_of - 1)
    while rest > 0:
        movable = [i for i in range(1, number_of) if counts[i] < largest] or [i for i in range(1, number_of) if counts[i] < most]
        pool, remaining = sum([weights[i] for i in movable]), rest
        for i in movable:
            addition = min(most - counts[i], max(1, remaining * weights[i] // pool), rest)
            counts[i] = counts[i] + addition
            rest = rest - addition
    return np.array(counts)


def normal_values(key, shape, scale, reach, shards=(), kind=jnp.bfloat16):
    level = shard_levels(key, shape, shards, -0.22, 0.18) if shards else 1.0
    values = jax.random.normal(key, shape, jnp.float32) * scale * level
    return jnp.minimum(jnp.maximum(values, -reach), reach).astype(kind)


def setup_inputs(seed: int = 0) -> dict:
    streams_of = jax.random.split(jax.random.key(seed), 23)
    query_nope = normal_values(streams_of[0], (TOKENS, H, NOPE), 1.0, 6.0, ((0, 16), (1, 16)))
    query_rope = draw_query_rope(jax.random.fold_in(streams_of[22], 71), 0)
    absorb_weight = normal_values(streams_of[2], (H, NOPE, LAT), NOPE ** -0.5, 0.5, ((0, 16),))
    value_weight = normal_values(streams_of[3], (H, LAT, VDIM), (LAT // 16) ** -0.5, 1.0, ((0, 16),))
    output_weight = normal_values(streams_of[4], (H * VDIM, D), (H * VDIM // 4) ** -0.5, 0.25, ((0, 16),))
    cache_latent = normal_values(streams_of[5], (NODES, LVL, LAT), 1.0, 6.0, ((0, 16),))
    cache_rope = draw_cache_rope(jax.random.fold_in(streams_of[22], 71), 0)
    node_length = draw_node_length(jax.random.fold_in(streams_of[22], 71), 0)
    new_latent = normal_values(streams_of[8], (TOKENS, LAT), 1.0, 6.0, ((0, 16),))
    new_rope = draw_new_rope(jax.random.fold_in(streams_of[22], 71), 0)
    parent_node = draw_parent_node(jax.random.fold_in(streams_of[22], 71), 0)
    leaf_node = draw_leaf_node(jax.random.fold_in(streams_of[22], 71), 0)
    residual = normal_values(streams_of[12], (TOKENS, D), 1.0, 6.0, ((0, 256),))
    norm_gain = jnp.clip(1.0 + 0.1 * jax.random.normal(streams_of[13], (D,), jnp.float32), 0.5, 1.5).astype(jnp.bfloat16)
    router_weight = normal_values(streams_of[14], (D, EXPERTS), (D // 4) ** -0.5, 0.25)
    routes_keys = jax.random.split(jax.random.fold_in(streams_of[15], 1), TOKENS // TOK_DEV)
    routes_turns = jax.random.permutation(jax.random.fold_in(streams_of[15], 3), TOKENS // TOK_DEV)
    routes = jax.vmap(lambda own, number: assign_block(jax.random.fold_in(streams_of[15], 2), own, number, TOK_DEV, EXPERTS, TOPK, CAP, 2))(routes_keys, routes_turns).reshape((TOKENS, TOPK))
    expert_gate = normal_values(streams_of[16], (EXPERTS * FF_BLOCKS, D, FF_BLK), D ** -0.5, 0.125, ((0, 256),))
    expert_up = normal_values(streams_of[17], (EXPERTS * FF_BLOCKS, D, FF_BLK), D ** -0.5, 0.125, ((0, 256),))
    expert_down = normal_values(streams_of[18], (EXPERTS * FF_BLOCKS, FF_BLK, D), MOE_FF ** -0.5, 0.15625, ((0, 256),))
    shared_gate = normal_values(streams_of[19], (D, SHARED_FF), D ** -0.5, 0.125, ((1, 16),))
    shared_up = normal_values(streams_of[20], (D, SHARED_FF), D ** -0.5, 0.125, ((1, 16),))
    shared_down = normal_values(streams_of[21], (SHARED_FF, D), SHARED_FF ** -0.5, 0.109375, ((0, 16),))
    return dict(query_nope=query_nope, query_rope=query_rope, absorb_weight=absorb_weight, value_weight=value_weight, output_weight=output_weight, cache_latent=cache_latent, cache_rope=cache_rope, node_length=node_length, new_latent=new_latent, new_rope=new_rope, parent_node=parent_node, leaf_node=leaf_node, residual=residual, norm_gain=norm_gain, router_weight=router_weight, routes=routes, expert_gate=expert_gate, expert_up=expert_up, expert_down=expert_down, shared_gate=shared_gate, shared_up=shared_up, shared_down=shared_down)


ROUTE_SCALE = 2.446
NEGATIVE = -1e+30
EPSILON = 1e-06

def block_partial(query_lat, query_rot, key_lat, key_rot, usable, scaling):
    scores = jnp.einsum('bhl,kl->bhk', query_lat.astype(jnp.float32), key_lat.astype(jnp.float32))
    scores = scores + jnp.einsum('bhr,kr->bhk', query_rot.astype(jnp.float32), key_rot.astype(jnp.float32))
    scores = jnp.where(usable[:, None, :], scores * scaling, NEGATIVE)
    top_score = lax.optimization_barrier(jnp.max(scores, axis=-1))
    weights = jnp.where(usable[:, None, :], jnp.exp(scores - top_score[..., None]), 0.0).astype(jnp.bfloat16)
    widened = weights.astype(jnp.float32)
    totals = lax.optimization_barrier(jnp.sum(widened, axis=-1))
    summed = jnp.einsum('bhk,kl->bhl', widened, key_lat.astype(jnp.float32))
    return (top_score, totals, summed)

def reference(query_nope, query_rope, absorb_weight, value_weight, output_weight, cache_latent, cache_rope, node_length, new_latent, new_rope, parent_node, leaf_node, residual, norm_gain, router_weight, routes, expert_gate, expert_up, expert_down, shared_gate, shared_up, shared_down):
    scaling = float(NOPE + ROPE) ** (-0.5)
    query_latent = jnp.einsum('thn,hnl->thl', query_nope.astype(jnp.float32), absorb_weight.astype(jnp.float32)).astype(jnp.bfloat16)
    middle = parent_node[leaf_node]
    root_node = parent_node[middle]
    path_table = jnp.stack([leaf_node, middle, root_node], axis=1)
    positions = jnp.arange(LVL, dtype=jnp.int32)
    order_pos = jnp.arange(QT, dtype=jnp.int32)
    causal = order_pos[None, :] <= order_pos[:, None]

    def one_request(request):
        first_row = (request * QT).astype(jnp.int32)
        query_lat = lax.dynamic_slice_in_dim(query_latent, first_row, QT, 0)
        query_rot = lax.dynamic_slice_in_dim(query_rope, first_row, QT, 0)
        block_list = []
        for depth_level in range(3):
            node_id = path_table[request, depth_level]
            usable = jnp.broadcast_to((positions < node_length[node_id])[None, :], (QT, LVL))
            block_list.append(block_partial(query_lat, query_rot, cache_latent[node_id], cache_rope[node_id], usable, scaling))
        fresh_lat = lax.dynamic_slice_in_dim(new_latent, first_row, QT, 0)
        fresh_rot = lax.dynamic_slice_in_dim(new_rope, first_row, QT, 0)
        block_list.append(block_partial(query_lat, query_rot, fresh_lat, fresh_rot, causal, scaling))
        top_score = block_list[0][0]
        for block_part in block_list[1:]:
            top_score = jnp.maximum(top_score, block_part[0])
        totals = jnp.zeros_like(block_list[0][1])
        summed = jnp.zeros_like(block_list[0][2])
        for block_part in block_list:
            factor = jnp.exp(block_part[0] - top_score)
            totals = totals + block_part[1] * factor
            summed = summed + block_part[2] * factor[..., None]
        return (summed / totals[..., None]).astype(jnp.bfloat16)
    attended = lax.map(one_request, jnp.arange(REQUESTS, dtype=jnp.int32)).reshape(TOKENS, H, LAT)
    valued = jnp.einsum('thl,hlv->thv', attended.astype(jnp.float32), value_weight.astype(jnp.float32)).astype(jnp.bfloat16)
    attention = jnp.dot(valued.reshape(TOKENS, H * VDIM), output_weight, preferred_element_type=jnp.float32)
    hidden_state = residual.astype(jnp.float32) + attention
    normed = (hidden_state * lax.rsqrt(lax.optimization_barrier(jnp.mean(hidden_state * hidden_state, axis=-1, keepdims=True)) + EPSILON) * norm_gain.astype(jnp.float32)).astype(jnp.bfloat16)
    logits = jnp.dot(normed, router_weight, preferred_element_type=jnp.float32)
    sigma = jax.nn.sigmoid(logits)
    picked = jnp.take_along_axis(sigma, routes, axis=1)
    route_w = ROUTE_SCALE * picked / lax.optimization_barrier(jnp.sum(picked, axis=1, keepdims=True))
    devices_all = N_GROUP * N_EXPERT
    dev_routes = routes.reshape(devices_all, TOK_DEV * TOPK)
    chosen = (dev_routes[:, :, None] == jnp.arange(EXPERTS, dtype=jnp.int32)).astype(jnp.int32)
    earlier = jnp.cumsum(chosen, axis=1) - chosen
    ranking = lax.optimization_barrier(jnp.sum(earlier * chosen, axis=2))
    slot_ids = (jnp.arange(devices_all, dtype=jnp.int32)[:, None] * CAP + ranking).reshape(-1).astype(jnp.int32)
    expert_ids = routes.reshape(-1).astype(jnp.int32)
    token_ids = (jnp.arange(TOKENS * TOPK, dtype=jnp.int32) // TOPK).astype(jnp.int32)
    buffer = jnp.zeros((EXPERTS, devices_all * CAP, D), jnp.bfloat16).at[expert_ids, slot_ids].set(normed[token_ids])
    gate_full = expert_gate.reshape(EXPERTS, FF_BLOCKS, D, FF_BLK).transpose(0, 2, 1, 3).reshape(EXPERTS, D, MOE_FF)
    up_full = expert_up.reshape(EXPERTS, FF_BLOCKS, D, FF_BLK).transpose(0, 2, 1, 3).reshape(EXPERTS, D, MOE_FF)
    down_full = expert_down.reshape(EXPERTS, MOE_FF, D)

    def expert_rows(operands):
        rows_in, w_gate, w_up, w_down = operands
        gate_val = jnp.dot(rows_in, w_gate, preferred_element_type=jnp.float32)
        up_val = jnp.dot(rows_in, w_up, preferred_element_type=jnp.float32)
        hidden = (jax.nn.silu(gate_val) * up_val).astype(jnp.bfloat16)
        sliced = hidden.reshape(rows_in.shape[0], FF_BLOCKS, FF_BLK).astype(jnp.float32)
        blocks = jnp.einsum('sgf,gfd->gsd', sliced, w_down.reshape(FF_BLOCKS, FF_BLK, D).astype(jnp.float32))
        rounded = lax.optimization_barrier(blocks.astype(jnp.bfloat16))
        return lax.optimization_barrier(jnp.sum(rounded.astype(jnp.float32), axis=0))
    expert_out = lax.map(expert_rows, (buffer, gate_full, up_full, down_full))
    picked_out = expert_out[expert_ids, slot_ids].reshape(TOKENS, TOPK, D)
    routed = lax.optimization_barrier(jnp.sum(route_w[:, :, None] * picked_out, axis=1))
    shared_gate_val = jnp.dot(normed, shared_gate, preferred_element_type=jnp.float32)
    shared_up_val = jnp.dot(normed, shared_up, preferred_element_type=jnp.float32)
    shared_act = (jax.nn.silu(shared_gate_val) * shared_up_val).astype(jnp.bfloat16)
    shared_out = jnp.dot(shared_act, shared_down, preferred_element_type=jnp.float32)
    return (hidden_state + routed + shared_out).astype(jnp.bfloat16)
```

```python
import jax
import jax.numpy as jnp
from jax import lax
from jax.experimental import pallas as pl
from jax.experimental.pallas import tpu as pltpu
from jax.sharding import PartitionSpec as P

ROUTE_SCALE = 2.446
NEGATIVE = -1e30
EPSILON = 1e-06
MESH = pl.DeviceIdType.MESH
F32 = jnp.float32
BF16 = jnp.bfloat16
VMEM = pltpu.VMEM
DMA = pltpu.SemaphoreType.DMA

REQ = 16
QT = 8
MSG = 1024 + 128


def vmem_spec():
    return pl.BlockSpec(memory_space=pltpu.VMEM)


def any_spec():
    return pl.BlockSpec(memory_space=pl.ANY)


def coords():
    g = lax.axis_index("group")
    e = lax.axis_index("expert")
    zl, x = g // 4, g % 4
    y, zh, c = e // 4, (e % 4) // 2, e % 2
    return g, e, x, y, zl, zh, c


def dev(x, y, zl, zh, c):
    return (zl * 4 + x, y * 4 + zh * 2 + c)


def remote(src, dst, send, recv, device):
    return pltpu.make_async_remote_copy(
        src_ref=src,
        dst_ref=dst,
        send_sem=send,
        recv_sem=recv,
        device_id=device,
        device_id_type=MESH,
    )


def greet(barrier, device):
    pl.semaphore_signal(barrier, inc=1, device_id=device, device_id_type=MESH)


def dot(a, b):
    return jnp.dot(a, b, preferred_element_type=F32)


def flag(condition):
    return jnp.where(condition, 1.0, 0.0).astype(BF16)


def dot_nt(a, b):
    return lax.dot_general(a, b, (((1,), (1,)), ((), ())), preferred_element_type=F32)


def gather_kernel(q_ref, routes_ref, resid_ref, qall, routes8, resid2, qs, qr, rs, rr, zs, zr):
    g, e, x, y, zl, zh, c = coords()
    barrier = pltpu.get_barrier_semaphore()

    def hello(i, carry):
        greet(barrier, (lax.rem(g + i, 16), e))
        return carry

    lax.fori_loop(1, 16, hello, 0)
    for k in (1, 3, 5, 7):
        s = lax.rem(zl * 2 + zh + k, 8)
        greet(barrier, dev(x, y, s // 2, s % 2, c))
    pl.semaphore_wait(barrier, 19)

    def send(i, carry):
        remote(q_ref, qall.at[g], qs.at[i], qr.at[i], (lax.rem(g + i, 16), e)).start()
        return carry

    lax.fori_loop(1, 16, send, 0)
    me = zl * 2 + zh
    for k in range(1, 8):
        s = lax.rem(me + k, 8)
        remote(routes_ref, routes8.at[me], rs.at[k], rr.at[k], dev(x, y, s // 2, s % 2, c)).start()
    partner = dev(x, y, zl, 1 - zh, c)
    remote(resid_ref, resid2.at[zh], zs, zr, partner).start()
    qall[g] = q_ref[...]
    routes8[me] = routes_ref[...]
    resid2[zh] = resid_ref[...]
    remote(resid_ref, resid2.at[1 - zh], zs, zr, partner).wait()
    for k in range(1, 8):
        s = lax.rem(me - k + 8, 8)
        remote(routes_ref, routes8.at[s], rs.at[k], rr.at[k], partner).wait()

    def wait(i, carry):
        remote(q_ref, qall.at[lax.rem(g - i + 16, 16)], qs.at[i], qr.at[i], partner).wait()
        return carry

    lax.fori_loop(1, 16, wait, 0)


def gather(q2, routes_pad, residual):
    return pl.pallas_call(
        gather_kernel,
        name="gather_queries",
        out_shape=(
            jax.ShapeDtypeStruct((16,) + q2.shape, q2.dtype),
            jax.ShapeDtypeStruct((8,) + routes_pad.shape, routes_pad.dtype),
            jax.ShapeDtypeStruct((2,) + residual.shape, residual.dtype),
        ),
        in_specs=[vmem_spec()] * 3,
        out_specs=(vmem_spec(),) * 3,
        scratch_shapes=[
            DMA((16,)),
            DMA((16,)),
            DMA((8,)),
            DMA((8,)),
            DMA,
            DMA,
        ],
        compiler_params=pltpu.CompilerParams(
            collective_id=0, has_side_effects=True, vmem_limit_bytes=32 << 20
        ),
    )(q2, routes_pad, residual)


TILE = 32


def split3(v):
    hi = v.astype(BF16)
    rest = v - hi.astype(F32)
    mid = rest.astype(BF16)
    low = (rest - mid.astype(F32)).astype(BF16)
    return hi.astype(F32), mid.astype(F32), low.astype(F32)


def join3(part):
    return part[:, 0:8] + part[:, 8:16] + part[:, 16:24]


def on_path_row(leaf_row, parent_col, node):
    nodes = parent_col.shape[0]
    ids = lax.broadcasted_iota(jnp.int32, (nodes, leaf_row.shape[1]), 0)
    mid = jnp.sum(jnp.where(leaf_row == ids, parent_col, 0), axis=0, keepdims=True)
    top = jnp.sum(jnp.where(mid == ids, parent_col, 0), axis=0, keepdims=True)
    return (leaf_row == node) | (mid == node) | (top == node)


def on_path_col(leaf_col, parent_row, node):
    nodes = parent_row.shape[1]
    ids = lax.broadcasted_iota(jnp.int32, (leaf_col.shape[0], nodes), 1)
    mid = jnp.sum(jnp.where(leaf_col == ids, parent_row, 0), axis=1, keepdims=True)
    top = jnp.sum(jnp.where(mid == ids, parent_row, 0), axis=1, keepdims=True)
    return (leaf_col == node) | (mid == node) | (top == node)


def attn_kernel(
    len_ref,
    q_ref,
    absorb_ref,
    value_ref,
    lat_ref,
    rope_ref,
    leaf_row_ref,
    leaf_col_ref,
    parent_row_ref,
    parent_col_ref,
    out_ref,
    acc,
):
    g = lax.axis_index("group")
    requests = q_ref.shape[0]
    slots, keys = lat_ref.shape[0], lat_ref.shape[1]
    scaling = float(128 + 64) ** (-0.5)
    earlier = flag(
        lax.broadcasted_iota(jnp.int32, (requests, requests), 0)
        < lax.broadcasted_iota(jnp.int32, (requests, requests), 1)
    )
    later = flag(
        lax.broadcasted_iota(jnp.int32, (requests, requests), 1)
        < lax.broadcasted_iota(jnp.int32, (requests, requests), 0)
    )
    acc[...] = jnp.zeros_like(acc)
    lane = lax.broadcasted_iota(jnp.int32, (TILE, 128), 1)
    positions = lax.broadcasted_iota(jnp.int32, (1, keys), 1)
    on_cols = []
    for slot in range(slots):
        node = g * slots + slot
        on_row = on_path_row(leaf_row_ref[...], parent_col_ref[...], node)
        on_col = on_path_col(leaf_col_ref[...], parent_row_ref[...], node)
        on_cols.append(on_col)
        row_f = jnp.where(on_row, 1.0, 0.0)
        count = jnp.sum(row_f).astype(jnp.int32)
        rank_row = dot(jnp.broadcast_to(row_f, (8, requests)).astype(BF16), earlier)[0:1]
        rank_row = jnp.where(on_row, rank_row, -1.0).astype(jnp.int32)
        rank_col = dot(
            later, jnp.broadcast_to(jnp.where(on_col, 1.0, 0.0), (requests, 128)).astype(BF16)
        )[:, 0:1]
        rank_col = jnp.where(on_col, rank_col, -1.0).astype(jnp.int32)
        length = len_ref[slot]

        def tile(step, carry):
            base = step * TILE
            pick = flag(rank_row == lax.broadcasted_iota(jnp.int32, (TILE, requests), 0) + base)
            place = flag(rank_col == lax.broadcasted_iota(jnp.int32, (requests, TILE), 1) + base)
            qt = dot(pick, q_ref[...]).astype(BF16)
            nope = jnp.concatenate([qt[:, j * 128 : j * 128 + 128] for j in range(QT)], axis=0)
            rot = jnp.concatenate(
                [qt[:, 1024 + j * 64 : 1024 + j * 64 + 64] for j in range(QT)], axis=0
            )
            lat = dot(nope, absorb_ref[...]).astype(BF16)
            scores = dot_nt(lat, lat_ref[slot]) + dot_nt(rot, rope_ref[slot])
            scores = jnp.where(positions < length, scores * scaling, NEGATIVE)
            top = jnp.max(scores, axis=1, keepdims=True)
            weights = jnp.exp(scores - top).astype(BF16)
            total = jnp.sum(weights.astype(F32), axis=1, keepdims=True)
            summed = dot(weights, lat_ref[slot])
            attended = (summed / total).astype(BF16)
            valued = dot(attended, value_ref[...]).astype(BF16)
            log_sum = top + jnp.log(total)
            parts = split3(log_sum)
            tail = jnp.zeros((TILE, 128), F32)
            for j in range(QT):
                for k in range(3):
                    piece = parts[k][j * TILE : (j + 1) * TILE]
                    tail = jnp.where(lane == k * 8 + j, piece, tail)
            block = jnp.concatenate(
                [valued[j * TILE : (j + 1) * TILE] for j in range(QT)] + [tail.astype(BF16)],
                axis=1,
            )
            acc[slot] += dot(place, block)
            return carry

        lax.fori_loop(0, (count + TILE - 1) // TILE, tile, 0)

    logs = [
        jnp.where(on_cols[s], join3(acc[s, :, 1024:]), NEGATIVE) for s in range(slots)
    ]
    top = logs[0]
    for s in range(1, slots):
        top = jnp.maximum(top, logs[s])
    shares = [jnp.exp(v - top) for v in logs]
    total = shares[0]
    for s in range(1, slots):
        total = total + shares[s]
    log_sum = top + jnp.log(total)
    for j in range(QT):
        out = 0.0
        for s in range(slots):
            out = out + (shares[s] / total)[:, j : j + 1] * acc[s, :, j * 128 : j * 128 + 128]
        out_ref[:, j * 128 : j * 128 + 128] = out.astype(BF16)
    parts = split3(log_sum)
    lane = lax.broadcasted_iota(jnp.int32, (requests, 128), 1)
    tail = jnp.zeros((requests, 128), F32)
    for j in range(QT):
        for k in range(3):
            tail = jnp.where(lane == k * 8 + j, parts[k][:, j : j + 1], tail)
    out_ref[:, 1024:] = tail.astype(BF16)


def attend(node_length, q_all, absorb, value, cache_latent, cache_rope, leaf, parent):
    requests = q_all.shape[0]
    slots = cache_latent.shape[0]
    return pl.pallas_call(
        attn_kernel,
        name="attend_nodes",
        out_shape=jax.ShapeDtypeStruct((requests, MSG), BF16),
        in_specs=[pl.BlockSpec(memory_space=pltpu.SMEM)] + [vmem_spec()] * 9,
        out_specs=vmem_spec(),
        scratch_shapes=[VMEM((slots, requests, MSG), F32)],
        compiler_params=pltpu.CompilerParams(vmem_limit_bytes=48 << 20),
    )(
        node_length,
        q_all,
        absorb,
        value,
        cache_latent,
        cache_rope,
        leaf[None, :],
        leaf[:, None],
        parent[None, :],
        parent[:, None],
    )


def merge_kernel(
    msg_ref,
    q_ref,
    absorb_ref,
    value_ref,
    newlat_ref,
    newrope_ref,
    outw_ref,
    resid_ref,
    gain_ref,
    hidden_ref,
    normed_ref,
    got,
    valued_s,
    csend,
    crecv,
    acc,
    ysend,
    yrecv,
    zsend,
    zrecv,
    ms,
    mr,
    cs,
    cr,
    ys,
    yr,
    hs,
    hr,
    ls,
    lr,
):
    g, e, x, y, zl, zh, c = coords()
    barrier = pltpu.get_barrier_semaphore()

    def hello(i, carry):
        greet(barrier, (lax.rem(g + i, 16), e))
        return carry

    lax.fori_loop(1, 16, hello, 0)
    other = dev(x, y, zl, zh, 1 - c)
    partner = dev(x, y, zl, 1 - zh, c)
    greet(barrier, other)
    greet(barrier, partner)
    for i in range(1, 4):
        greet(barrier, dev(x, lax.rem(y + i, 4), zl, zh, c))
    pl.semaphore_wait(barrier, 20)

    def send(i, carry):
        peer = lax.rem(g + i, 16)
        remote(msg_ref.at[peer], got.at[g], ms.at[i], mr.at[i], (peer, e)).start()
        return carry

    lax.fori_loop(1, 16, send, 0)
    got[g] = msg_ref[g]

    scaling = float(128 + 64) ** (-0.5)
    q = q_ref[...]
    nope = jnp.concatenate([q[:, j * 128 : j * 128 + 128] for j in range(QT)], axis=0)
    rot = jnp.concatenate([q[:, 1024 + j * 64 : 1024 + j * 64 + 64] for j in range(QT)], axis=0)
    lat = dot(nope, absorb_ref[...]).astype(BF16)
    scores = dot_nt(lat, newlat_ref[...]) + dot_nt(rot, newrope_ref[...])
    rows = REQ * QT
    qi = lax.broadcasted_iota(jnp.int32, (rows, rows), 0)
    ki = lax.broadcasted_iota(jnp.int32, (rows, rows), 1)
    usable = ((qi % REQ) == (ki // QT)) & ((ki % QT) <= (qi // REQ))
    scores = jnp.where(usable, scores * scaling, NEGATIVE)
    top = jnp.max(scores, axis=1, keepdims=True)
    weights = jnp.where(usable, jnp.exp(scores - top), 0.0).astype(BF16)
    total = jnp.sum(weights.astype(F32), axis=1, keepdims=True)
    summed = dot(weights, newlat_ref[...]) / total
    new_valued = dot(summed.astype(BF16), value_ref[...])
    new_log = top + jnp.log(total)

    def wait(i, carry):
        src = lax.rem(g - i + 16, 16)
        remote(msg_ref.at[src], got.at[src], ms.at[i], mr.at[i], other).wait()
        return carry

    lax.fori_loop(1, 16, wait, 0)

    logs = join3(got[:, :, 1024:].astype(F32).reshape(16 * REQ, 128)).reshape(16, REQ, 8)
    pieces = []
    for j in range(QT):
        log_j = logs[:, :, j : j + 1]
        new_j = new_log[j * REQ : (j + 1) * REQ]
        peak = jnp.maximum(jnp.max(log_j, axis=0), new_j)
        share = jnp.exp(log_j - peak[None])
        new_share = jnp.exp(new_j - peak)
        whole = jnp.sum(share, axis=0) + new_share
        value = jnp.sum(share * got[:, :, j * 128 : j * 128 + 128].astype(F32), axis=0)
        value = value + new_share * new_valued[j * REQ : (j + 1) * REQ]
        pieces.append((value / whole).astype(BF16))
    valued = jnp.concatenate(pieces, axis=0)
    di = lax.broadcasted_iota(jnp.int32, (rows, rows), 0)
    si = lax.broadcasted_iota(jnp.int32, (rows, rows), 1)
    req = ((di % 64) // 16) * 4 + ((di % 16) // 8) * 2 + di // 64
    perm = flag(si == (di % 8) * REQ + req)
    valued_s[...] = dot(perm, valued).astype(BF16).reshape(2, 64, 128)

    csend[...] = dot(valued_s[1 - c], outw_ref[...]).astype(BF16)
    remote(csend, crecv, cs, cr, other).start()
    own = dot(valued_s[c], outw_ref[...])
    remote(csend, crecv, cs, cr, other).wait()
    acc[...] = (own + crecv[...].astype(F32)).reshape(4, 16, 2048)
    ysend[...] = acc[...].astype(BF16)
    for i in range(1, 4):
        peer = lax.rem(y + i, 4)
        remote(ysend.at[peer], yrecv.at[i], ys.at[i], yr.at[i], dev(x, peer, zl, zh, c)).start()
    for i in range(1, 4):
        remote(ysend.at[0], yrecv.at[i], ys.at[i], yr.at[i], other).wait()
    mine = acc[y]
    for i in range(1, 4):
        mine = mine + yrecv[i].astype(F32)
    zsend[...] = mine.astype(BF16)
    remote(zsend, zrecv, hs, hr, partner).start()
    remote(zsend, zrecv, hs, hr, partner).wait()
    hidden = mine + zrecv[...].astype(F32) + resid_ref[...].reshape(16, 2048).astype(F32)
    hidden_ref[...] = hidden.reshape(2, 8, 2048)
    square = jnp.mean(hidden * hidden, axis=1, keepdims=True)
    normed = (hidden * lax.rsqrt(square + EPSILON) * gain_ref[...].astype(F32)).astype(BF16)
    normed_ref[zl] = normed
    for i in range(1, 4):
        peer = lax.rem(zl + i, 4)
        remote(
            normed_ref.at[zl], normed_ref.at[zl], ls.at[i], lr.at[i], dev(x, y, peer, zh, c)
        ).start()
    for i in range(1, 4):
        src = lax.rem(zl - i + 4, 4)
        remote(normed_ref.at[zl], normed_ref.at[src], ls.at[i], lr.at[i], other).wait()


def merge(msg, q2, absorb, value, new_latent, new_rope, outw, resid2, gain):
    return pl.pallas_call(
        merge_kernel,
        name="merge_project_norm",
        out_shape=(
            jax.ShapeDtypeStruct((2, 8, 2048), F32),
            jax.ShapeDtypeStruct((4, 16, 2048), BF16),
        ),
        in_specs=[vmem_spec()] * 9,
        out_specs=(vmem_spec(),) * 2,
        scratch_shapes=[
            VMEM((16, REQ, MSG), BF16),
            VMEM((2, 64, 128), BF16),
            VMEM((64, 2048), BF16),
            VMEM((64, 2048), BF16),
            VMEM((4, 16, 2048), F32),
            VMEM((4, 16, 2048), BF16),
            VMEM((4, 16, 2048), BF16),
            VMEM((16, 2048), BF16),
            VMEM((16, 2048), BF16),
            DMA((16,)),
            DMA((16,)),
            DMA,
            DMA,
            DMA((4,)),
            DMA((4,)),
            DMA,
            DMA,
            DMA((4,)),
            DMA((4,)),
        ],
        compiler_params=pltpu.CompilerParams(
            collective_id=1, has_side_effects=True, vmem_limit_bytes=48 << 20
        ),
    )(msg, q2, absorb, value, new_latent, new_rope, outw, resid2, gain)


def expert_kernel(
    normed_ref,
    hidden_ref,
    place_ref,
    pick_ref,
    chosen_ref,
    router_ref,
    gate_hbm,
    up_hbm,
    down_hbm,
    sgate_hbm,
    sup_hbm,
    sdown_hbm,
    out_ref,
    gate_w,
    up_w,
    down_w,
    sgate_w,
    sup_w,
    sdown_w,
    packed,
    arrived,
    across,
    own_out,
    cross_send,
    cross_recv,
    ret_send,
    ret_recv,
    share_in,
    share_send,
    share_recv,
    part,
    lsend,
    lrecv,
    hsend,
    hrecv,
    wsem,
    ds,
    dr,
    cs,
    cr,
    os_,
    or_,
    rs,
    rr,
    xs,
    xr,
    bs,
    br,
    ls,
    lr,
    hs,
    hr,
):
    g, e, x, y, zl, zh, c = coords()
    mine = x * 4 + y
    loads = [
        pltpu.make_async_copy(src, dst, wsem.at[i])
        for i, (src, dst) in enumerate(
            [
                (gate_hbm, gate_w),
                (up_hbm, up_w),
                (down_hbm, down_w),
                (sgate_hbm, sgate_w),
                (sup_hbm, sup_w),
                (sdown_hbm, sdown_w),
            ]
        )
    ]
    for load in loads:
        load.start()
    barrier = pltpu.get_barrier_semaphore()

    def plane(p):
        return dev(p // 4, p % 4, zl, zh, c)

    def hello(i, carry):
        greet(barrier, plane(lax.rem(mine + i, 16)))
        return carry

    lax.fori_loop(1, 16, hello, 0)
    other = dev(x, y, zl, zh, 1 - c)
    partner = dev(x, y, zl, 1 - zh, c)
    greet(barrier, other)
    greet(barrier, partner)
    for i in range(1, 4):
        greet(barrier, dev(x, y, lax.rem(zl + i, 4), zh, c))

    tokens = normed_ref[...]
    packed[...] = dot(place_ref[...], tokens).astype(BF16).reshape(16, 16, 2048)
    share_in[x] = normed_ref[...].reshape(4, 2, 8, 2048)[:, 0].reshape(32, 2048)

    @pl.when(zh == 1)
    def _():
        share_in[x] = normed_ref[...].reshape(4, 2, 8, 2048)[:, 1].reshape(32, 2048)

    pl.semaphore_wait(barrier, 20)

    def send(i, carry):
        p = lax.rem(mine + i, 16)
        remote(packed.at[p], arrived.at[mine], ds.at[i], dr.at[i], plane(p)).start()
        return carry

    lax.fori_loop(1, 16, send, 0)
    arrived[mine] = packed[mine]
    remote(arrived.at[mine], across.at[mine], cs.at[0], cr.at[0], other).start()
    for i in range(1, 4):
        peer = lax.rem(x + i, 4)
        remote(share_in.at[x], share_in.at[x], xs.at[i], xr.at[i], dev(peer, y, zl, zh, c)).start()

    sigma = jax.nn.sigmoid(dot(tokens, router_ref[...])) * chosen_ref[...]
    route_w = ROUTE_SCALE * sigma / jnp.sum(sigma, axis=1, keepdims=True)
    experts = chosen_ref.shape[1]
    spread = flag(
        lax.broadcasted_iota(jnp.int32, (experts, 256), 0)
        == zl * 16 + lax.broadcasted_iota(jnp.int32, (experts, 256), 1) // 16
    )
    w_hi, w_mid, w_low = split3(route_w)
    combine = (
        dot(w_hi.astype(BF16), spread)
        + dot(w_mid.astype(BF16), spread)
        + dot(w_low.astype(BF16), spread)
    ) * pick_ref[...].astype(F32)

    def forward(i, carry):
        src = lax.rem(mine - i + 16, 16)
        remote(packed.at[src], arrived.at[src], ds.at[i], dr.at[i], other).wait()
        remote(arrived.at[src], across.at[src], cs.at[i], cr.at[i], other).start()
        return carry

    lax.fori_loop(1, 16, forward, 0)
    for load in loads[:3]:
        load.wait()

    def ffn(rows, gate, up, down):
        gate_val = dot(rows, gate[...])
        up_val = dot(rows, up[...])
        hidden = (jax.nn.silu(gate_val) * up_val).astype(BF16)
        return dot(hidden, down[...])

    own_out[...] = ffn(arrived[...].reshape(256, 2048), gate_w, up_w, down_w)

    def cross(i, carry):
        src = lax.rem(mine - i + 16, 16)
        remote(arrived.at[src], across.at[src], cs.at[i], cr.at[i], other).wait()
        return carry

    lax.fori_loop(0, 16, cross, 0)
    cross_send[...] = ffn(across[...].reshape(256, 2048), gate_w, up_w, down_w).astype(BF16)
    remote(cross_send, cross_recv, os_, or_, other).start()

    for load in loads[3:]:
        load.wait()
    for i in range(1, 4):
        src = lax.rem(x - i + 4, 4)
        remote(share_in.at[x], share_in.at[src], xs.at[i], xr.at[i], other).wait()
    shared = ffn(share_in[...].reshape(128, 2048), sgate_w, sup_w, sdown_w)
    share_send[...] = shared.astype(BF16).reshape(4, 32, 2048)
    for i in range(1, 4):
        peer = lax.rem(x + i, 4)
        remote(
            share_send.at[peer], share_recv.at[i], bs.at[i], br.at[i], dev(peer, y, zl, zh, c)
        ).start()

    remote(cross_send, cross_recv, os_, or_, other).wait()
    ret_send[...] = (
        (own_out[...] + cross_recv[...].astype(F32)).astype(BF16).reshape(16, 16, 2048)
    )

    def give(i, carry):
        p = lax.rem(mine + i, 16)
        remote(ret_send.at[p], ret_recv.at[mine], rs.at[i], rr.at[i], plane(p)).start()
        return carry

    lax.fori_loop(1, 16, give, 0)
    ret_recv[mine] = ret_send[mine]
    for i in range(1, 4):
        remote(share_send.at[0], share_recv.at[i], bs.at[i], br.at[i], other).wait()
    share_sum = share_send[x].astype(F32)
    for i in range(1, 4):
        share_sum = share_sum + share_recv[i].astype(F32)

    def take(i, carry):
        src = lax.rem(mine - i + 16, 16)
        remote(ret_send.at[src], ret_recv.at[src], rs.at[i], rr.at[i], other).wait()
        return carry

    lax.fori_loop(1, 16, take, 0)
    back = ret_recv[...].reshape(256, 2048)
    c_hi = combine.astype(BF16)
    c_low = (combine - c_hi.astype(F32)).astype(BF16)
    routed = (dot(c_hi, back) + dot(c_low, back)).reshape(4, 2, 8, 2048)
    is_own = jnp.where(lax.broadcasted_iota(jnp.int32, (4, 2, 8, 2048), 1) == zh, 1.0, 0.0)
    part[...] = (routed + share_sum.reshape(4, 1, 8, 2048) * is_own).reshape(4, 16, 2048)
    lsend[...] = part[...].astype(BF16)
    for i in range(1, 4):
        peer = lax.rem(zl + i, 4)
        remote(lsend.at[peer], lrecv.at[i], ls.at[i], lr.at[i], dev(x, y, peer, zh, c)).start()
    for i in range(1, 4):
        remote(lsend.at[0], lrecv.at[i], ls.at[i], lr.at[i], other).wait()
    both = part[zl]
    for i in range(1, 4):
        both = both + lrecv[i].astype(F32)
    hsend[...] = both.reshape(2, 8, 2048).astype(BF16)
    remote(hsend.at[1 - zh], hrecv, hs, hr, partner).start()
    remote(hsend.at[1 - zh], hrecv, hs, hr, partner).wait()
    kept = jnp.where(zh == 0, both[0:8], both[8:16])
    out_ref[...] = (hidden_ref[zh] + kept + hrecv[...].astype(F32)).astype(BF16)


def experts_layer(normed, hidden, place, pick, chosen, router, weights):
    shapes = [w.shape for w in weights]
    return pl.pallas_call(
        expert_kernel,
        name="experts",
        out_shape=jax.ShapeDtypeStruct((8, 2048), BF16),
        in_specs=[vmem_spec()] * 6 + [any_spec()] * 6,
        out_specs=vmem_spec(),
        scratch_shapes=[VMEM(s, BF16) for s in shapes]
        + [
            VMEM((16, 16, 2048), BF16),
            VMEM((16, 16, 2048), BF16),
            VMEM((16, 16, 2048), BF16),
            VMEM((256, 2048), F32),
            VMEM((256, 2048), BF16),
            VMEM((256, 2048), BF16),
            VMEM((16, 16, 2048), BF16),
            VMEM((16, 16, 2048), BF16),
            VMEM((4, 32, 2048), BF16),
            VMEM((4, 32, 2048), BF16),
            VMEM((4, 32, 2048), BF16),
            VMEM((4, 16, 2048), F32),
            VMEM((4, 16, 2048), BF16),
            VMEM((4, 16, 2048), BF16),
            VMEM((2, 8, 2048), BF16),
            VMEM((8, 2048), BF16),
            DMA((6,)),
            DMA((16,)),
            DMA((16,)),
            DMA((16,)),
            DMA((16,)),
            DMA,
            DMA,
            DMA((16,)),
            DMA((16,)),
            DMA((4,)),
            DMA((4,)),
            DMA((4,)),
            DMA((4,)),
            DMA((4,)),
            DMA((4,)),
            DMA,
            DMA,
        ],
        compiler_params=pltpu.CompilerParams(
            collective_id=2, has_side_effects=True, vmem_limit_bytes=56 << 20
        ),
    )(normed, hidden, place, pick, chosen, router, *weights)


def slot_tables(routes8, experts):
    zl = lax.axis_index("group") // 4
    routes = routes8[:, :, :6].reshape(64, 6)
    ids = jnp.arange(experts, dtype=jnp.int32)
    chosen = jnp.any(routes[:, :, None] == ids, axis=1)
    token = jnp.arange(64, dtype=jnp.int32)
    before = (token[:, None] // 8 == token[None, :] // 8) & (token[None, :] < token[:, None])
    rank = jnp.dot(before.astype(BF16), chosen.astype(BF16), preferred_element_type=F32)
    rank = jnp.where(chosen, rank, -1.0)
    here = lax.dynamic_slice_in_dim(rank, zl * 16, 16, 1)
    pick = (
        (here[:, :, None, None] == jnp.arange(2, dtype=F32))
        & (token[:, None, None, None] // 8 == jnp.arange(8)[None, None, :, None])
    ).astype(BF16)
    pick = pick.reshape(64, 256)
    return pick.T, pick, chosen.astype(F32)


def on_device(
    query_nope,
    query_rope,
    absorb_weight,
    value_weight,
    output_weight,
    cache_latent,
    cache_rope,
    node_length,
    new_latent,
    new_rope,
    parent_node,
    leaf_node,
    residual,
    norm_gain,
    router_weight,
    routes,
    expert_gate,
    expert_up,
    expert_down,
    shared_gate,
    shared_up,
    shared_down,
):
    q2 = jnp.concatenate(
        [query_nope.reshape(REQ, QT * 128), query_rope.reshape(REQ, QT * 64)], axis=1
    )
    routes_pad = jnp.pad(routes, ((0, 0), (0, 128 - routes.shape[1])), constant_values=-1)
    q_all, routes8, resid2 = gather(q2, routes_pad, residual)
    absorb, value = absorb_weight[0], value_weight[0]
    msg = attend(
        node_length,
        q_all.reshape(16 * REQ, -1),
        absorb,
        value,
        cache_latent,
        cache_rope,
        leaf_node,
        parent_node,
    )
    place, pick, chosen = slot_tables(routes8, router_weight.shape[1])
    hidden, normed = merge(
        msg.reshape(16, REQ, MSG),
        q2,
        absorb,
        value,
        new_latent,
        new_rope,
        output_weight,
        resid2,
        norm_gain[None, :],
    )
    weights = [
        expert_gate[0],
        expert_up[0],
        expert_down[0],
        shared_gate,
        shared_up,
        shared_down,
    ]
    return experts_layer(
        normed.reshape(64, 2048), hidden, place, pick, chosen, router_weight, weights
    )


def solution(mesh):
    in_specs = (
        P("group", "expert", None),
        P("group", "expert", None),
        P("expert", None, None),
        P("expert", None, None),
        P("expert", None),
        P("group", None, None),
        P("group", None, None),
        P("group"),
        P("group", None),
        P("group", None),
        P(),
        P(),
        P(("group", "expert"), None),
        P(),
        P(),
        P(("group", "expert"), None),
        P(("group", "expert"), None, None),
        P(("group", "expert"), None, None),
        P(("group", "expert"), None, None),
        P(None, "group"),
        P(None, "group"),
        P("group", None),
    )
    out_specs = P(("group", "expert"), None)
    return jax.shard_map(
        on_device, mesh=mesh, in_specs=in_specs, out_specs=out_specs, check_vma=False
    )
```

```python
import jax
import jax.numpy as jnp
from jax import lax
from jax.experimental import pallas as pl
from jax.experimental.pallas import tpu as pltpu
from jax.sharding import PartitionSpec as P

ROUTE_SCALE = 2.446
NEGATIVE = -1e30
EPSILON = 1e-06
MESH = pl.DeviceIdType.MESH
F32 = jnp.float32
BF16 = jnp.bfloat16
VMEM = pltpu.VMEM
DMA = pltpu.SemaphoreType.DMA

REQ = 16
QT = 8
MSG = 1024 + 128


def vmem_spec():
    return pl.BlockSpec(memory_space=pltpu.VMEM)


def any_spec():
    return pl.BlockSpec(memory_space=pl.ANY)


def coords():
    g = lax.axis_index("group")
    e = lax.axis_index("expert")
    zl, x = g // 4, g % 4
    y, zh, c = e // 4, (e % 4) // 2, e % 2
    return g, e, x, y, zl, zh, c


def dev(x, y, zl, zh, c):
    return (zl * 4 + x, y * 4 + zh * 2 + c)


def remote(src, dst, send, recv, device):
    return pltpu.make_async_remote_copy(
        src_ref=src,
        dst_ref=dst,
        send_sem=send,
        recv_sem=recv,
        device_id=device,
        device_id_type=MESH,
    )


def greet(barrier, device):
    pl.semaphore_signal(barrier, inc=1, device_id=device, device_id_type=MESH)


def dot(a, b):
    return jnp.dot(a, b, preferred_element_type=F32)


def eye_column(row):
    n = row.shape[1]
    same = lax.broadcasted_iota(jnp.int32, (n, n), 0) == lax.broadcasted_iota(jnp.int32, (n, n), 1)
    return jnp.sum(jnp.where(same, row, 0), axis=1, keepdims=True)


def flag(condition):
    return jnp.where(condition, 1.0, 0.0).astype(BF16)


def dot_nt(a, b):
    return lax.dot_general(a, b, (((1,), (1,)), ((), ())), preferred_element_type=F32)


def gather_kernel(
    nope_ref, rope_ref, routes_ref, resid_ref, qall, routes8, resid2, mine, zq, zqr, xq, xqr, rs, rr, zs, zr
):
    g, e, x, y, zl, zh, c = coords()
    barrier = pltpu.get_barrier_semaphore()
    partner = dev(x, y, zl, 1 - zh, c)
    me = zl * 2 + zh
    for i in range(1, 4):
        greet(barrier, dev(lax.rem(x + i, 4), y, zl, zh, c))
        greet(barrier, dev(x, y, lax.rem(zl + i, 4), zh, c))
    for k in (1, 3, 5, 7):
        s = lax.rem(me + k, 8)
        greet(barrier, dev(x, y, s // 2, s % 2, c))

    rows = REQ * QT
    di = lax.broadcasted_iota(jnp.int32, (rows, rows), 0)
    si = lax.broadcasted_iota(jnp.int32, (rows, rows), 1)
    perm = flag(si == (di % REQ) * QT + di // REQ)
    nope = dot(perm, nope_ref[...]).astype(BF16)
    rope = dot_nt(perm, rope_ref[...]).astype(BF16)
    qall[g] = jnp.concatenate(
        [nope[j * REQ : (j + 1) * REQ] for j in range(QT)]
        + [rope[j * REQ : (j + 1) * REQ] for j in range(QT)],
        axis=1,
    )
    mine[...] = jnp.zeros_like(mine)
    mine[:, 0 : routes_ref.shape[1]] = routes_ref[...]
    routes8[me] = mine[...]
    resid2[zh] = resid_ref[...]
    pl.semaphore_wait(barrier, 10)

    own = qall.at[g]
    for i in (1, 3, 2):
        remote(own, own, zq.at[i], zqr.at[i], dev(x, y, lax.rem(zl + i, 4), zh, c)).start()
    for k in (1, 3, 2):
        remote(own, own, xq.at[0, k], xqr.at[0, k], dev(lax.rem(x + k, 4), y, zl, zh, c)).start()
    remote(resid_ref, resid2.at[zh], zs, zr, partner).start()
    for k in range(1, 8):
        s = lax.rem(me + k, 8)
        remote(mine, routes8.at[me], rs.at[k], rr.at[k], dev(x, y, s // 2, s % 2, c)).start()
    for i in (1, 3, 2):
        block = qall.at[lax.rem(zl - i + 4, 4) * 4 + x]
        remote(own, block, zq.at[i], zqr.at[i], partner).wait()
        for k in (1, 3, 2):
            remote(
                block, block, xq.at[i, k], xqr.at[i, k], dev(lax.rem(x + k, 4), y, zl, zh, c)
            ).start()
    remote(resid_ref, resid2.at[1 - zh], zs, zr, partner).wait()
    for k in range(1, 8):
        s = lax.rem(me - k + 8, 8)
        remote(mine, routes8.at[s], rs.at[k], rr.at[k], partner).wait()
    for i in range(4):
        for k in (1, 3, 2):
            block = qall.at[lax.rem(zl - i + 4, 4) * 4 + lax.rem(x - k + 4, 4)]
            remote(own, block, xq.at[i, k], xqr.at[i, k], partner).wait()


def gather(nope, rope_t, routes, residual):
    return pl.pallas_call(
        gather_kernel,
        name="gather_queries",
        out_shape=(
            jax.ShapeDtypeStruct((16, REQ, QT * 192), BF16),
            jax.ShapeDtypeStruct((8, 8, 128), jnp.int32),
            jax.ShapeDtypeStruct((2,) + residual.shape, BF16),
        ),
        in_specs=[vmem_spec()] * 4,
        out_specs=(vmem_spec(),) * 3,
        scratch_shapes=[
            VMEM((8, 128), jnp.int32),
            DMA((4,)),
            DMA((4,)),
            DMA((4, 4)),
            DMA((4, 4)),
            DMA((8,)),
            DMA((8,)),
            DMA,
            DMA,
        ],
        compiler_params=pltpu.CompilerParams(
            collective_id=0, has_side_effects=True, vmem_limit_bytes=24 << 20
        ),
    )(nope, rope_t, routes, residual)


TILE = 32
KEYS = 256


def split3(v):
    hi = v.astype(BF16)
    rest = v - hi.astype(F32)
    mid = rest.astype(BF16)
    low = (rest - mid.astype(F32)).astype(BF16)
    return hi.astype(F32), mid.astype(F32), low.astype(F32)


def join3(part):
    return part[:, 0:8] + part[:, 8:16] + part[:, 16:24]


def on_path(leaf_row, parent_col, node):
    nodes = parent_col.shape[0]
    ids = lax.broadcasted_iota(jnp.int32, (nodes, leaf_row.shape[1]), 0)
    mid = jnp.sum(jnp.where(leaf_row == ids, parent_col, 0), axis=0, keepdims=True)
    top = jnp.sum(jnp.where(mid == ids, parent_col, 0), axis=0, keepdims=True)
    return (leaf_row == node) | (mid == node) | (top == node)


def attn_kernel(
    len_ref,
    q_ref,
    absorb_ref,
    value_ref,
    lat_ref,
    rope_ref,
    leaf_ref,
    parent_ref,
    out_ref,
    acc,
):
    g = lax.axis_index("group")
    requests = q_ref.shape[0]
    slots, most = lat_ref.shape[0], lat_ref.shape[1]
    scaling = float(128 + 64) ** (-0.5)
    earlier = flag(
        lax.broadcasted_iota(jnp.int32, (requests, requests), 0)
        < lax.broadcasted_iota(jnp.int32, (requests, requests), 1)
    )
    acc[...] = jnp.zeros_like(acc)
    lane = lax.broadcasted_iota(jnp.int32, (TILE, 128), 1)
    parent_col = eye_column(parent_ref[...])
    on_cols = []
    for slot in range(slots):
        on_row = on_path(leaf_ref[...], parent_col, g * slots + slot)
        row_f = jnp.where(on_row, 1.0, 0.0)
        count = jnp.sum(row_f).astype(jnp.int32)
        rank_row = dot(jnp.broadcast_to(row_f, (8, requests)).astype(BF16), earlier)[0:1]
        rank_row = jnp.where(on_row, rank_row, -1.0)
        rank_col = eye_column(rank_row)
        on_cols.append(rank_col >= 0.0)
        rank_row = rank_row.astype(jnp.int32)
        rank_col = rank_col.astype(jnp.int32)
        length = len_ref[slot]

        def tile(keys, step, carry):
            base = step * TILE
            pick = flag(rank_row == lax.broadcasted_iota(jnp.int32, (TILE, requests), 0) + base)
            place = flag(rank_col == lax.broadcasted_iota(jnp.int32, (requests, TILE), 1) + base)
            qt = dot(pick, q_ref[...]).astype(BF16)
            nope = jnp.concatenate([qt[:, j * 128 : j * 128 + 128] for j in range(QT)], axis=0)
            rot = jnp.concatenate(
                [qt[:, 1024 + j * 64 : 1024 + j * 64 + 64] for j in range(QT)], axis=0
            )
            lat = dot(nope, absorb_ref[...]).astype(BF16)
            scores = dot_nt(lat, lat_ref[slot, :keys]) + dot(rot, rope_ref[slot, :, :keys])
            positions = lax.broadcasted_iota(jnp.int32, (1, keys), 1)
            scores = jnp.where(positions < length, scores * scaling, NEGATIVE)
            top = jnp.max(scores, axis=1, keepdims=True)
            weights = jnp.exp(scores - top).astype(BF16)
            total = jnp.sum(weights.astype(F32), axis=1, keepdims=True)
            summed = dot(weights, lat_ref[slot, :keys])
            attended = (summed / total).astype(BF16)
            valued = dot(attended, value_ref[...]).astype(BF16)
            parts = split3(top + jnp.log(total))
            tail = jnp.zeros((TILE, 128), F32)
            for j in range(QT):
                for k in range(3):
                    piece = parts[k][j * TILE : (j + 1) * TILE]
                    tail = jnp.where(lane == k * 8 + j, piece, tail)
            block = jnp.concatenate(
                [valued[j * TILE : (j + 1) * TILE] for j in range(QT)] + [tail.astype(BF16)],
                axis=1,
            )
            acc[slot] += dot(place, block)
            return carry

        tiles = (count + TILE - 1) // TILE
        for keys in range(KEYS, most + 1, KEYS):

            @pl.when((length > keys - KEYS) & (length <= keys))
            def _():
                lax.fori_loop(0, tiles, lambda step, carry: tile(keys, step, carry), 0)

    logs = [jnp.where(on_cols[s], join3(acc[s, :, 1024:]), NEGATIVE) for s in range(slots)]
    top = logs[0]
    for s in range(1, slots):
        top = jnp.maximum(top, logs[s])
    shares = [jnp.exp(v - top) for v in logs]
    total = shares[0]
    for s in range(1, slots):
        total = total + shares[s]
    log_sum = top + jnp.log(total)
    for j in range(QT):
        out = 0.0
        for s in range(slots):
            out = out + (shares[s] / total)[:, j : j + 1] * acc[s, :, j * 128 : j * 128 + 128]
        out_ref[:, j * 128 : j * 128 + 128] = out.astype(BF16)
    parts = split3(log_sum)
    lane = lax.broadcasted_iota(jnp.int32, (requests, 128), 1)
    tail = jnp.zeros((requests, 128), F32)
    for j in range(QT):
        for k in range(3):
            tail = jnp.where(lane == k * 8 + j, parts[k][:, j : j + 1], tail)
    out_ref[:, 1024:] = tail.astype(BF16)


def attend(node_length, q_all, absorb, value, cache_latent, rope_t, leaf, parent):
    requests = q_all.shape[0]
    slots = cache_latent.shape[0]
    return pl.pallas_call(
        attn_kernel,
        name="attend_nodes",
        out_shape=jax.ShapeDtypeStruct((requests, MSG), BF16),
        in_specs=[pl.BlockSpec(memory_space=pltpu.SMEM)] + [vmem_spec()] * 7,
        out_specs=vmem_spec(),
        scratch_shapes=[VMEM((slots, requests, MSG), F32)],
        compiler_params=pltpu.CompilerParams(vmem_limit_bytes=32 << 20),
    )(node_length, q_all, absorb, value, cache_latent, rope_t, leaf[None, :], parent[None, :])


GAP = 384
SGAP = 256


def layer_kernel(
    msg_ref,
    q_ref,
    routes_ref,
    resid_ref,
    absorb_ref,
    value_ref,
    newlat_ref,
    newrope_ref,
    outw_ref,
    gain_ref,
    router_ref,
    gate_hbm,
    up_hbm,
    down_hbm,
    sgate_hbm,
    sup_hbm,
    sdown_hbm,
    out_ref,
    gate_up,
    down_w,
    sgate_up,
    sdown_w,
    got,
    valued_s,
    csend,
    crecv,
    acc,
    ysend,
    yrecv,
    zsend,
    zrecv,
    hidden_s,
    normed,
    packed,
    arrived,
    own_out,
    cross_send,
    cross_recv,
    ret_send,
    ret_recv,
    share_in,
    share_send,
    share_recv,
    part,
    lsend,
    lrecv,
    hsend,
    hrecv,
    wsem,
    ms,
    mr,
    cs,
    cr,
    ys,
    yr,
    zs,
    zr,
    ns,
    nr,
    ds,
    dr,
    fs,
    fr,
    os_,
    or_,
    rs,
    rr,
    xs,
    xr,
    bs,
    br,
    ls,
    lr,
    hs,
    hr,
):
    g, e, x, y, zl, zh, c = coords()
    mine = x * 4 + y
    ff = gate_hbm.shape[0]
    sff = sgate_hbm.shape[0]
    barrier = pltpu.get_barrier_semaphore()

    def plane(p):
        return dev(p // 4, p % 4, zl, zh, c)

    def hello(i, carry):
        greet(barrier, (lax.rem(g + i, 16), e))
        return carry

    lax.fori_loop(1, 16, hello, 0)
    other = dev(x, y, zl, zh, 1 - c)
    partner = dev(x, y, zl, 1 - zh, c)
    greet(barrier, other)
    greet(barrier, partner)
    for i in range(4):
        for k in range(1, 4):
            greet(barrier, dev(lax.rem(x + i, 4), lax.rem(y + k, 4), zl, zh, c))
    loads = [
        pltpu.make_async_copy(src, dst, wsem.at[i])
        for i, (src, dst) in enumerate(
            [
                (gate_hbm, gate_up.at[pl.ds(0, ff)]),
                (up_hbm, gate_up.at[pl.ds(GAP, ff)]),
                (down_hbm, down_w),
                (sgate_hbm, sgate_up.at[pl.ds(0, sff)]),
                (sup_hbm, sgate_up.at[pl.ds(SGAP, sff)]),
                (sdown_hbm, sdown_w),
            ]
        )
    ]
    for load in loads:
        load.start()
    gate_up[ff:GAP] = jnp.zeros((GAP - ff, gate_up.shape[1]), BF16)
    sgate_up[sff:SGAP] = jnp.zeros((SGAP - sff, sgate_up.shape[1]), BF16)

    scaling = float(128 + 64) ** (-0.5)
    q = q_ref[g]
    nope = jnp.concatenate([q[:, j * 128 : j * 128 + 128] for j in range(QT)], axis=0)
    rot = jnp.concatenate([q[:, 1024 + j * 64 : 1024 + j * 64 + 64] for j in range(QT)], axis=0)
    lat = dot(nope, absorb_ref[...]).astype(BF16)
    scores = dot_nt(lat, newlat_ref[...]) + dot(rot, newrope_ref[...])
    rows = REQ * QT
    qi = lax.broadcasted_iota(jnp.int32, (rows, rows), 0)
    ki = lax.broadcasted_iota(jnp.int32, (rows, rows), 1)
    usable = ((qi % REQ) == (ki // QT)) & ((ki % QT) <= (qi // REQ))
    scores = jnp.where(usable, scores * scaling, NEGATIVE)
    top = jnp.max(scores, axis=1, keepdims=True)
    weights = jnp.where(usable, jnp.exp(scores - top), 0.0).astype(BF16)
    total = jnp.sum(weights.astype(F32), axis=1, keepdims=True)
    summed = dot(weights, newlat_ref[...]) / total
    new_valued = dot(summed.astype(BF16), value_ref[...])
    new_log = top + jnp.log(total)

    pl.semaphore_wait(barrier, 29)

    def send(i, carry):
        peer = lax.rem(g + i, 16)
        remote(msg_ref.at[peer], got.at[g], ms.at[i], mr.at[i], (peer, e)).start()
        return carry

    lax.fori_loop(1, 16, send, 0)
    got[g] = msg_ref[g]

    experts = router_ref.shape[0]
    pairs = (zl // 2, 1 - zl // 2)
    picks, masks = [], []
    for q_ in range(2):
        routes = routes_ref[pl.ds(pairs[q_] * 4, 4)].reshape(32, 128)
        ids = lax.broadcasted_iota(jnp.int32, (32, experts), 1)
        chosen = jnp.zeros((32, experts), F32)
        for k in range(6):
            chosen = jnp.where(routes[:, k : k + 1] == ids, 1.0, chosen)
        ti = lax.broadcasted_iota(jnp.int32, (32, 32), 0)
        tj = lax.broadcasted_iota(jnp.int32, (32, 32), 1)
        before = flag((ti // 8 == tj // 8) & (tj < ti))
        rank = jnp.where(chosen > 0.0, dot(before, chosen.astype(BF16)), -1.0)
        col = lax.broadcasted_iota(jnp.int32, (experts, 128), 1)
        spread = flag(lax.broadcasted_iota(jnp.int32, (experts, 128), 0) == zl * 16 + col // 8)
        spread_rank = dot(rank.astype(BF16), spread)
        ct = lax.broadcasted_iota(jnp.int32, (32, 128), 1)
        rt = lax.broadcasted_iota(jnp.int32, (32, 128), 0)
        pick = jnp.where(
            (spread_rank == (ct % 2).astype(F32)) & (rt // 8 == (ct // 2) % 4), 1.0, 0.0
        )
        picks.append(pick)
        masks.append(chosen)

    def wait(i, carry):
        src = lax.rem(g - i + 16, 16)
        remote(msg_ref.at[src], got.at[src], ms.at[i], mr.at[i], other).wait()
        return carry

    lax.fori_loop(1, 16, wait, 0)

    logs = join3(got[:, :, 1024:].astype(F32).reshape(16 * REQ, 128)).reshape(16, REQ, 8)
    pieces = []
    for j in range(QT):
        log_j = logs[:, :, j : j + 1]
        new_j = new_log[j * REQ : (j + 1) * REQ]
        peak = jnp.maximum(jnp.max(log_j, axis=0), new_j)
        share = jnp.exp(log_j - peak[None])
        new_share = jnp.exp(new_j - peak)
        whole = jnp.sum(share, axis=0) + new_share
        value = jnp.sum(share * got[:, :, j * 128 : j * 128 + 128].astype(F32), axis=0)
        value = value + new_share * new_valued[j * REQ : (j + 1) * REQ]
        pieces.append((value / whole).astype(BF16))
    valued = jnp.concatenate(pieces, axis=0)
    di = lax.broadcasted_iota(jnp.int32, (rows, rows), 0)
    si = lax.broadcasted_iota(jnp.int32, (rows, rows), 1)
    req = ((di % 64) // 16) * 4 + ((di % 16) // 8) * 2 + di // 64
    perm = flag(si == (di % 8) * REQ + req)
    valued_s[...] = dot(perm, valued).astype(BF16).reshape(2, 64, 128)

    csend[...] = dot(valued_s[1 - c], outw_ref[...]).astype(BF16)
    remote(csend, crecv, cs, cr, other).start()
    own = dot(valued_s[c], outw_ref[...])
    remote(csend, crecv, cs, cr, other).wait()
    acc[...] = (own + crecv[...].astype(F32)).reshape(4, 16, 2048)
    ysend[...] = acc[...].astype(BF16)
    for i in (2, 1, 3):
        peer = lax.rem(y + i, 4)
        remote(ysend.at[peer], yrecv.at[i], ys.at[i], yr.at[i], dev(x, peer, zl, zh, c)).start()
    total_row = acc[y]
    for i in (1, 3, 2):
        remote(ysend.at[0], yrecv.at[i], ys.at[i], yr.at[i], other).wait()
        total_row = total_row + yrecv[i].astype(F32)
    zsend[...] = total_row.astype(BF16)
    remote(zsend, zrecv, zs, zr, partner).start()
    total_row = total_row + resid_ref[...].reshape(16, 2048).astype(F32)
    remote(zsend, zrecv, zs, zr, partner).wait()
    hidden = total_row + zrecv[...].astype(F32)
    hidden_s[...] = hidden.reshape(2, 8, 2048)
    square = jnp.mean(hidden * hidden, axis=1, keepdims=True)
    normed[zl] = (hidden * lax.rsqrt(square + EPSILON) * gain_ref[...].astype(F32)).astype(BF16)
    near = zl + 1 - 2 * (zl % 2)
    far = (2 - 2 * (zl // 2), 3 - 2 * (zl // 2))
    row = normed.at[zl]
    remote(row, row, ns.at[0], nr.at[0], dev(x, y, near, zh, c)).start()
    for i in range(2):
        remote(row, row, ns.at[1 + i], nr.at[1 + zl % 2], dev(x, y, far[i], zh, c)).start()

    def pack(chunk):
        tokens = normed[pl.ds(pairs[chunk] * 2, 2)].reshape(32, 2048)
        packed[chunk] = (
            lax.dot_general(
                picks[chunk].astype(BF16),
                tokens,
                (((0,), (0,)), ((), ())),
                preferred_element_type=F32,
            )
            .astype(BF16)
            .reshape(16, 8, 2048)
        )

        def send(i, carry):
            p = lax.rem(mine + i, 16)
            remote(
                packed.at[chunk, p],
                arrived.at[chunk, c, mine],
                ds.at[chunk, i],
                dr.at[chunk, i],
                plane(p),
            ).start()
            return carry

        lax.fori_loop(1, 16, send, 0)
        arrived[chunk, c, mine] = packed[chunk, mine]
        here = arrived.at[chunk, c, mine]
        remote(here, here, fs.at[chunk, 0], fr.at[chunk, 0], other).start()
        logits = dot_nt(tokens, router_ref[...])
        sigma = jax.nn.sigmoid(logits) * masks[chunk]
        route_w = ROUTE_SCALE * sigma / jnp.sum(sigma, axis=1, keepdims=True)
        col = lax.broadcasted_iota(jnp.int32, (experts, 128), 1)
        spread = flag(lax.broadcasted_iota(jnp.int32, (experts, 128), 0) == zl * 16 + col // 8)
        w_hi, w_mid, w_low = split3(route_w)
        return (
            dot(w_hi.astype(BF16), spread)
            + dot(w_mid.astype(BF16), spread)
            + dot(w_low.astype(BF16), spread)
        ) * picks[chunk]

    remote(row, normed.at[near], ns.at[0], nr.at[0], other).wait()
    combine0 = pack(0)
    for i in range(2):
        remote(row, normed.at[far[i]], ns.at[1 + i], nr.at[1 + i], other).wait()
    combine1 = pack(1)
    combines = (combine0, combine1)
    for z in range(4):
        both = normed[z].reshape(2, 8, 2048)
        share_in[x, z] = jnp.where(zh == 0, both[0], both[1])
    for i in (2, 1, 3):
        peer = lax.rem(x + i, 4)
        remote(share_in.at[x], share_in.at[x], xs.at[i], xr.at[i], dev(peer, y, zl, zh, c)).start()

    def forward(chunk):
        def step(i, carry):
            src = lax.rem(mine - i + 16, 16)
            block = arrived.at[chunk, c, src]
            remote(packed.at[chunk, src], block, ds.at[chunk, i], dr.at[chunk, i], other).wait()
            remote(block, block, fs.at[chunk, i], fr.at[chunk, i], other).start()
            return carry

        lax.fori_loop(1, 16, step, 0)

    def crossed(chunk):
        def step(i, carry):
            src = lax.rem(mine - i + 16, 16)
            block = arrived.at[chunk, c, src]
            remote(
                block, arrived.at[chunk, 1 - c, src], fs.at[chunk, i], fr.at[chunk, i], other
            ).wait()
            return carry

        lax.fori_loop(0, 16, step, 0)

    def ffn(rows_in, both_w, gap, units, down):
        val = dot_nt(rows_in, both_w[...])
        hidden = (jax.nn.silu(val[:, :units]) * val[:, gap : gap + units]).astype(BF16)
        return dot(hidden, down[...])

    def routed_ffn(chunk):
        out = ffn(arrived[chunk].reshape(256, 2048), gate_up, GAP, ff, down_w)
        first, second = out[:128], out[128:]
        own_out[chunk] = jnp.where(c == 0, first, second)
        cross_send[chunk] = jnp.where(c == 0, second, first).astype(BF16)
        remote(
            cross_send.at[chunk], cross_recv.at[chunk], os_.at[chunk], or_.at[chunk], other
        ).start()

    def give(chunk):
        remote(
            cross_send.at[chunk], cross_recv.at[chunk], os_.at[chunk], or_.at[chunk], other
        ).wait()
        ret_send[chunk] = (
            (own_out[chunk] + cross_recv[chunk].astype(F32)).astype(BF16).reshape(16, 8, 2048)
        )

        def step(i, carry):
            p = lax.rem(mine + i, 16)
            remote(
                ret_send.at[chunk, p],
                ret_recv.at[chunk, mine],
                rs.at[chunk, i],
                rr.at[chunk, i],
                plane(p),
            ).start()
            return carry

        lax.fori_loop(1, 16, step, 0)
        ret_recv[chunk, mine] = ret_send[chunk, mine]

    forward(0)
    for load in loads[:3]:
        load.wait()
    crossed(0)
    routed_ffn(0)
    forward(1)
    give(0)
    crossed(1)
    routed_ffn(1)

    for load in loads[3:]:
        load.wait()
    for i in range(1, 4):
        src = lax.rem(x - i + 4, 4)
        remote(share_in.at[x], share_in.at[src], xs.at[i], xr.at[i], other).wait()
    shared = ffn(share_in[...].reshape(128, 2048), sgate_up, SGAP, sff, sdown_w)
    share_send[...] = shared.astype(BF16).reshape(4, 32, 2048)
    for i in (2, 1, 3):
        peer = lax.rem(x + i, 4)
        remote(
            share_send.at[peer], share_recv.at[i], bs.at[i], br.at[i], dev(peer, y, zl, zh, c)
        ).start()
    give(1)
    for i in range(1, 4):
        remote(share_send.at[0], share_recv.at[i], bs.at[i], br.at[i], other).wait()
    share_sum = share_send[x].astype(F32)
    for i in range(1, 4):
        share_sum = share_sum + share_recv[i].astype(F32)
    for z in range(4):
        mine_z = share_sum[z * 8 : z * 8 + 8]
        part[z, 0] = jnp.where(zh == 0, mine_z, 0.0)
        part[z, 1] = jnp.where(zh == 1, mine_z, 0.0)

    def take(chunk):
        def step(i, carry):
            src = lax.rem(mine - i + 16, 16)
            remote(
                ret_send.at[chunk, src],
                ret_recv.at[chunk, src],
                rs.at[chunk, i],
                rr.at[chunk, i],
                other,
            ).wait()
            return carry

        lax.fori_loop(1, 16, step, 0)
        back = ret_recv[chunk].reshape(128, 2048)
        w_hi = combines[chunk].astype(BF16)
        w_low = (combines[chunk] - w_hi.astype(F32)).astype(BF16)
        routed = (dot(w_hi, back) + dot(w_low, back)).reshape(2, 2, 8, 2048)
        first = pl.ds(pairs[chunk] * 2, 2)
        part[first] = part[first] + routed
        lsend[first] = part[first].reshape(2, 16, 2048).astype(BF16)

    take(0)
    remote(lsend.at[near], lrecv.at[0], ls.at[0], lr.at[0], dev(x, y, near, zh, c)).start()
    take(1)
    for i in range(2):
        remote(
            lsend.at[far[i]],
            lrecv.at[1 + zl % 2],
            ls.at[1 + i],
            lr.at[1 + zl % 2],
            dev(x, y, far[i], zh, c),
        ).start()
    remote(lsend.at[near], lrecv.at[0], ls.at[0], lr.at[0], other).wait()
    for i in range(2):
        remote(lsend.at[far[i]], lrecv.at[1 + i], ls.at[1 + i], lr.at[1 + i], other).wait()
    both = part[zl].reshape(16, 2048)
    for i in range(3):
        both = both + lrecv[i].astype(F32)
    hsend[...] = jnp.where(zh == 0, both[8:], both[:8]).astype(BF16)
    remote(hsend, hrecv, hs, hr, partner).start()
    kept = hidden_s[zh] + jnp.where(zh == 0, both[:8], both[8:])
    remote(hsend, hrecv, hs, hr, partner).wait()
    out_ref[...] = (kept + hrecv[...].astype(F32)).astype(BF16)


def layer(vmem_args, weights):
    gate, up, down, sgate, sup, sdown = weights
    width = gate.shape[1]
    return pl.pallas_call(
        layer_kernel,
        name="layer",
        out_shape=jax.ShapeDtypeStruct((8, width), BF16),
        in_specs=[vmem_spec()] * len(vmem_args) + [any_spec()] * 6,
        out_specs=vmem_spec(),
        scratch_shapes=[
            VMEM((GAP + gate.shape[0], width), BF16),
            VMEM(down.shape, BF16),
            VMEM((SGAP + sgate.shape[0], width), BF16),
            VMEM(sdown.shape, BF16),
            VMEM((16, REQ, MSG), BF16),
            VMEM((2, 64, 128), BF16),
            VMEM((64, width), BF16),
            VMEM((64, width), BF16),
            VMEM((4, 16, width), F32),
            VMEM((4, 16, width), BF16),
            VMEM((4, 16, width), BF16),
            VMEM((16, width), BF16),
            VMEM((16, width), BF16),
            VMEM((2, 8, width), F32),
            VMEM((4, 16, width), BF16),
            VMEM((2, 16, 8, width), BF16),
            VMEM((2, 2, 16, 8, width), BF16),
            VMEM((2, 128, width), F32),
            VMEM((2, 128, width), BF16),
            VMEM((2, 128, width), BF16),
            VMEM((2, 16, 8, width), BF16),
            VMEM((2, 16, 8, width), BF16),
            VMEM((4, 4, 8, width), BF16),
            VMEM((4, 32, width), BF16),
            VMEM((4, 32, width), BF16),
            VMEM((4, 2, 8, width), F32),
            VMEM((4, 16, width), BF16),
            VMEM((3, 16, width), BF16),
            VMEM((8, width), BF16),
            VMEM((8, width), BF16),
            DMA((6,)),
            DMA((16,)),
            DMA((16,)),
            DMA,
            DMA,
            DMA((4,)),
            DMA((4,)),
            DMA,
            DMA,
            DMA((3,)),
            DMA((3,)),
            DMA((2, 16)),
            DMA((2, 16)),
            DMA((2, 16)),
            DMA((2, 16)),
            DMA((2,)),
            DMA((2,)),
            DMA((2, 16)),
            DMA((2, 16)),
            DMA((4,)),
            DMA((4,)),
            DMA((4,)),
            DMA((4,)),
            DMA((3,)),
            DMA((3,)),
            DMA,
            DMA,
        ],
        compiler_params=pltpu.CompilerParams(
            collective_id=1, has_side_effects=True, vmem_limit_bytes=44 << 20
        ),
    )(*vmem_args, *weights)


def on_device(
    query_nope,
    query_rope,
    absorb_weight,
    value_weight,
    output_weight,
    cache_latent,
    cache_rope,
    node_length,
    new_latent,
    new_rope,
    parent_node,
    leaf_node,
    residual,
    norm_gain,
    router_weight,
    routes,
    expert_gate,
    expert_up,
    expert_down,
    shared_gate,
    shared_up,
    shared_down,
):
    q_all, routes8, resid2 = gather(
        query_nope[:, 0, :], query_rope[:, 0, :].T, routes, residual
    )
    absorb, value = absorb_weight[0], value_weight[0]
    msg = attend(
        node_length,
        q_all.reshape(16 * REQ, -1),
        absorb,
        value,
        cache_latent,
        jnp.swapaxes(cache_rope, 1, 2),
        leaf_node,
        parent_node,
    )
    return layer(
        (
            msg.reshape(16, REQ, MSG),
            q_all,
            routes8,
            resid2,
            absorb,
            value,
            new_latent,
            new_rope.T,
            output_weight,
            norm_gain[None, :],
            router_weight.T,
        ),
        (
            expert_gate[0].T,
            expert_up[0].T,
            expert_down[0],
            shared_gate.T,
            shared_up.T,
            shared_down,
        ),
    )


def solution(mesh):
    in_specs = (
        P("group", "expert", None),
        P("group", "expert", None),
        P("expert", None, None),
        P("expert", None, None),
        P("expert", None),
        P("group", None, None),
        P("group", None, None),
        P("group"),
        P("group", None),
        P("group", None),
        P(),
        P(),
        P(("group", "expert"), None),
        P(),
        P(),
        P(("group", "expert"), None),
        P(("group", "expert"), None, None),
        P(("group", "expert"), None, None),
        P(("group", "expert"), None, None),
        P(None, "group"),
        P(None, "group"),
        P("group", None),
    )
    out_specs = P(("group", "expert"), None)
    return jax.shard_map(
        on_device, mesh=mesh, in_specs=in_specs, out_specs=out_specs, check_vma=False
    )
```

```python
import jax
import jax.numpy as jnp
from jax import lax
from jax.experimental import pallas as pl
from jax.experimental.pallas import tpu as pltpu
from jax.sharding import PartitionSpec as P

ROUTE_SCALE = 2.446
NEGATIVE = -1e30
EPSILON = 1e-06
MESH = pl.DeviceIdType.MESH
F32 = jnp.float32
BF16 = jnp.bfloat16
VMEM = pltpu.VMEM
DMA = pltpu.SemaphoreType.DMA

REQ = 16
QT = 8
MSG = 1024 + 128


def vmem_spec():
    return pl.BlockSpec(memory_space=pltpu.VMEM)


def hbm_spec():
    return pl.BlockSpec(memory_space=pltpu.HBM)


def stay(x):
    return pltpu.with_memory_space_constraint(x, pltpu.HBM)


def start_loads(pairs, sem):
    loads = [pltpu.make_async_copy(src, dst, sem.at[i]) for i, (src, dst) in enumerate(pairs)]
    for load in loads:
        load.start()
    return loads


def coords():
    g = lax.axis_index("group")
    e = lax.axis_index("expert")
    zl, x = g // 4, g % 4
    y, zh, c = e // 4, (e % 4) // 2, e % 2
    return g, e, x, y, zl, zh, c


def dev(x, y, zl, zh, c):
    return (zl * 4 + x, y * 4 + zh * 2 + c)


def remote(src, dst, send, recv, device):
    return pltpu.make_async_remote_copy(
        src_ref=src,
        dst_ref=dst,
        send_sem=send,
        recv_sem=recv,
        device_id=device,
        device_id_type=MESH,
    )


def greet(barrier, device):
    pl.semaphore_signal(barrier, inc=1, device_id=device, device_id_type=MESH)


def dot(a, b):
    return jnp.dot(a, b, preferred_element_type=F32)


def eye_column(row):
    n = row.shape[1]
    same = lax.broadcasted_iota(jnp.int32, (n, n), 0) == lax.broadcasted_iota(jnp.int32, (n, n), 1)
    return jnp.sum(jnp.where(same, row, 0), axis=1, keepdims=True)


def flag(condition):
    return jnp.where(condition, 1.0, 0.0).astype(BF16)


def dot_nt(a, b):
    return lax.dot_general(a, b, (((1,), (1,)), ((), ())), preferred_element_type=F32)


def gather_kernel(
    nope_hbm, rope_hbm, routes_hbm, qall, routes8, nope_v, rope_v, routes_v, mine, wsem, zq, zqr, xq, xqr, rs, rr
):
    g, e, x, y, zl, zh, c = coords()
    loads = start_loads([(nope_hbm, nope_v), (rope_hbm, rope_v), (routes_hbm, routes_v)], wsem)
    barrier = pltpu.get_barrier_semaphore()
    partner = dev(x, y, zl, 1 - zh, c)
    me = zl * 2 + zh
    for i in range(1, 4):
        greet(barrier, dev(lax.rem(x + i, 4), y, zl, zh, c))
        greet(barrier, dev(x, y, lax.rem(zl + i, 4), zh, c))
    for k in (1, 3, 5, 7):
        s = lax.rem(me + k, 8)
        greet(barrier, dev(x, y, s // 2, s % 2, c))

    rows = REQ * QT
    di = lax.broadcasted_iota(jnp.int32, (rows, rows), 0)
    si = lax.broadcasted_iota(jnp.int32, (rows, rows), 1)
    perm = flag(si == (di % REQ) * QT + di // REQ)
    for load in loads:
        load.wait()
    nope = dot(perm, nope_v[...]).astype(BF16)
    rope = dot_nt(perm, rope_v[...]).astype(BF16)
    qall[g] = jnp.concatenate(
        [nope[j * REQ : (j + 1) * REQ] for j in range(QT)]
        + [rope[j * REQ : (j + 1) * REQ] for j in range(QT)],
        axis=1,
    )
    mine[...] = jnp.zeros_like(mine)
    mine[:, 0 : routes_v.shape[1]] = routes_v[...]
    routes8[me] = mine[...]
    pl.semaphore_wait(barrier, 10)

    own = qall.at[g]
    for i in (1, 3, 2):
        remote(own, own, zq.at[i], zqr.at[i], dev(x, y, lax.rem(zl + i, 4), zh, c)).start()
    for k in (1, 3, 2):
        remote(own, own, xq.at[0, k], xqr.at[0, k], dev(lax.rem(x + k, 4), y, zl, zh, c)).start()
    for k in range(1, 8):
        s = lax.rem(me + k, 8)
        remote(mine, routes8.at[me], rs.at[k], rr.at[k], dev(x, y, s // 2, s % 2, c)).start()
    for i in (1, 3, 2):
        block = qall.at[lax.rem(zl - i + 4, 4) * 4 + x]
        remote(own, block, zq.at[i], zqr.at[i], partner).wait()
        for k in (1, 3, 2):
            remote(
                block, block, xq.at[i, k], xqr.at[i, k], dev(lax.rem(x + k, 4), y, zl, zh, c)
            ).start()
    for k in range(1, 8):
        s = lax.rem(me - k + 8, 8)
        remote(mine, routes8.at[s], rs.at[k], rr.at[k], partner).wait()
    for i in range(4):
        for k in (1, 3, 2):
            block = qall.at[lax.rem(zl - i + 4, 4) * 4 + lax.rem(x - k + 4, 4)]
            remote(own, block, xq.at[i, k], xqr.at[i, k], partner).wait()


def gather(nope, rope_t, routes):
    return pl.pallas_call(
        gather_kernel,
        name="gather_queries",
        out_shape=(
            jax.ShapeDtypeStruct((16, REQ, QT * 192), BF16),
            jax.ShapeDtypeStruct((8, 8, 128), jnp.int32),
        ),
        in_specs=[hbm_spec()] * 3,
        out_specs=(vmem_spec(),) * 2,
        scratch_shapes=[
            VMEM(nope.shape, BF16),
            VMEM(rope_t.shape, BF16),
            VMEM(routes.shape, jnp.int32),
            VMEM((8, 128), jnp.int32),
            DMA((3,)),
            DMA((4,)),
            DMA((4,)),
            DMA((4, 4)),
            DMA((4, 4)),
            DMA((8,)),
            DMA((8,)),
        ],
        compiler_params=pltpu.CompilerParams(
            collective_id=0, has_side_effects=True, vmem_limit_bytes=24 << 20
        ),
    )(stay(nope), stay(rope_t), stay(routes))


TILE = 32
KEYS = 256


def split3(v):
    hi = v.astype(BF16)
    rest = v - hi.astype(F32)
    mid = rest.astype(BF16)
    low = (rest - mid.astype(F32)).astype(BF16)
    return hi.astype(F32), mid.astype(F32), low.astype(F32)


def join3(part):
    return part[:, 0:8] + part[:, 8:16] + part[:, 16:24]


def on_path(leaf_row, parent_col, node):
    nodes = parent_col.shape[0]
    ids = lax.broadcasted_iota(jnp.int32, (nodes, leaf_row.shape[1]), 0)
    mid = jnp.sum(jnp.where(leaf_row == ids, parent_col, 0), axis=0, keepdims=True)
    top = jnp.sum(jnp.where(mid == ids, parent_col, 0), axis=0, keepdims=True)
    return (leaf_row == node) | (mid == node) | (top == node)


def attn_kernel(
    q_ref,
    len_hbm,
    absorb_hbm,
    value_hbm,
    lat_hbm,
    rope_hbm,
    leaf_hbm,
    parent_hbm,
    out_ref,
    len_ref,
    absorb_ref,
    value_ref,
    lat_ref,
    rope_ref,
    leaf_ref,
    parent_ref,
    picked,
    done,
    wsem,
):
    g = lax.axis_index("group")
    loads = start_loads(
        [
            (leaf_hbm, leaf_ref),
            (parent_hbm, parent_ref),
            (len_hbm, len_ref),
            (absorb_hbm, absorb_ref),
            (lat_hbm, lat_ref),
            (rope_hbm, rope_ref),
            (value_hbm, value_ref),
        ],
        wsem,
    )
    requests = q_ref.shape[0]
    slots, most = lat_ref.shape[0], lat_ref.shape[1]
    scaling = float(128 + 64) ** (-0.5)
    ids_0 = lax.broadcasted_iota(jnp.int32, (requests, requests), 0)
    ids_1 = lax.broadcasted_iota(jnp.int32, (requests, requests), 1)
    earlier = flag(ids_0 < ids_1)
    done[...] = jnp.zeros_like(done)
    lane = lax.broadcasted_iota(jnp.int32, (TILE, 128), 1)
    for load in loads[:2]:
        load.wait()
    parent_col = eye_column(parent_ref[...])
    places, on_cols, counts = [], [], []
    for slot in range(slots):
        on_row = on_path(leaf_ref[...], parent_col, g * slots + slot)
        row_f = jnp.where(on_row, 1.0, 0.0)
        counts.append(jnp.sum(row_f).astype(jnp.int32))
        rank_row = dot(jnp.broadcast_to(row_f, (8, requests)).astype(BF16), earlier)[0:1]
        rank_row = jnp.where(on_row, rank_row, -1.0)
        rank_col = eye_column(rank_row)
        on_cols.append(rank_col >= 0.0)
        places.append(rank_col.astype(jnp.int32))
        picked[slot] = dot(flag(rank_row.astype(jnp.int32) == ids_0), q_ref[...]).astype(BF16)
    for load in loads[2:]:
        load.wait()

    for slot in range(slots):
        length = len_ref[slot]

        def tile(keys, step, carry):
            here = pl.ds(pl.multiple_of(step * TILE, TILE), TILE)
            qt = picked[slot, here]
            nope = jnp.concatenate([qt[:, j * 128 : j * 128 + 128] for j in range(QT)], axis=0)
            rot = jnp.concatenate(
                [qt[:, 1024 + j * 64 : 1024 + j * 64 + 64] for j in range(QT)], axis=0
            )
            lat = dot(nope, absorb_ref[...]).astype(BF16)
            scores = dot_nt(lat, lat_ref[slot, :keys]) + dot(rot, rope_ref[slot, :, :keys])
            positions = lax.broadcasted_iota(jnp.int32, (1, keys), 1)
            scores = jnp.where(positions < length, scores * scaling, NEGATIVE)
            top = jnp.max(scores, axis=1, keepdims=True)
            weights = jnp.exp(scores - top).astype(BF16)
            total = jnp.sum(weights.astype(F32), axis=1, keepdims=True)
            summed = dot(weights, lat_ref[slot, :keys])
            attended = (summed / total).astype(BF16)
            valued = dot(attended, value_ref[...]).astype(BF16)
            parts = split3(top + jnp.log(total))
            tail = jnp.zeros((TILE, 128), F32)
            for j in range(QT):
                for k in range(3):
                    piece = parts[k][j * TILE : (j + 1) * TILE]
                    tail = jnp.where(lane == k * 8 + j, piece, tail)
            done[slot, here] = jnp.concatenate(
                [valued[j * TILE : (j + 1) * TILE] for j in range(QT)] + [tail.astype(BF16)],
                axis=1,
            )
            return carry

        tiles = (counts[slot] + TILE - 1) // TILE
        for keys in range(KEYS, most + 1, KEYS):

            @pl.when((length > keys - KEYS) & (length <= keys))
            def _():
                lax.fori_loop(0, tiles, lambda step, carry: tile(keys, step, carry), 0)

    acc = [dot(flag(places[s] == ids_1), done[s]) for s in range(slots)]
    logs = [jnp.where(on_cols[s], join3(acc[s][:, 1024:]), NEGATIVE) for s in range(slots)]
    top = logs[0]
    for s in range(1, slots):
        top = jnp.maximum(top, logs[s])
    shares = [jnp.exp(v - top) for v in logs]
    total = shares[0]
    for s in range(1, slots):
        total = total + shares[s]
    log_sum = top + jnp.log(total)
    for j in range(QT):
        out = 0.0
        for s in range(slots):
            out = out + (shares[s] / total)[:, j : j + 1] * acc[s][:, j * 128 : j * 128 + 128]
        out_ref[:, j * 128 : j * 128 + 128] = out.astype(BF16)
    parts = split3(log_sum)
    lane = lax.broadcasted_iota(jnp.int32, (requests, 128), 1)
    tail = jnp.zeros((requests, 128), F32)
    for j in range(QT):
        for k in range(3):
            tail = jnp.where(lane == k * 8 + j, parts[k][:, j : j + 1], tail)
    out_ref[:, 1024:] = tail.astype(BF16)


def attend(node_length, q_all, absorb, value, cache_latent, rope_t, leaf, parent):
    requests = q_all.shape[0]
    slots = cache_latent.shape[0]
    return pl.pallas_call(
        attn_kernel,
        name="attend_nodes",
        out_shape=jax.ShapeDtypeStruct((requests, MSG), BF16),
        in_specs=[vmem_spec()] + [hbm_spec()] * 7,
        out_specs=vmem_spec(),
        scratch_shapes=[
            pltpu.SMEM(node_length.shape, jnp.int32),
            VMEM(absorb.shape, BF16),
            VMEM(value.shape, BF16),
            VMEM(cache_latent.shape, BF16),
            VMEM(rope_t.shape, BF16),
            VMEM((1, leaf.shape[0]), jnp.int32),
            VMEM((1, parent.shape[0]), jnp.int32),
            VMEM((slots, requests, q_all.shape[1]), BF16),
            VMEM((slots, requests, MSG), BF16),
            DMA((7,)),
        ],
        compiler_params=pltpu.CompilerParams(vmem_limit_bytes=32 << 20),
    )(
        q_all,
        *map(
            stay,
            (
                node_length,
                absorb,
                value,
                cache_latent,
                rope_t,
                leaf[None, :],
                parent[None, :],
            ),
        ),
    )


GAP = 384
SGAP = 256


def layer_kernel(
    msg_ref,
    q_ref,
    routes_ref,
    gain_ref,
    absorb_hbm,
    value_hbm,
    newlat_hbm,
    newrope_hbm,
    outw_hbm,
    resid_hbm,
    router_hbm,
    gate_hbm,
    up_hbm,
    down_hbm,
    sgate_hbm,
    sup_hbm,
    sdown_hbm,
    out_ref,
    absorb_ref,
    value_ref,
    newlat_ref,
    newrope_ref,
    outw_ref,
    resid_ref,
    router_ref,
    gate_up,
    down_w,
    sgate_up,
    sdown_w,
    got,
    valued_s,
    csend,
    crecv,
    acc,
    ysend,
    yrecv,
    zsend,
    zrecv,
    hidden_s,
    normed,
    packed,
    arrived,
    own_out,
    cross_send,
    cross_recv,
    ret_send,
    ret_recv,
    share_in,
    share_send,
    share_recv,
    part,
    lsend,
    lrecv,
    wsem,
    ms,
    mr,
    cs,
    cr,
    ys,
    yr,
    ns,
    nr,
    ds,
    dr,
    fs,
    fr,
    os_,
    or_,
    rs,
    rr,
    xs,
    xr,
    bs,
    br,
    ls,
    lr,
):
    g, e, x, y, zl, zh, c = coords()
    mine = x * 4 + y
    ff = gate_hbm.shape[0]
    sff = sgate_hbm.shape[0]
    barrier = pltpu.get_barrier_semaphore()

    def plane(p):
        return dev(p // 4, p % 4, zl, zh, c)

    def hello(i, carry):
        greet(barrier, (lax.rem(g + i, 16), e))
        return carry

    lax.fori_loop(1, 16, hello, 0)
    other = dev(x, y, zl, zh, 1 - c)
    partner = dev(x, y, zl, 1 - zh, c)
    greet(barrier, other)
    greet(barrier, partner)
    for i in range(4):
        for k in range(1, 4):
            greet(barrier, dev(lax.rem(x + i, 4), lax.rem(y + k, 4), zl, zh, c))
    lines = (zl, zl + 1 - 2 * (zl % 2), zl + 2 - 4 * (zl // 2), 3 - zl)
    halves = (zh, 1 - zh)

    def line(d):
        return dev(x, y, lines[d // 2], halves[d % 2], c)

    for d in (3, 5, 7):
        greet(barrier, line(d))
    loads = start_loads(
        [
            (absorb_hbm, absorb_ref),
            (value_hbm, value_ref),
            (newlat_hbm, newlat_ref),
            (newrope_hbm, newrope_ref),
            (outw_hbm, outw_ref),
            (resid_hbm, resid_ref),
            (router_hbm, router_ref),
            (gate_hbm, gate_up.at[pl.ds(0, ff)]),
            (up_hbm, gate_up.at[pl.ds(GAP, ff)]),
            (down_hbm, down_w),
            (sgate_hbm, sgate_up.at[pl.ds(0, sff)]),
            (sup_hbm, sgate_up.at[pl.ds(SGAP, sff)]),
            (sdown_hbm, sdown_w),
        ],
        wsem,
    )
    gate_up[ff:GAP] = jnp.zeros((GAP - ff, gate_up.shape[1]), BF16)
    sgate_up[sff:SGAP] = jnp.zeros((SGAP - sff, sgate_up.shape[1]), BF16)

    scaling = float(128 + 64) ** (-0.5)
    for load in loads[:4]:
        load.wait()
    q = q_ref[g]
    nope = jnp.concatenate([q[:, j * 128 : j * 128 + 128] for j in range(QT)], axis=0)
    rot = jnp.concatenate([q[:, 1024 + j * 64 : 1024 + j * 64 + 64] for j in range(QT)], axis=0)
    lat = dot(nope, absorb_ref[...]).astype(BF16)
    scores = dot_nt(lat, newlat_ref[...]) + dot(rot, newrope_ref[...])
    rows = REQ * QT
    qi = lax.broadcasted_iota(jnp.int32, (rows, rows), 0)
    ki = lax.broadcasted_iota(jnp.int32, (rows, rows), 1)
    usable = ((qi % REQ) == (ki // QT)) & ((ki % QT) <= (qi // REQ))
    scores = jnp.where(usable, scores * scaling, NEGATIVE)
    top = jnp.max(scores, axis=1, keepdims=True)
    weights = jnp.where(usable, jnp.exp(scores - top), 0.0).astype(BF16)
    total = jnp.sum(weights.astype(F32), axis=1, keepdims=True)
    summed = dot(weights, newlat_ref[...]) / total
    new_valued = dot(summed.astype(BF16), value_ref[...])
    new_log = top + jnp.log(total)

    pl.semaphore_wait(barrier, 32)

    def send(i, carry):
        peer = lax.rem(g + i, 16)
        remote(msg_ref.at[peer], got.at[g], ms.at[i], mr.at[i], (peer, e)).start()
        return carry

    lax.fori_loop(1, 16, send, 0)
    got[g] = msg_ref[g]

    experts = router_ref.shape[0]
    pairs = (zl // 2, 1 - zl // 2)
    picks, masks = [], []
    for q_ in range(2):
        routes = routes_ref[pl.ds(pairs[q_] * 4, 4)].reshape(32, 128)
        ids = lax.broadcasted_iota(jnp.int32, (32, experts), 1)
        chosen = jnp.zeros((32, experts), F32)
        for k in range(6):
            chosen = jnp.where(routes[:, k : k + 1] == ids, 1.0, chosen)
        ti = lax.broadcasted_iota(jnp.int32, (32, 32), 0)
        tj = lax.broadcasted_iota(jnp.int32, (32, 32), 1)
        before = flag((ti // 8 == tj // 8) & (tj < ti))
        rank = jnp.where(chosen > 0.0, dot(before, chosen.astype(BF16)), -1.0)
        col = lax.broadcasted_iota(jnp.int32, (experts, 128), 1)
        spread = flag(lax.broadcasted_iota(jnp.int32, (experts, 128), 0) == zl * 16 + col // 8)
        spread_rank = dot(rank.astype(BF16), spread)
        ct = lax.broadcasted_iota(jnp.int32, (32, 128), 1)
        rt = lax.broadcasted_iota(jnp.int32, (32, 128), 0)
        pick = jnp.where(
            (spread_rank == (ct % 2).astype(F32)) & (rt // 8 == (ct // 2) % 4), 1.0, 0.0
        )
        picks.append(pick)
        masks.append(chosen)

    def wait(i, carry):
        src = lax.rem(g - i + 16, 16)
        remote(msg_ref.at[src], got.at[src], ms.at[i], mr.at[i], other).wait()
        return carry

    lax.fori_loop(1, 16, wait, 0)

    logs = join3(got[:, :, 1024:].astype(F32).reshape(16 * REQ, 128)).reshape(16, REQ, 8)
    pieces = []
    for j in range(QT):
        log_j = logs[:, :, j : j + 1]
        new_j = new_log[j * REQ : (j + 1) * REQ]
        peak = jnp.maximum(jnp.max(log_j, axis=0), new_j)
        share = jnp.exp(log_j - peak[None])
        new_share = jnp.exp(new_j - peak)
        whole = jnp.sum(share, axis=0) + new_share
        value = jnp.sum(share * got[:, :, j * 128 : j * 128 + 128].astype(F32), axis=0)
        value = value + new_share * new_valued[j * REQ : (j + 1) * REQ]
        pieces.append((value / whole).astype(BF16))
    valued = jnp.concatenate(pieces, axis=0)
    di = lax.broadcasted_iota(jnp.int32, (rows, rows), 0)
    si = lax.broadcasted_iota(jnp.int32, (rows, rows), 1)
    req = ((di % 64) // 16) * 4 + ((di % 16) // 8) * 2 + di // 64
    perm = flag(si == (di % 8) * REQ + req)
    valued_s[...] = dot(perm, valued).astype(BF16).reshape(2, 64, 128)

    for load in loads[4:7]:
        load.wait()
    csend[...] = dot(valued_s[1 - c], outw_ref[...]).astype(BF16)
    remote(csend, crecv, cs, cr, other).start()
    own = dot(valued_s[c], outw_ref[...])
    remote(csend, crecv, cs, cr, other).wait()
    acc[...] = (own + crecv[...].astype(F32)).reshape(4, 16, 2048)
    ysend[...] = acc[...].astype(BF16)
    for i in (2, 1, 3):
        peer = lax.rem(y + i, 4)
        remote(ysend.at[peer], yrecv.at[i], ys.at[i], yr.at[i], dev(x, peer, zl, zh, c)).start()
    total_row = acc[y]
    for i in (1, 3, 2):
        remote(ysend.at[0], yrecv.at[i], ys.at[i], yr.at[i], other).wait()
        total_row = total_row + yrecv[i].astype(F32)
    own_8 = lax.broadcasted_iota(jnp.int32, (16, 1), 0) // 8 == zh
    resid = resid_ref[...].astype(F32)
    total_row = total_row + jnp.where(own_8, jnp.concatenate([resid, resid], axis=0), 0.0)
    zsend[...] = total_row.astype(BF16)
    for d in (1, 3, 2, 5, 7, 4, 6):
        remote(zsend, zrecv.at[d], ns.at[d], nr.at[d], line(d)).start()

    def column(d):
        remote(zsend, zrecv.at[d], ns.at[d], nr.at[d], other).wait()
        return zrecv[d].astype(F32)

    def norm(hidden):
        square = jnp.mean(hidden * hidden, axis=1, keepdims=True)
        return (hidden * lax.rsqrt(square + EPSILON) * gain_ref[...].astype(F32)).astype(BF16)

    hidden = total_row + column(1)
    hidden_s[...] = hidden.reshape(2, 8, 2048)
    normed[zl] = norm(hidden)
    share_in[x, zl] = normed[zl].reshape(2, 8, 2048)[0]

    @pl.when(zh == 1)
    def _():
        share_in[x, zl] = normed[zl].reshape(2, 8, 2048)[1]

    for i in (2, 1, 3):
        block = share_in.at[x, zl]
        peer = dev(lax.rem(x + i, 4), y, zl, zh, c)
        remote(block, block, xs.at[0, i], xr.at[0, i], peer).start()

    def pack(chunk):
        tokens = normed[pl.ds(pairs[chunk] * 2, 2)].reshape(32, 2048)
        packed[chunk] = (
            lax.dot_general(
                picks[chunk].astype(BF16),
                tokens,
                (((0,), (0,)), ((), ())),
                preferred_element_type=F32,
            )
            .astype(BF16)
            .reshape(16, 8, 2048)
        )

        def send(i, carry):
            p = lax.rem(mine + i, 16)
            remote(
                packed.at[chunk, p],
                arrived.at[chunk, c, mine],
                ds.at[chunk, i],
                dr.at[chunk, i],
                plane(p),
            ).start()
            return carry

        lax.fori_loop(1, 16, send, 0)
        arrived[chunk, c, mine] = packed[chunk, mine]
        here = arrived.at[chunk, c, mine]
        remote(here, here, fs.at[chunk, 0], fr.at[chunk, 0], other).start()
        logits = dot_nt(tokens, router_ref[...])
        sigma = jax.nn.sigmoid(logits) * masks[chunk]
        route_w = ROUTE_SCALE * sigma / jnp.sum(sigma, axis=1, keepdims=True)
        col = lax.broadcasted_iota(jnp.int32, (experts, 128), 1)
        spread = flag(lax.broadcasted_iota(jnp.int32, (experts, 128), 0) == zl * 16 + col // 8)
        w_hi, w_mid, w_low = split3(route_w)
        return (
            dot(w_hi.astype(BF16), spread)
            + dot(w_mid.astype(BF16), spread)
            + dot(w_low.astype(BF16), spread)
        ) * picks[chunk]

    normed[lines[1]] = norm(column(2) + column(3))
    combine0 = pack(0)
    normed[lines[2]] = norm(column(4) + column(5))
    normed[lines[3]] = norm(column(6) + column(7))
    combine1 = pack(1)
    combines = (combine0, combine1)
    for d in range(1, 4):
        both = normed[lines[d]].reshape(2, 8, 2048)
        share_in[x, lines[d]] = jnp.where(zh == 0, both[0], both[1])
    for i in (1, 3, 2):
        block = share_in.at[lax.rem(x - i + 4, 4), zl]
        remote(share_in.at[x, zl], block, xs.at[0, i], xr.at[0, i], other).wait()
        for d in range(1, 4):
            remote(block, block, xs.at[d, i], xr.at[d, i], line(2 * d)).start()

    def forward(chunk):
        def step(i, carry):
            src = lax.rem(mine - i + 16, 16)
            block = arrived.at[chunk, c, src]
            remote(packed.at[chunk, src], block, ds.at[chunk, i], dr.at[chunk, i], other).wait()
            remote(block, block, fs.at[chunk, i], fr.at[chunk, i], other).start()
            return carry

        lax.fori_loop(1, 16, step, 0)

    def crossed(chunk):
        def step(i, carry):
            src = lax.rem(mine - i + 16, 16)
            block = arrived.at[chunk, c, src]
            remote(
                block, arrived.at[chunk, 1 - c, src], fs.at[chunk, i], fr.at[chunk, i], other
            ).wait()
            return carry

        lax.fori_loop(0, 16, step, 0)

    def ffn(rows_in, both_w, gap, units, down):
        val = dot_nt(rows_in, both_w[...])
        hidden = (jax.nn.silu(val[:, :units]) * val[:, gap : gap + units]).astype(BF16)
        return dot(hidden, down[...])

    def routed_ffn(chunk):
        out = ffn(arrived[chunk].reshape(256, 2048), gate_up, GAP, ff, down_w)
        first, second = out[:128], out[128:]
        own_out[chunk] = jnp.where(c == 0, first, second)
        cross_send[chunk] = jnp.where(c == 0, second, first).astype(BF16)
        remote(
            cross_send.at[chunk], cross_recv.at[chunk], os_.at[chunk], or_.at[chunk], other
        ).start()

    def give(chunk):
        remote(
            cross_send.at[chunk], cross_recv.at[chunk], os_.at[chunk], or_.at[chunk], other
        ).wait()
        ret_send[chunk] = (
            (own_out[chunk] + cross_recv[chunk].astype(F32)).astype(BF16).reshape(16, 8, 2048)
        )

        def step(i, carry):
            p = lax.rem(mine + i, 16)
            remote(
                ret_send.at[chunk, p],
                ret_recv.at[chunk, mine],
                rs.at[chunk, i],
                rr.at[chunk, i],
                plane(p),
            ).start()
            return carry

        lax.fori_loop(1, 16, step, 0)
        ret_recv[chunk, mine] = ret_send[chunk, mine]

    forward(0)
    for load in loads[7:10]:
        load.wait()
    crossed(0)
    routed_ffn(0)
    forward(1)
    give(0)
    crossed(1)
    routed_ffn(1)

    for load in loads[10:]:
        load.wait()
    for i in (1, 3, 2):
        src = lax.rem(x - i + 4, 4)
        for d in range(1, 4):
            remote(
                share_in.at[src, zl], share_in.at[src, lines[d]], xs.at[d, i], xr.at[d, i], other
            ).wait()
    shared = ffn(share_in[...].reshape(128, 2048), sgate_up, SGAP, sff, sdown_w)
    share_send[...] = shared.astype(BF16).reshape(4, 32, 2048)
    for i in (2, 1, 3):
        peer = lax.rem(x + i, 4)
        remote(
            share_send.at[peer], share_recv.at[i], bs.at[i], br.at[i], dev(peer, y, zl, zh, c)
        ).start()
    give(1)
    for i in range(1, 4):
        remote(share_send.at[0], share_recv.at[i], bs.at[i], br.at[i], other).wait()
    share_sum = share_send[x].astype(F32)
    for i in range(1, 4):
        share_sum = share_sum + share_recv[i].astype(F32)
    for z in range(4):
        mine_z = share_sum[z * 8 : z * 8 + 8]
        part[z, 0] = jnp.where(zh == 0, mine_z, 0.0)
        part[z, 1] = jnp.where(zh == 1, mine_z, 0.0)

    def take(chunk):
        def step(i, carry):
            src = lax.rem(mine - i + 16, 16)
            remote(
                ret_send.at[chunk, src],
                ret_recv.at[chunk, src],
                rs.at[chunk, i],
                rr.at[chunk, i],
                other,
            ).wait()
            return carry

        lax.fori_loop(1, 16, step, 0)
        back = ret_recv[chunk].reshape(128, 2048)
        w_hi = combines[chunk].astype(BF16)
        w_low = (combines[chunk] - w_hi.astype(F32)).astype(BF16)
        routed = (dot(w_hi, back) + dot(w_low, back)).reshape(2, 2, 8, 2048)
        first = pl.ds(pairs[chunk] * 2, 2)
        part[first] = part[first] + routed
        lsend[first] = part[first].astype(BF16)

    def hand(d):
        block = lsend.at[lines[d // 2], halves[d % 2]]
        return remote(block, lrecv.at[d], ls.at[d], lr.at[d], line(d))

    take(0)
    for d in (1, 3, 2):
        hand(d).start()
    take(1)
    for d in (5, 7, 4, 6):
        hand(d).start()
    result = hidden_s[zh] + part[zl, zh]
    for d in (2, 1, 3, 4, 6, 5, 7):
        hand(d).wait()
        result = result + lrecv[d].astype(F32)
    out_ref[...] = result.astype(BF16)


def layer(vmem_args, more, weights):
    gate, up, down, sgate, sup, sdown = weights
    width = gate.shape[1]
    return pl.pallas_call(
        layer_kernel,
        name="layer",
        out_shape=jax.ShapeDtypeStruct((8, width), BF16),
        in_specs=[vmem_spec()] * len(vmem_args) + [hbm_spec()] * (len(more) + 6),
        out_specs=vmem_spec(),
        scratch_shapes=[VMEM(m.shape, BF16) for m in more]
        + [
            VMEM((GAP + gate.shape[0], width), BF16),
            VMEM(down.shape, BF16),
            VMEM((SGAP + sgate.shape[0], width), BF16),
            VMEM(sdown.shape, BF16),
            VMEM((16, REQ, MSG), BF16),
            VMEM((2, 64, 128), BF16),
            VMEM((64, width), BF16),
            VMEM((64, width), BF16),
            VMEM((4, 16, width), F32),
            VMEM((4, 16, width), BF16),
            VMEM((4, 16, width), BF16),
            VMEM((16, width), BF16),
            VMEM((8, 16, width), BF16),
            VMEM((2, 8, width), F32),
            VMEM((4, 16, width), BF16),
            VMEM((2, 16, 8, width), BF16),
            VMEM((2, 2, 16, 8, width), BF16),
            VMEM((2, 128, width), F32),
            VMEM((2, 128, width), BF16),
            VMEM((2, 128, width), BF16),
            VMEM((2, 16, 8, width), BF16),
            VMEM((2, 16, 8, width), BF16),
            VMEM((4, 4, 8, width), BF16),
            VMEM((4, 32, width), BF16),
            VMEM((4, 32, width), BF16),
            VMEM((4, 2, 8, width), F32),
            VMEM((4, 2, 8, width), BF16),
            VMEM((8, 8, width), BF16),
            DMA((13,)),
            DMA((16,)),
            DMA((16,)),
            DMA,
            DMA,
            DMA((4,)),
            DMA((4,)),
            DMA((8,)),
            DMA((8,)),
            DMA((2, 16)),
            DMA((2, 16)),
            DMA((2, 16)),
            DMA((2, 16)),
            DMA((2,)),
            DMA((2,)),
            DMA((2, 16)),
            DMA((2, 16)),
            DMA((4, 4)),
            DMA((4, 4)),
            DMA((4,)),
            DMA((4,)),
            DMA((8,)),
            DMA((8,)),
        ],
        compiler_params=pltpu.CompilerParams(
            collective_id=1, has_side_effects=True, vmem_limit_bytes=44 << 20
        ),
    )(*vmem_args, *map(stay, more), *map(stay, weights))


def on_device(
    query_nope,
    query_rope,
    absorb_weight,
    value_weight,
    output_weight,
    cache_latent,
    cache_rope,
    node_length,
    new_latent,
    new_rope,
    parent_node,
    leaf_node,
    residual,
    norm_gain,
    router_weight,
    routes,
    expert_gate,
    expert_up,
    expert_down,
    shared_gate,
    shared_up,
    shared_down,
):
    q_all, routes8 = gather(query_nope[:, 0, :], query_rope[:, 0, :].T, routes)
    absorb, value = absorb_weight[0], value_weight[0]
    msg = attend(
        node_length,
        q_all.reshape(16 * REQ, -1),
        absorb,
        value,
        cache_latent,
        jnp.swapaxes(cache_rope, 1, 2),
        leaf_node,
        parent_node,
    )
    return layer(
        (
            msg.reshape(16, REQ, MSG),
            q_all,
            routes8,
            norm_gain[None, :],
        ),
        (
            absorb,
            value,
            new_latent,
            new_rope.T,
            output_weight,
            residual,
            router_weight.T,
        ),
        (
            expert_gate[0].T,
            expert_up[0].T,
            expert_down[0],
            shared_gate.T,
            shared_up.T,
            shared_down,
        ),
    )


def solution(mesh):
    in_specs = (
        P("group", "expert", None),
        P("group", "expert", None),
        P("expert", None, None),
        P("expert", None, None),
        P("expert", None),
        P("group", None, None),
        P("group", None, None),
        P("group"),
        P("group", None),
        P("group", None),
        P(),
        P(),
        P(("group", "expert"), None),
        P(),
        P(),
        P(("group", "expert"), None),
        P(("group", "expert"), None, None),
        P(("group", "expert"), None, None),
        P(("group", "expert"), None, None),
        P(None, "group"),
        P(None, "group"),
        P("group", None),
    )
    out_specs = P(("group", "expert"), None)
    return jax.shard_map(
        on_device, mesh=mesh, in_specs=in_specs, out_specs=out_specs, check_vma=False
    )
```

```python
import jax
import jax.numpy as jnp
from jax import lax
from jax.experimental import pallas as pl
from jax.experimental.pallas import tpu as pltpu
from jax.sharding import PartitionSpec as P

ROUTE_SCALE = 2.446
NEGATIVE = -1e30
EPSILON = 1e-06
MESH = pl.DeviceIdType.MESH
F32 = jnp.float32
BF16 = jnp.bfloat16
VMEM = pltpu.VMEM
DMA = pltpu.SemaphoreType.DMA

REQ = 16
QT = 8
MSG = 1024 + 128


def vmem_spec():
    return pl.BlockSpec(memory_space=pltpu.VMEM)


def hbm_spec():
    return pl.BlockSpec(memory_space=pltpu.HBM)


def stay(x):
    return pltpu.with_memory_space_constraint(x, pltpu.HBM)


def start_loads(pairs, sem):
    loads = [pltpu.make_async_copy(src, dst, sem.at[i]) for i, (src, dst) in enumerate(pairs)]
    for load in loads:
        load.start()
    return loads


def coords():
    g = lax.axis_index("group")
    e = lax.axis_index("expert")
    zl, x = g // 4, g % 4
    y, zh, c = e // 4, (e % 4) // 2, e % 2
    return g, e, x, y, zl, zh, c


def dev(x, y, zl, zh, c):
    return (zl * 4 + x, y * 4 + zh * 2 + c)


def remote(src, dst, send, recv, device):
    return pltpu.make_async_remote_copy(
        src_ref=src,
        dst_ref=dst,
        send_sem=send,
        recv_sem=recv,
        device_id=device,
        device_id_type=MESH,
    )


def greet(barrier, device):
    pl.semaphore_signal(barrier, inc=1, device_id=device, device_id_type=MESH)


def dot(a, b):
    return jnp.dot(a, b, preferred_element_type=F32)


def eye_column(row):
    n = row.shape[1]
    same = lax.broadcasted_iota(jnp.int32, (n, n), 0) == lax.broadcasted_iota(jnp.int32, (n, n), 1)
    return jnp.sum(jnp.where(same, row, 0), axis=1, keepdims=True)


def flag(condition):
    return jnp.where(condition, 1.0, 0.0).astype(BF16)


def dot_nt(a, b):
    return lax.dot_general(a, b, (((1,), (1,)), ((), ())), preferred_element_type=F32)


def on_path(leaf_row, parent_col, node):
    nodes = parent_col.shape[0]
    ids = lax.broadcasted_iota(jnp.int32, (nodes, leaf_row.shape[1]), 0)
    mid = jnp.sum(jnp.where(leaf_row == ids, parent_col, 0), axis=0, keepdims=True)
    top = jnp.sum(jnp.where(mid == ids, parent_col, 0), axis=0, keepdims=True)
    return (leaf_row == node) | (mid == node) | (top == node)


def gather_kernel(
    nope_hbm,
    rope_hbm,
    routes_hbm,
    leaf_hbm,
    parent_hbm,
    outw_hbm,
    lat_hbm,
    krope_hbm,
    absorb_hbm,
    value_hbm,
    qall,
    routes8,
    pick_ref,
    place_ref,
    outw,
    lat_ref,
    krope_ref,
    absorb_ref,
    value_ref,
    nope_v,
    rope_v,
    routes_v,
    leaf_v,
    parent_v,
    mine,
    wsem,
    zq,
    zqr,
    xq,
    xqr,
    rs,
    rr,
    ys,
    yr,
    cs,
    cr,
):
    g, e, x, y, zl, zh, c = coords()
    half = outw.shape[3]
    loads = start_loads(
        [
            (nope_hbm, nope_v),
            (rope_hbm, rope_v),
            (routes_hbm, routes_v),
            (leaf_hbm, leaf_v),
            (parent_hbm, parent_v),
            (outw_hbm.at[:, pl.ds(0, half)], outw.at[y, c]),
            (lat_hbm, lat_ref),
            (krope_hbm, krope_ref),
            (absorb_hbm, absorb_ref),
            (value_hbm, value_ref),
        ],
        wsem,
    )
    barrier = pltpu.get_barrier_semaphore()
    partner = dev(x, y, zl, 1 - zh, c)
    other = dev(x, y, zl, zh, 1 - c)
    me = zl * 2 + zh
    for i in range(1, 4):
        greet(barrier, dev(lax.rem(x + i, 4), y, zl, zh, c))
        greet(barrier, dev(x, y, lax.rem(zl + i, 4), zh, c))
        greet(barrier, dev(x, lax.rem(y + i, 4), zl, zh, c))
    greet(barrier, other)
    for k in (1, 3, 5, 7):
        s = lax.rem(me + k, 8)
        greet(barrier, dev(x, y, s // 2, s % 2, c))

    rows = REQ * QT
    di = lax.broadcasted_iota(jnp.int32, (rows, rows), 0)
    si = lax.broadcasted_iota(jnp.int32, (rows, rows), 1)
    perm = flag(si == (di % REQ) * QT + di // REQ)
    for load in loads[:3]:
        load.wait()
    nope = dot(perm, nope_v[...]).astype(BF16)
    rope = dot_nt(perm, rope_v[...]).astype(BF16)
    qall[g] = jnp.concatenate(
        [nope[j * REQ : (j + 1) * REQ] for j in range(QT)]
        + [rope[j * REQ : (j + 1) * REQ] for j in range(QT)],
        axis=1,
    )
    mine[...] = jnp.zeros_like(mine)
    mine[:, 0 : routes_v.shape[1]] = routes_v[...]
    routes8[me] = mine[...]
    pl.semaphore_wait(barrier, 14)

    own = qall.at[g]
    for i in (1, 3, 2):
        remote(own, own, zq.at[i], zqr.at[i], dev(x, y, lax.rem(zl + i, 4), zh, c)).start()
    for k in (1, 3, 2):
        remote(own, own, xq.at[0, k], xqr.at[0, k], dev(lax.rem(x + k, 4), y, zl, zh, c)).start()
    for load in loads[3:6]:
        load.wait()
    own_w = outw.at[y, c]
    for i in (1, 3, 2):
        remote(own_w, own_w, ys.at[i], yr.at[i], dev(x, lax.rem(y + i, 4), zl, zh, c)).start()
    remote(own_w, own_w, cs.at[0], cr.at[0], other).start()
    for k in range(1, 8):
        s = lax.rem(me + k, 8)
        remote(mine, routes8.at[me], rs.at[k], rr.at[k], dev(x, y, s // 2, s % 2, c)).start()

    def pass_on(i):
        block = qall.at[lax.rem(zl - i + 4, 4) * 4 + x]
        remote(own, block, zq.at[i], zqr.at[i], partner).wait()
        for k in (1, 3, 2):
            remote(
                block, block, xq.at[i, k], xqr.at[i, k], dev(lax.rem(x + k, 4), y, zl, zh, c)
            ).start()

    pass_on(1)
    pass_on(3)
    pass_on(2)

    slots, _, requests = pick_ref.shape
    ids_0 = lax.broadcasted_iota(jnp.int32, (requests, requests), 0)
    ids_1 = lax.broadcasted_iota(jnp.int32, (requests, requests), 1)
    earlier = flag(ids_0 < ids_1)
    parent_col = eye_column(parent_v[...])
    for slot in range(slots):
        on_row = on_path(leaf_v[...], parent_col, g * slots + slot)
        row_f = jnp.where(on_row, 1.0, 0.0)
        rank_row = dot(jnp.broadcast_to(row_f, (8, requests)).astype(BF16), earlier)[0:1]
        rank_row = jnp.where(on_row, rank_row, -1.0)
        pick_ref[slot] = flag(rank_row.astype(jnp.int32) == ids_0)
        place_ref[slot] = flag(eye_column(rank_row).astype(jnp.int32) == ids_1)

    for i in (1, 3, 2):
        block = outw.at[lax.rem(y - i + 4, 4), c]
        remote(own_w, block, ys.at[i], yr.at[i], other).wait()
        remote(block, block, cs.at[i], cr.at[i], other).start()
    for load in loads[6:]:
        load.wait()
    for k in range(1, 8):
        s = lax.rem(me - k + 8, 8)
        remote(mine, routes8.at[s], rs.at[k], rr.at[k], partner).wait()
    for i in range(4):
        for k in (1, 3, 2):
            block = qall.at[lax.rem(zl - i + 4, 4) * 4 + lax.rem(x - k + 4, 4)]
            remote(own, block, xq.at[i, k], xqr.at[i, k], partner).wait()
    for i in range(4):
        y_of = lax.rem(y - i + 4, 4)
        remote(outw.at[y_of, c], outw.at[y_of, 1 - c], cs.at[i], cr.at[i], other).wait()


def gather(nope, rope_t, routes, leaf, parent, outw, lat, krope_t, absorb, value):
    requests = leaf.shape[0]
    slots = lat.shape[0]
    return pl.pallas_call(
        gather_kernel,
        name="gather_queries",
        out_shape=(
            jax.ShapeDtypeStruct((16, REQ, QT * 192), BF16),
            jax.ShapeDtypeStruct((8, 8, 128), jnp.int32),
            jax.ShapeDtypeStruct((slots, requests, requests), BF16),
            jax.ShapeDtypeStruct((slots, requests, requests), BF16),
            jax.ShapeDtypeStruct((4, 2, outw.shape[0], outw.shape[1] // 2), BF16),
            jax.ShapeDtypeStruct(lat.shape, BF16),
            jax.ShapeDtypeStruct(krope_t.shape, BF16),
            jax.ShapeDtypeStruct(absorb.shape, BF16),
            jax.ShapeDtypeStruct(value.shape, BF16),
        ),
        in_specs=[hbm_spec()] * 10,
        out_specs=(vmem_spec(),) * 9,
        scratch_shapes=[
            VMEM(nope.shape, BF16),
            VMEM(rope_t.shape, BF16),
            VMEM(routes.shape, jnp.int32),
            VMEM((1, requests), jnp.int32),
            VMEM((1, parent.shape[0]), jnp.int32),
            VMEM((8, 128), jnp.int32),
            DMA((10,)),
            DMA((4,)),
            DMA((4,)),
            DMA((4, 4)),
            DMA((4, 4)),
            DMA((8,)),
            DMA((8,)),
            DMA((4,)),
            DMA((4,)),
            DMA((4,)),
            DMA((4,)),
        ],
        compiler_params=pltpu.CompilerParams(
            collective_id=0, has_side_effects=True, vmem_limit_bytes=24 << 20
        ),
    )(
        *map(
            stay,
            (nope, rope_t, routes, leaf[None, :], parent[None, :], outw, lat, krope_t, absorb, value),
        )
    )


TILE = 32
KEYS = 256


def split3(v):
    hi = v.astype(BF16)
    rest = v - hi.astype(F32)
    mid = rest.astype(BF16)
    low = (rest - mid.astype(F32)).astype(BF16)
    return hi.astype(F32), mid.astype(F32), low.astype(F32)


def join3(part):
    return part[:, 0:8] + part[:, 8:16] + part[:, 16:24]


def attn_kernel(
    q_ref,
    pick_ref,
    place_ref,
    absorb_ref,
    value_ref,
    lat_ref,
    rope_ref,
    len_hbm,
    out_ref,
    len_ref,
    picked,
    done,
    wsem,
):
    (load,) = start_loads([(len_hbm, len_ref)], wsem)
    requests = q_ref.shape[0]
    slots, most = lat_ref.shape[0], lat_ref.shape[1]
    scaling = float(128 + 64) ** (-0.5)
    done[...] = jnp.zeros_like(done)
    lane = lax.broadcasted_iota(jnp.int32, (TILE, 128), 1)
    counts = []
    for slot in range(slots):
        picked[slot] = dot(pick_ref[slot], q_ref[...]).astype(BF16)
        counts.append(jnp.sum(pick_ref[slot].astype(F32)).astype(jnp.int32))
    load.wait()

    for slot in range(slots):
        length = len_ref[slot]

        def tile(keys, step, carry):
            here = pl.ds(pl.multiple_of(step * TILE, TILE), TILE)
            qt = picked[slot, here]
            nope = jnp.concatenate([qt[:, j * 128 : j * 128 + 128] for j in range(QT)], axis=0)
            rot = jnp.concatenate(
                [qt[:, 1024 + j * 64 : 1024 + j * 64 + 64] for j in range(QT)], axis=0
            )
            lat = dot(nope, absorb_ref[...]).astype(BF16)
            scores = dot_nt(lat, lat_ref[slot, :keys]) + dot(rot, rope_ref[slot, :, :keys])
            positions = lax.broadcasted_iota(jnp.int32, (1, keys), 1)
            scores = jnp.where(positions < length, scores * scaling, NEGATIVE)
            top = jnp.max(scores, axis=1, keepdims=True)
            weights = jnp.exp(scores - top).astype(BF16)
            total = jnp.sum(weights.astype(F32), axis=1, keepdims=True)
            summed = dot(weights, lat_ref[slot, :keys])
            attended = (summed / total).astype(BF16)
            valued = dot(attended, value_ref[...]).astype(BF16)
            parts = split3(top + jnp.log(total))
            tail = jnp.where(lane == 24, 1.0, 0.0)
            for j in range(QT):
                for k in range(3):
                    piece = parts[k][j * TILE : (j + 1) * TILE]
                    tail = jnp.where(lane == k * 8 + j, piece, tail)
            done[slot, here] = jnp.concatenate(
                [valued[j * TILE : (j + 1) * TILE] for j in range(QT)] + [tail.astype(BF16)],
                axis=1,
            )
            return carry

        tiles = (counts[slot] + TILE - 1) // TILE
        for keys in range(KEYS, most + 1, KEYS):

            @pl.when((length > keys - KEYS) & (length <= keys))
            def _():
                lax.fori_loop(0, tiles, lambda step, carry: tile(keys, step, carry), 0)

    acc = [dot(place_ref[s], done[s]) for s in range(slots)]
    logs = [
        jnp.where(a[:, 1048:1049] > 0.5, join3(a[:, 1024:]), NEGATIVE) for a in acc
    ]
    top = logs[0]
    for s in range(1, slots):
        top = jnp.maximum(top, logs[s])
    shares = [jnp.exp(v - top) for v in logs]
    total = shares[0]
    for s in range(1, slots):
        total = total + shares[s]
    log_sum = top + jnp.log(total)
    for j in range(QT):
        out = 0.0
        for s in range(slots):
            out = out + (shares[s] / total)[:, j : j + 1] * acc[s][:, j * 128 : j * 128 + 128]
        out_ref[:, j * 128 : j * 128 + 128] = out.astype(BF16)
    parts = split3(log_sum)
    lane = lax.broadcasted_iota(jnp.int32, (requests, 128), 1)
    tail = jnp.zeros((requests, 128), F32)
    for j in range(QT):
        for k in range(3):
            tail = jnp.where(lane == k * 8 + j, parts[k][:, j : j + 1], tail)
    out_ref[:, 1024:] = tail.astype(BF16)


def attend(node_length, q_all, pick, place, absorb, value, lat, rope_t):
    requests = q_all.shape[0]
    slots = lat.shape[0]
    return pl.pallas_call(
        attn_kernel,
        name="attend_nodes",
        out_shape=jax.ShapeDtypeStruct((requests, MSG), BF16),
        in_specs=[vmem_spec()] * 7 + [hbm_spec()],
        out_specs=vmem_spec(),
        scratch_shapes=[
            pltpu.SMEM(node_length.shape, jnp.int32),
            VMEM((slots, requests, q_all.shape[1]), BF16),
            VMEM((slots, requests, MSG), BF16),
            DMA((1,)),
        ],
        compiler_params=pltpu.CompilerParams(vmem_limit_bytes=32 << 20),
    )(q_all, pick, place, absorb, value, lat, rope_t, stay(node_length))


GAP = 384
SGAP = 256


def layer_kernel(
    msg_ref,
    q_ref,
    routes_ref,
    outw1,
    absorb_ref,
    value_ref,
    gain_hbm,
    newlat_hbm,
    newrope_hbm,
    resid_hbm,
    router_hbm,
    outw_hbm,
    gate_hbm,
    up_hbm,
    down_hbm,
    sgate_hbm,
    sup_hbm,
    sdown_hbm,
    out_ref,
    gain_ref,
    newlat_ref,
    newrope_ref,
    resid_ref,
    router_ref,
    outw2,
    gate_up,
    down_w,
    sgate_up,
    sdown_w,
    got,
    valued_s,
    vin,
    zsend,
    zrecv,
    hidden_s,
    normed,
    packed,
    arrived,
    own_out,
    cross_send,
    cross_recv,
    ret_send,
    ret_recv,
    share_in,
    share_send,
    share_recv,
    part,
    lsend,
    lrecv,
    wsem,
    ms,
    mr,
    cs,
    cr,
    ys,
    yr,
    vs,
    vr,
    ns,
    nr,
    ds,
    dr,
    fs,
    fr,
    os_,
    or_,
    rs,
    rr,
    xs,
    xr,
    bs,
    br,
    ls,
    lr,
):
    g, e, x, y, zl, zh, c = coords()
    mine = x * 4 + y
    half = outw2.shape[3]
    ff = gate_hbm.shape[0]
    sff = sgate_hbm.shape[0]
    barrier = pltpu.get_barrier_semaphore()

    def plane(p):
        return dev(p // 4, p % 4, zl, zh, c)

    def hello(i, carry):
        greet(barrier, (lax.rem(g + i, 16), e))
        return carry

    lax.fori_loop(1, 16, hello, 0)
    other = dev(x, y, zl, zh, 1 - c)
    partner = dev(x, y, zl, 1 - zh, c)
    greet(barrier, other)
    greet(barrier, partner)
    for i in range(4):
        for k in range(1, 4):
            greet(barrier, dev(lax.rem(x + i, 4), lax.rem(y + k, 4), zl, zh, c))
    lines = (zl, zl + 1 - 2 * (zl % 2), zl + 2 - 4 * (zl // 2), 3 - zl)
    halves = (zh, 1 - zh)

    def line(d):
        return dev(x, y, lines[d // 2], halves[d % 2], c)

    for d in (3, 5, 7):
        greet(barrier, line(d))
    for i in range(1, 4):
        greet(barrier, dev(x, lax.rem(y + i, 4), zl, zh, 1 - c))
    loads = start_loads(
        [
            (gain_hbm, gain_ref),
            (newlat_hbm, newlat_ref),
            (newrope_hbm, newrope_ref),
            (resid_hbm, resid_ref),
            (router_hbm, router_ref),
            (outw_hbm.at[:, pl.ds(half, half)], outw2.at[y, c]),
            (gate_hbm, gate_up.at[pl.ds(0, ff)]),
            (up_hbm, gate_up.at[pl.ds(GAP, ff)]),
            (down_hbm, down_w),
            (sgate_hbm, sgate_up.at[pl.ds(0, sff)]),
            (sup_hbm, sgate_up.at[pl.ds(SGAP, sff)]),
            (sdown_hbm, sdown_w),
        ],
        wsem,
    )
    gate_up[ff:GAP] = jnp.zeros((GAP - ff, gate_up.shape[1]), BF16)
    sgate_up[sff:SGAP] = jnp.zeros((SGAP - sff, sgate_up.shape[1]), BF16)

    pl.semaphore_wait(barrier, 35)

    def send(i, carry):
        peer = lax.rem(g + i, 16)
        remote(msg_ref.at[peer], got.at[g], ms.at[i], mr.at[i], (peer, e)).start()
        return carry

    lax.fori_loop(1, 16, send, 0)
    got[g] = msg_ref[g]

    loads[5].wait()
    own_w = outw2.at[y, c]
    for i in (1, 3, 2):
        remote(own_w, own_w, ys.at[i], yr.at[i], dev(x, lax.rem(y + i, 4), zl, zh, c)).start()
    remote(own_w, own_w, cs.at[0], cr.at[0], other).start()

    scaling = float(128 + 64) ** (-0.5)
    for load in loads[:5]:
        load.wait()
    q = q_ref[g]
    nope = jnp.concatenate([q[:, j * 128 : j * 128 + 128] for j in range(QT)], axis=0)
    rot = jnp.concatenate([q[:, 1024 + j * 64 : 1024 + j * 64 + 64] for j in range(QT)], axis=0)
    lat = dot(nope, absorb_ref[...]).astype(BF16)
    scores = dot_nt(lat, newlat_ref[...]) + dot(rot, newrope_ref[...])
    rows = REQ * QT
    qi = lax.broadcasted_iota(jnp.int32, (rows, rows), 0)
    ki = lax.broadcasted_iota(jnp.int32, (rows, rows), 1)
    usable = ((qi % REQ) == (ki // QT)) & ((ki % QT) <= (qi // REQ))
    scores = jnp.where(usable, scores * scaling, NEGATIVE)
    top = jnp.max(scores, axis=1, keepdims=True)
    weights = jnp.where(usable, jnp.exp(scores - top), 0.0).astype(BF16)
    total = jnp.sum(weights.astype(F32), axis=1, keepdims=True)
    summed = dot(weights, newlat_ref[...]) / total
    new_valued = dot(summed.astype(BF16), value_ref[...])
    new_log = top + jnp.log(total)

    experts = router_ref.shape[0]
    pairs = (zl // 2, 1 - zl // 2)
    picks, masks = [], []
    for q_ in range(2):
        routes = routes_ref[pl.ds(pairs[q_] * 4, 4)].reshape(32, 128)
        ids = lax.broadcasted_iota(jnp.int32, (32, experts), 1)
        chosen = jnp.zeros((32, experts), F32)
        for k in range(6):
            chosen = jnp.where(routes[:, k : k + 1] == ids, 1.0, chosen)
        ti = lax.broadcasted_iota(jnp.int32, (32, 32), 0)
        tj = lax.broadcasted_iota(jnp.int32, (32, 32), 1)
        before = flag((ti // 8 == tj // 8) & (tj < ti))
        rank = jnp.where(chosen > 0.0, dot(before, chosen.astype(BF16)), -1.0)
        col = lax.broadcasted_iota(jnp.int32, (experts, 128), 1)
        spread = flag(lax.broadcasted_iota(jnp.int32, (experts, 128), 0) == zl * 16 + col // 8)
        spread_rank = dot(rank.astype(BF16), spread)
        ct = lax.broadcasted_iota(jnp.int32, (32, 128), 1)
        rt = lax.broadcasted_iota(jnp.int32, (32, 128), 0)
        pick = jnp.where(
            (spread_rank == (ct % 2).astype(F32)) & (rt // 8 == (ct // 2) % 4), 1.0, 0.0
        )
        picks.append(pick)
        masks.append(chosen)

    for i in (1, 3, 2):
        block = outw2.at[lax.rem(y - i + 4, 4), c]
        remote(own_w, block, ys.at[i], yr.at[i], other).wait()
        remote(block, block, cs.at[i], cr.at[i], other).start()

    def wait(i, carry):
        src = lax.rem(g - i + 16, 16)
        remote(msg_ref.at[src], got.at[src], ms.at[i], mr.at[i], other).wait()
        return carry

    lax.fori_loop(1, 16, wait, 0)

    logs = join3(got[:, :, 1024:].astype(F32).reshape(16 * REQ, 128)).reshape(16, REQ, 8)
    pieces = []
    for j in range(QT):
        log_j = logs[:, :, j : j + 1]
        new_j = new_log[j * REQ : (j + 1) * REQ]
        peak = jnp.maximum(jnp.max(log_j, axis=0), new_j)
        share = jnp.exp(log_j - peak[None])
        new_share = jnp.exp(new_j - peak)
        whole = jnp.sum(share, axis=0) + new_share
        value = jnp.sum(share * got[:, :, j * 128 : j * 128 + 128].astype(F32), axis=0)
        value = value + new_share * new_valued[j * REQ : (j + 1) * REQ]
        pieces.append((value / whole).astype(BF16))
    valued = jnp.concatenate(pieces, axis=0)
    di = lax.broadcasted_iota(jnp.int32, (rows, rows), 0)
    si = lax.broadcasted_iota(jnp.int32, (rows, rows), 1)
    req = ((di % 64) // 16) * 4 + ((di % 16) // 8) * 2 + di // 64
    perm = flag(si == (di % 8) * REQ + req)
    valued_s[...] = dot(perm, valued).astype(BF16).reshape(2, 4, 16, 128)
    vin[y, c] = valued_s[c, y]
    for k in (5, 7, 6, 2, 1, 3, 4):
        to_y, to_c = lax.rem(y + k % 4, 4), lax.rem(c + k // 4, 2)
        remote(
            valued_s.at[to_c, to_y], vin.at[y, c], vs.at[k], vr.at[k], dev(x, to_y, zl, zh, to_c)
        ).start()
    for i in range(4):
        y_of = lax.rem(y - i + 4, 4)
        remote(outw2.at[y_of, c], outw2.at[y_of, 1 - c], cs.at[i], cr.at[i], other).wait()
    for k in (4, 1, 3, 5, 7, 2, 6):
        block = vin.at[lax.rem(y - k % 4 + 4, 4), lax.rem(c + k // 4, 2)]
        remote(valued_s.at[0, 0], block, vs.at[k], vr.at[k], other).wait()
    heads = jnp.concatenate([vin[k // 2, k % 2] for k in range(8)], axis=1)
    total_row = jnp.concatenate(
        [
            dot(heads, outw1[...].reshape(1024, half)),
            dot(heads, outw2[...].reshape(1024, half)),
        ],
        axis=1,
    )
    own_8 = lax.broadcasted_iota(jnp.int32, (16, 1), 0) // 8 == zh
    resid = resid_ref[...].astype(F32)
    total_row = total_row + jnp.where(own_8, jnp.concatenate([resid, resid], axis=0), 0.0)
    zsend[...] = total_row.astype(BF16)
    for d in (1, 3, 2, 5, 7, 4, 6):
        remote(zsend, zrecv.at[d], ns.at[d], nr.at[d], line(d)).start()

    def column(d):
        remote(zsend, zrecv.at[d], ns.at[d], nr.at[d], other).wait()
        return zrecv[d].astype(F32)

    gain = gain_ref[...].reshape(1, gain_ref.shape[0]).astype(F32)

    def norm(hidden):
        square = jnp.mean(hidden * hidden, axis=1, keepdims=True)
        return (hidden * lax.rsqrt(square + EPSILON) * gain).astype(BF16)

    hidden = total_row + column(1)
    hidden_s[...] = hidden.reshape(2, 8, 2048)
    normed[zl] = norm(hidden)
    share_in[x, zl] = normed[zl].reshape(2, 8, 2048)[0]

    @pl.when(zh == 1)
    def _():
        share_in[x, zl] = normed[zl].reshape(2, 8, 2048)[1]

    for i in (2, 1, 3):
        block = share_in.at[x, zl]
        peer = dev(lax.rem(x + i, 4), y, zl, zh, c)
        remote(block, block, xs.at[0, i], xr.at[0, i], peer).start()

    def pack(chunk):
        tokens = normed[pl.ds(pairs[chunk] * 2, 2)].reshape(32, 2048)
        packed[chunk] = (
            lax.dot_general(
                picks[chunk].astype(BF16),
                tokens,
                (((0,), (0,)), ((), ())),
                preferred_element_type=F32,
            )
            .astype(BF16)
            .reshape(16, 8, 2048)
        )

        def send(i, carry):
            p = lax.rem(mine + i, 16)
            remote(
                packed.at[chunk, p],
                arrived.at[chunk, c, mine],
                ds.at[chunk, i],
                dr.at[chunk, i],
                plane(p),
            ).start()
            return carry

        lax.fori_loop(1, 16, send, 0)
        arrived[chunk, c, mine] = packed[chunk, mine]
        here = arrived.at[chunk, c, mine]
        remote(here, here, fs.at[chunk, 0], fr.at[chunk, 0], other).start()
        logits = dot_nt(tokens, router_ref[...])
        sigma = jax.nn.sigmoid(logits) * masks[chunk]
        route_w = ROUTE_SCALE * sigma / jnp.sum(sigma, axis=1, keepdims=True)
        col = lax.broadcasted_iota(jnp.int32, (experts, 128), 1)
        spread = flag(lax.broadcasted_iota(jnp.int32, (experts, 128), 0) == zl * 16 + col // 8)
        w_hi, w_mid, w_low = split3(route_w)
        return (
            dot(w_hi.astype(BF16), spread)
            + dot(w_mid.astype(BF16), spread)
            + dot(w_low.astype(BF16), spread)
        ) * picks[chunk]

    normed[lines[1]] = norm(column(2) + column(3))
    combine0 = pack(0)
    normed[lines[2]] = norm(column(4) + column(5))
    normed[lines[3]] = norm(column(6) + column(7))
    combine1 = pack(1)
    combines = (combine0, combine1)
    for d in range(1, 4):
        both = normed[lines[d]].reshape(2, 8, 2048)
        share_in[x, lines[d]] = jnp.where(zh == 0, both[0], both[1])
    for i in (1, 3, 2):
        block = share_in.at[lax.rem(x - i + 4, 4), zl]
        remote(share_in.at[x, zl], block, xs.at[0, i], xr.at[0, i], other).wait()
        for d in range(1, 4):
            remote(block, block, xs.at[d, i], xr.at[d, i], line(2 * d)).start()

    def forward(chunk):
        def step(i, carry):
            src = lax.rem(mine - i + 16, 16)
            block = arrived.at[chunk, c, src]
            remote(packed.at[chunk, src], block, ds.at[chunk, i], dr.at[chunk, i], other).wait()
            remote(block, block, fs.at[chunk, i], fr.at[chunk, i], other).start()
            return carry

        lax.fori_loop(1, 16, step, 0)

    def crossed(chunk):
        def step(i, carry):
            src = lax.rem(mine - i + 16, 16)
            block = arrived.at[chunk, c, src]
            remote(
                block, arrived.at[chunk, 1 - c, src], fs.at[chunk, i], fr.at[chunk, i], other
            ).wait()
            return carry

        lax.fori_loop(0, 16, step, 0)

    def ffn(rows_in, both_w, gap, units, down):
        val = dot_nt(rows_in, both_w[...])
        hidden = (jax.nn.silu(val[:, :units]) * val[:, gap : gap + units]).astype(BF16)
        return dot(hidden, down[...])

    def routed_ffn(chunk):
        out = ffn(arrived[chunk].reshape(256, 2048), gate_up, GAP, ff, down_w)
        first, second = out[:128], out[128:]
        own_out[chunk] = jnp.where(c == 0, first, second)
        cross_send[chunk] = jnp.where(c == 0, second, first).astype(BF16)
        remote(
            cross_send.at[chunk], cross_recv.at[chunk], os_.at[chunk], or_.at[chunk], other
        ).start()

    def give(chunk):
        remote(
            cross_send.at[chunk], cross_recv.at[chunk], os_.at[chunk], or_.at[chunk], other
        ).wait()
        ret_send[chunk] = (
            (own_out[chunk] + cross_recv[chunk].astype(F32)).astype(BF16).reshape(16, 8, 2048)
        )

        def step(i, carry):
            p = lax.rem(mine + i, 16)
            remote(
                ret_send.at[chunk, p],
                ret_recv.at[chunk, mine],
                rs.at[chunk, i],
                rr.at[chunk, i],
                plane(p),
            ).start()
            return carry

        lax.fori_loop(1, 16, step, 0)
        ret_recv[chunk, mine] = ret_send[chunk, mine]

    forward(0)
    for load in loads[6:9]:
        load.wait()
    crossed(0)
    routed_ffn(0)
    forward(1)
    give(0)
    crossed(1)
    routed_ffn(1)

    for load in loads[9:]:
        load.wait()
    for i in (1, 3, 2):
        src = lax.rem(x - i + 4, 4)
        for d in range(1, 4):
            remote(
                share_in.at[src, zl], share_in.at[src, lines[d]], xs.at[d, i], xr.at[d, i], other
            ).wait()
    shared = ffn(share_in[...].reshape(128, 2048), sgate_up, SGAP, sff, sdown_w)
    share_send[...] = shared.astype(BF16).reshape(4, 32, 2048)
    for i in (2, 1, 3):
        peer = lax.rem(x + i, 4)
        remote(
            share_send.at[peer], share_recv.at[i], bs.at[i], br.at[i], dev(peer, y, zl, zh, c)
        ).start()
    give(1)
    for i in range(1, 4):
        remote(share_send.at[0], share_recv.at[i], bs.at[i], br.at[i], other).wait()
    share_sum = share_send[x].astype(F32)
    for i in range(1, 4):
        share_sum = share_sum + share_recv[i].astype(F32)
    for z in range(4):
        mine_z = share_sum[z * 8 : z * 8 + 8]
        part[z, 0] = jnp.where(zh == 0, mine_z, 0.0)
        part[z, 1] = jnp.where(zh == 1, mine_z, 0.0)

    def take(chunk):
        def step(i, carry):
            src = lax.rem(mine - i + 16, 16)
            remote(
                ret_send.at[chunk, src],
                ret_recv.at[chunk, src],
                rs.at[chunk, i],
                rr.at[chunk, i],
                other,
            ).wait()
            return carry

        lax.fori_loop(1, 16, step, 0)
        back = ret_recv[chunk].reshape(128, 2048)
        w_hi = combines[chunk].astype(BF16)
        w_low = (combines[chunk] - w_hi.astype(F32)).astype(BF16)
        routed = (dot(w_hi, back) + dot(w_low, back)).reshape(2, 2, 8, 2048)
        first = pl.ds(pairs[chunk] * 2, 2)
        part[first] = part[first] + routed
        lsend[first] = part[first].astype(BF16)

    def hand(d):
        block = lsend.at[lines[d // 2], halves[d % 2]]
        return remote(block, lrecv.at[d], ls.at[d], lr.at[d], line(d))

    take(0)
    for d in (1, 3, 2):
        hand(d).start()
    take(1)
    for d in (5, 7, 4, 6):
        hand(d).start()
    result = hidden_s[zh] + part[zl, zh]
    for d in (2, 1, 3, 4, 6, 5, 7):
        hand(d).wait()
        result = result + lrecv[d].astype(F32)
    out_ref[...] = result.astype(BF16)


def layer(vmem_args, more, weights):
    gate, up, down, sgate, sup, sdown = weights
    width = gate.shape[1]
    return pl.pallas_call(
        layer_kernel,
        name="layer",
        out_shape=jax.ShapeDtypeStruct((8, width), BF16),
        in_specs=[vmem_spec()] * len(vmem_args) + [hbm_spec()] * (len(more) + 6),
        out_specs=vmem_spec(),
        scratch_shapes=[VMEM(m.shape, BF16) for m in more[:-1]]
        + [
            VMEM((4, 2, 128, width // 2), BF16),
            VMEM((GAP + gate.shape[0], width), BF16),
            VMEM(down.shape, BF16),
            VMEM((SGAP + sgate.shape[0], width), BF16),
            VMEM(sdown.shape, BF16),
            VMEM((16, REQ, MSG), BF16),
            VMEM((2, 4, 16, 128), BF16),
            VMEM((4, 2, 16, 128), BF16),
            VMEM((16, width), BF16),
            VMEM((8, 16, width), BF16),
            VMEM((2, 8, width), F32),
            VMEM((4, 16, width), BF16),
            VMEM((2, 16, 8, width), BF16),
            VMEM((2, 2, 16, 8, width), BF16),
            VMEM((2, 128, width), F32),
            VMEM((2, 128, width), BF16),
            VMEM((2, 128, width), BF16),
            VMEM((2, 16, 8, width), BF16),
            VMEM((2, 16, 8, width), BF16),
            VMEM((4, 4, 8, width), BF16),
            VMEM((4, 32, width), BF16),
            VMEM((4, 32, width), BF16),
            VMEM((4, 2, 8, width), F32),
            VMEM((4, 2, 8, width), BF16),
            VMEM((8, 8, width), BF16),
            DMA((12,)),
            DMA((16,)),
            DMA((16,)),
            DMA((4,)),
            DMA((4,)),
            DMA((4,)),
            DMA((4,)),
            DMA((8,)),
            DMA((8,)),
            DMA((8,)),
            DMA((8,)),
            DMA((2, 16)),
            DMA((2, 16)),
            DMA((2, 16)),
            DMA((2, 16)),
            DMA((2,)),
            DMA((2,)),
            DMA((2, 16)),
            DMA((2, 16)),
            DMA((4, 4)),
            DMA((4, 4)),
            DMA((4,)),
            DMA((4,)),
            DMA((8,)),
            DMA((8,)),
        ],
        compiler_params=pltpu.CompilerParams(
            collective_id=1, has_side_effects=True, vmem_limit_bytes=44 << 20
        ),
    )(*vmem_args, *map(stay, more), *map(stay, weights))


def on_device(
    query_nope,
    query_rope,
    absorb_weight,
    value_weight,
    output_weight,
    cache_latent,
    cache_rope,
    node_length,
    new_latent,
    new_rope,
    parent_node,
    leaf_node,
    residual,
    norm_gain,
    router_weight,
    routes,
    expert_gate,
    expert_up,
    expert_down,
    shared_gate,
    shared_up,
    shared_down,
):
    q_all, routes8, pick, place, outw, lat, krope, absorb, value = gather(
        query_nope[:, 0, :],
        query_rope[:, 0, :].T,
        routes,
        leaf_node,
        parent_node,
        output_weight,
        cache_latent,
        jnp.swapaxes(cache_rope, 1, 2),
        absorb_weight[0],
        value_weight[0],
    )
    msg = attend(
        node_length, q_all.reshape(16 * REQ, -1), pick, place, absorb, value, lat, krope
    )
    return layer(
        (msg.reshape(16, REQ, MSG), q_all, routes8, outw, absorb, value),
        (norm_gain, new_latent, new_rope.T, residual, router_weight.T, output_weight),
        (
            expert_gate[0].T,
            expert_up[0].T,
            expert_down[0],
            shared_gate.T,
            shared_up.T,
            shared_down,
        ),
    )


def solution(mesh):
    in_specs = (
        P("group", "expert", None),
        P("group", "expert", None),
        P("expert", None, None),
        P("expert", None, None),
        P("expert", None),
        P("group", None, None),
        P("group", None, None),
        P("group"),
        P("group", None),
        P("group", None),
        P(),
        P(),
        P(("group", "expert"), None),
        P(),
        P(),
        P(("group", "expert"), None),
        P(("group", "expert"), None, None),
        P(("group", "expert"), None, None),
        P(("group", "expert"), None, None),
        P(None, "group"),
        P(None, "group"),
        P("group", None),
    )
    out_specs = P(("group", "expert"), None)
    return jax.shard_map(
        on_device, mesh=mesh, in_specs=in_specs, out_specs=out_specs, check_vma=False
    )
```

```python
import jax
import jax.numpy as jnp
from jax import lax
from jax.experimental import pallas as pl
from jax.experimental.pallas import tpu as pltpu
from jax.sharding import PartitionSpec as P

ROUTE_SCALE = 2.446
NEGATIVE = -1e30
EPSILON = 1e-06
MESH = pl.DeviceIdType.MESH
F32 = jnp.float32
BF16 = jnp.bfloat16
VMEM = pltpu.VMEM
DMA = pltpu.SemaphoreType.DMA

REQ = 16
QT = 8
MSG = 1024 + 128


def vmem_spec():
    return pl.BlockSpec(memory_space=pltpu.VMEM)


def hbm_spec():
    return pl.BlockSpec(memory_space=pltpu.HBM)


def stay(x):
    return pltpu.with_memory_space_constraint(x, pltpu.HBM)


def start_loads(pairs, sem):
    loads = [pltpu.make_async_copy(src, dst, sem.at[i]) for i, (src, dst) in enumerate(pairs)]
    for load in loads:
        load.start()
    return loads


def coords():
    g = lax.axis_index("group")
    e = lax.axis_index("expert")
    zl, x = g // 4, g % 4
    y, zh, c = e // 4, (e % 4) // 2, e % 2
    return g, e, x, y, zl, zh, c


def dev(x, y, zl, zh, c):
    return (zl * 4 + x, y * 4 + zh * 2 + c)


def remote(src, dst, send, recv, device):
    return pltpu.make_async_remote_copy(
        src_ref=src,
        dst_ref=dst,
        send_sem=send,
        recv_sem=recv,
        device_id=device,
        device_id_type=MESH,
    )


def greet(barrier, device):
    pl.semaphore_signal(barrier, inc=1, device_id=device, device_id_type=MESH)


def dot(a, b):
    return jnp.dot(a, b, preferred_element_type=F32)


def eye_column(row):
    n = row.shape[1]
    same = lax.broadcasted_iota(jnp.int32, (n, n), 0) == lax.broadcasted_iota(jnp.int32, (n, n), 1)
    return jnp.sum(jnp.where(same, row, 0), axis=1, keepdims=True)


def flag(condition):
    return jnp.where(condition, 1.0, 0.0).astype(BF16)


def dot_nt(a, b):
    return lax.dot_general(a, b, (((1,), (1,)), ((), ())), preferred_element_type=F32)


def on_path(leaf_row, parent_col, node):
    nodes = parent_col.shape[0]
    ids = lax.broadcasted_iota(jnp.int32, (nodes, leaf_row.shape[1]), 0)
    mid = jnp.sum(jnp.where(leaf_row == ids, parent_col, 0), axis=0, keepdims=True)
    top = jnp.sum(jnp.where(mid == ids, parent_col, 0), axis=0, keepdims=True)
    return (leaf_row == node) | (mid == node) | (top == node)


def gather_kernel(
    nope_hbm,
    rope_hbm,
    routes_hbm,
    leaf_hbm,
    parent_hbm,
    lat_hbm,
    krope_hbm,
    absorb_hbm,
    value_hbm,
    qall,
    routes8,
    pick_ref,
    place_ref,
    lat_ref,
    krope_ref,
    absorb_ref,
    value_ref,
    nope_v,
    rope_v,
    routes_v,
    leaf_v,
    parent_v,
    mine,
    wsem,
    zq,
    zqr,
    xq,
    xqr,
    rs,
    rr,
):
    g, e, x, y, zl, zh, c = coords()
    loads = start_loads(
        [
            (nope_hbm, nope_v),
            (rope_hbm, rope_v),
            (routes_hbm, routes_v),
            (leaf_hbm, leaf_v),
            (parent_hbm, parent_v),
            (lat_hbm, lat_ref),
            (krope_hbm, krope_ref),
            (absorb_hbm, absorb_ref),
            (value_hbm, value_ref),
        ],
        wsem,
    )
    barrier = pltpu.get_barrier_semaphore()
    partner = dev(x, y, zl, 1 - zh, c)
    me = zl * 2 + zh
    for i in range(1, 4):
        greet(barrier, dev(lax.rem(x + i, 4), y, zl, zh, c))
        greet(barrier, dev(x, y, lax.rem(zl + i, 4), zh, c))
    for k in (1, 3, 5, 7):
        s = lax.rem(me + k, 8)
        greet(barrier, dev(x, y, s // 2, s % 2, c))

    rows = REQ * QT
    di = lax.broadcasted_iota(jnp.int32, (rows, rows), 0)
    si = lax.broadcasted_iota(jnp.int32, (rows, rows), 1)
    perm = flag(si == (di % REQ) * QT + di // REQ)
    for load in loads[:3]:
        load.wait()
    nope = dot(perm, nope_v[...]).astype(BF16)
    rope = dot_nt(perm, rope_v[...]).astype(BF16)
    qall[g] = jnp.concatenate(
        [nope[j * REQ : (j + 1) * REQ] for j in range(QT)]
        + [rope[j * REQ : (j + 1) * REQ] for j in range(QT)],
        axis=1,
    )
    mine[...] = jnp.zeros_like(mine)
    mine[:, 0 : routes_v.shape[1]] = routes_v[...]
    routes8[me] = mine[...]
    pl.semaphore_wait(barrier, 10)

    own = qall.at[g]
    for i in (1, 3, 2):
        remote(own, own, zq.at[i], zqr.at[i], dev(x, y, lax.rem(zl + i, 4), zh, c)).start()
    for k in (1, 3, 2):
        remote(own, own, xq.at[0, k], xqr.at[0, k], dev(lax.rem(x + k, 4), y, zl, zh, c)).start()
    for k in range(1, 8):
        s = lax.rem(me + k, 8)
        remote(mine, routes8.at[me], rs.at[k], rr.at[k], dev(x, y, s // 2, s % 2, c)).start()

    def pass_on(i):
        block = qall.at[lax.rem(zl - i + 4, 4) * 4 + x]
        remote(own, block, zq.at[i], zqr.at[i], partner).wait()
        for k in (1, 3, 2):
            remote(
                block, block, xq.at[i, k], xqr.at[i, k], dev(lax.rem(x + k, 4), y, zl, zh, c)
            ).start()

    pass_on(1)
    pass_on(3)
    pass_on(2)

    for load in loads[3:5]:
        load.wait()
    slots, _, requests = pick_ref.shape
    ids_0 = lax.broadcasted_iota(jnp.int32, (requests, requests), 0)
    ids_1 = lax.broadcasted_iota(jnp.int32, (requests, requests), 1)
    earlier = flag(ids_0 < ids_1)
    parent_col = eye_column(parent_v[...])
    for slot in range(slots):
        on_row = on_path(leaf_v[...], parent_col, g * slots + slot)
        row_f = jnp.where(on_row, 1.0, 0.0)
        rank_row = dot(jnp.broadcast_to(row_f, (8, requests)).astype(BF16), earlier)[0:1]
        rank_row = jnp.where(on_row, rank_row, -1.0)
        pick_ref[slot] = flag(rank_row.astype(jnp.int32) == ids_0)
        place_ref[slot] = flag(eye_column(rank_row).astype(jnp.int32) == ids_1)

    for load in loads[5:]:
        load.wait()
    for k in range(1, 8):
        s = lax.rem(me - k + 8, 8)
        remote(mine, routes8.at[s], rs.at[k], rr.at[k], partner).wait()
    for i in range(4):
        for k in (1, 3, 2):
            block = qall.at[lax.rem(zl - i + 4, 4) * 4 + lax.rem(x - k + 4, 4)]
            remote(own, block, xq.at[i, k], xqr.at[i, k], partner).wait()


def gather(nope, rope_t, routes, leaf, parent, lat, krope_t, absorb, value):
    requests = leaf.shape[0]
    slots = lat.shape[0]
    return pl.pallas_call(
        gather_kernel,
        name="gather_queries",
        out_shape=(
            jax.ShapeDtypeStruct((16, REQ, QT * 192), BF16),
            jax.ShapeDtypeStruct((8, 8, 128), jnp.int32),
            jax.ShapeDtypeStruct((slots, requests, requests), BF16),
            jax.ShapeDtypeStruct((slots, requests, requests), BF16),
            jax.ShapeDtypeStruct(lat.shape, BF16),
            jax.ShapeDtypeStruct(krope_t.shape, BF16),
            jax.ShapeDtypeStruct(absorb.shape, BF16),
            jax.ShapeDtypeStruct(value.shape, BF16),
        ),
        in_specs=[hbm_spec()] * 9,
        out_specs=(vmem_spec(),) * 8,
        scratch_shapes=[
            VMEM(nope.shape, BF16),
            VMEM(rope_t.shape, BF16),
            VMEM(routes.shape, jnp.int32),
            VMEM((1, requests), jnp.int32),
            VMEM((1, parent.shape[0]), jnp.int32),
            VMEM((8, 128), jnp.int32),
            DMA((9,)),
            DMA((4,)),
            DMA((4,)),
            DMA((4, 4)),
            DMA((4, 4)),
            DMA((8,)),
            DMA((8,)),
        ],
        compiler_params=pltpu.CompilerParams(
            collective_id=0, has_side_effects=True, vmem_limit_bytes=24 << 20
        ),
    )(
        *map(
            stay,
            (nope, rope_t, routes, leaf[None, :], parent[None, :], lat, krope_t, absorb, value),
        )
    )


TILE = 32
KEYS = 256


def split3(v):
    hi = v.astype(BF16)
    rest = v - hi.astype(F32)
    mid = rest.astype(BF16)
    low = (rest - mid.astype(F32)).astype(BF16)
    return hi.astype(F32), mid.astype(F32), low.astype(F32)


def pack_logs(logs):
    hi, mid, low = split3(logs)
    return hi + pltpu.roll(mid, 8, 1) + pltpu.roll(low, 16, 1)


def join_logs(tail):
    return tail + pltpu.roll(tail, 120, 1) + pltpu.roll(tail, 112, 1)


def attn_kernel(
    q_ref,
    pick_ref,
    place_ref,
    absorb_ref,
    value_ref,
    lat_ref,
    rope_ref,
    len_hbm,
    out_ref,
    len_ref,
    picked,
    done,
    wsem,
):
    (load,) = start_loads([(len_hbm, len_ref)], wsem)
    requests = q_ref.shape[0]
    slots, most = lat_ref.shape[0], lat_ref.shape[1]
    scaling = float(128 + 64) ** (-0.5)
    done[...] = jnp.zeros_like(done)
    lane = lax.broadcasted_iota(jnp.int32, (TILE, 128), 1)
    counts = []
    for slot in range(slots):
        picked[slot] = dot(pick_ref[slot], q_ref[...]).astype(BF16)
        counts.append(jnp.sum(pick_ref[slot].astype(F32)).astype(jnp.int32))
    load.wait()

    for slot in range(slots):
        length = len_ref[slot]

        def tile(keys, step, carry):
            here = pl.ds(pl.multiple_of(step * TILE, TILE), TILE)
            qt = picked[slot, here]
            nope = jnp.concatenate([qt[:, j * 128 : j * 128 + 128] for j in range(QT)], axis=0)
            rot = jnp.concatenate(
                [qt[:, 1024 + j * 64 : 1024 + j * 64 + 64] for j in range(QT)], axis=0
            )
            lat = dot(nope, absorb_ref[...]).astype(BF16)
            scores = dot_nt(lat, lat_ref[slot, :keys]) + dot(rot, rope_ref[slot, :, :keys])
            positions = lax.broadcasted_iota(jnp.int32, (1, keys), 1)
            scores = jnp.where(positions < length, scores * scaling, NEGATIVE)
            top = jnp.max(scores, axis=1, keepdims=True)
            weights = jnp.exp(scores - top).astype(BF16)
            total = jnp.sum(weights.astype(F32), axis=1, keepdims=True)
            summed = dot(weights, lat_ref[slot, :keys])
            attended = (summed / total).astype(BF16)
            valued = dot(attended, value_ref[...]).astype(BF16)
            log_sum = top + jnp.log(total)
            logs = jnp.zeros((TILE, 128), F32)
            for j in range(QT):
                logs = jnp.where(lane == j, log_sum[j * TILE : (j + 1) * TILE], logs)
            tail = jnp.where((lane >= 24) & (lane < 32), 1.0, pack_logs(logs))
            done[slot, here] = jnp.concatenate(
                [valued[j * TILE : (j + 1) * TILE] for j in range(QT)] + [tail.astype(BF16)],
                axis=1,
            )
            return carry

        tiles = (counts[slot] + TILE - 1) // TILE
        for keys in range(KEYS, most + 1, KEYS):

            @pl.when((length > keys - KEYS) & (length <= keys))
            def _():
                lax.fori_loop(0, tiles, lambda step, carry: tile(keys, step, carry), 0)

    acc = [dot(place_ref[s], done[s]) for s in range(slots)]
    tails = [a[:, 1024:] for a in acc]
    logs = [jnp.where(pltpu.roll(t, 104, 1) > 0.5, join_logs(t), NEGATIVE) for t in tails]
    top = logs[0]
    for s in range(1, slots):
        top = jnp.maximum(top, logs[s])
    shares = [jnp.exp(v - top) for v in logs]
    total = shares[0]
    for s in range(1, slots):
        total = total + shares[s]
    shares = [v / total for v in shares]
    for j in range(QT):
        out = 0.0
        for s in range(slots):
            out = out + shares[s][:, j : j + 1] * acc[s][:, j * 128 : j * 128 + 128]
        out_ref[:, j * 128 : j * 128 + 128] = out.astype(BF16)
    lanes = lax.broadcasted_iota(jnp.int32, (requests, 128), 1)
    log_sum = jnp.where(lanes < QT, top + jnp.log(total), 0.0)
    out_ref[:, 1024:] = pack_logs(log_sum).astype(BF16)


def attend(node_length, q_all, pick, place, absorb, value, lat, rope_t):
    requests = q_all.shape[0]
    slots = lat.shape[0]
    return pl.pallas_call(
        attn_kernel,
        name="attend_nodes",
        out_shape=jax.ShapeDtypeStruct((requests, MSG), BF16),
        in_specs=[vmem_spec()] * 7 + [hbm_spec()],
        out_specs=vmem_spec(),
        scratch_shapes=[
            pltpu.SMEM(node_length.shape, jnp.int32),
            VMEM((slots, requests, q_all.shape[1]), BF16),
            VMEM((slots, requests, MSG), BF16),
            DMA((1,)),
        ],
        compiler_params=pltpu.CompilerParams(vmem_limit_bytes=32 << 20),
    )(q_all, pick, place, absorb, value, lat, rope_t, stay(node_length))


GAP = 384
SGAP = 256


def layer_kernel(
    msg_ref,
    q_ref,
    routes_ref,
    absorb_ref,
    value_ref,
    gain_hbm,
    newlat_hbm,
    newrope_hbm,
    resid_hbm,
    router_hbm,
    outw_hbm,
    gate_hbm,
    up_hbm,
    down_hbm,
    sgate_hbm,
    sup_hbm,
    sdown_hbm,
    out_ref,
    gain_ref,
    newlat_ref,
    newrope_ref,
    resid_ref,
    router_ref,
    outw_ref,
    gate_up,
    down_w,
    sgate_up,
    sdown_w,
    got,
    got_z,
    blended,
    valued_s,
    csend,
    crecv,
    acc,
    ysend,
    yrecv,
    zsend,
    zrecv,
    hidden_s,
    normed,
    packed,
    arrived,
    own_out,
    cross_send,
    cross_recv,
    ret_send,
    ret_recv,
    share_in,
    share_out,
    share_send,
    share_recv,
    share_sum,
    share_x,
    share_back,
    part,
    lsend,
    lrecv,
    wsem,
    ms,
    mr,
    gs,
    gr,
    cs,
    cr,
    ys,
    yr,
    ns,
    nr,
    ds,
    dr,
    fs,
    fr,
    os_,
    or_,
    rs,
    rr,
    xs,
    xr,
    bs,
    br,
    us,
    ur,
    ls,
    lr,
):
    g, e, x, y, zl, zh, c = coords()
    mine = x * 4 + y
    ff = gate_hbm.shape[0]
    sff = sgate_hbm.shape[0]
    barrier = pltpu.get_barrier_semaphore()

    def plane(p):
        return dev(p // 4, p % 4, zl, zh, c)

    other = dev(x, y, zl, zh, 1 - c)
    partner = dev(x, y, zl, 1 - zh, c)
    greet(barrier, other)
    greet(barrier, partner)
    for i in range(4):
        for k in range(1, 4):
            greet(barrier, dev(lax.rem(x + i, 4), lax.rem(y + k, 4), zl, zh, c))
    lines = (zl, zl + 1 - 2 * (zl % 2), zl + 2 - 4 * (zl // 2), 3 - zl)
    halves = (zh, 1 - zh)

    def line(d):
        return dev(x, y, lines[d // 2], halves[d % 2], c)

    for d in range(2, 8):
        greet(barrier, line(d))
    for i in range(1, 4):
        greet(barrier, dev(lax.rem(x + i, 4), y, zl, zh, c))
    loads = start_loads(
        [
            (gain_hbm, gain_ref),
            (newlat_hbm, newlat_ref),
            (newrope_hbm, newrope_ref),
            (resid_hbm, resid_ref),
            (router_hbm, router_ref),
            (outw_hbm, outw_ref),
            (gate_hbm, gate_up.at[pl.ds(0, ff)]),
            (up_hbm, gate_up.at[pl.ds(GAP, ff)]),
            (down_hbm, down_w),
            (sgate_hbm, sgate_up.at[pl.ds(0, sff)]),
            (sup_hbm, sgate_up.at[pl.ds(SGAP, sff)]),
            (sdown_hbm, sdown_w),
        ],
        wsem,
    )
    gate_up[ff:GAP] = jnp.zeros((GAP - ff, gate_up.shape[1]), BF16)
    sgate_up[sff:SGAP] = jnp.zeros((SGAP - sff, sgate_up.shape[1]), BF16)

    pl.semaphore_wait(barrier, 23)

    homes = (lines[2], lines[3], lines[1], zl)
    for n in range(4):
        for i in (2, 1, 3):
            peer = lax.rem(x + i, 4)
            remote(
                msg_ref.at[homes[n] * 4 + peer],
                got.at[n, i],
                ms.at[n, i],
                mr.at[n, i],
                dev(peer, y, zl, zh, c),
            ).start()

    scaling = float(128 + 64) ** (-0.5)
    for load in loads[:6]:
        load.wait()
    q = q_ref[g]
    nope = jnp.concatenate([q[:, j * 128 : j * 128 + 128] for j in range(QT)], axis=0)
    rot = jnp.concatenate([q[:, 1024 + j * 64 : 1024 + j * 64 + 64] for j in range(QT)], axis=0)
    lat = dot(nope, absorb_ref[...]).astype(BF16)
    scores = dot_nt(lat, newlat_ref[...]) + dot(rot, newrope_ref[...])
    rows = REQ * QT
    qi = lax.broadcasted_iota(jnp.int32, (rows, rows), 0)
    ki = lax.broadcasted_iota(jnp.int32, (rows, rows), 1)
    usable = ((qi % REQ) == (ki // QT)) & ((ki % QT) <= (qi // REQ))
    scores = jnp.where(usable, scores * scaling, NEGATIVE)
    top = jnp.max(scores, axis=1, keepdims=True)
    weights = jnp.where(usable, jnp.exp(scores - top), 0.0).astype(BF16)
    total = jnp.sum(weights.astype(F32), axis=1, keepdims=True)
    summed = dot(weights, newlat_ref[...]) / total
    new_valued = dot(summed.astype(BF16), value_ref[...])
    new_log = top + jnp.log(total)

    def blend(parts, more=None):
        logs = [join_logs(p[:, 1024:].astype(F32)) for p in parts]
        if more is not None:
            logs.append(more[1])
        peak = logs[0]
        for v in logs[1:]:
            peak = jnp.maximum(peak, v)
        shares = [jnp.exp(v - peak) for v in logs]
        whole = shares[0]
        for v in shares[1:]:
            whole = whole + v
        shares = [v / whole for v in shares]
        values = []
        for j in range(QT):
            value = 0.0
            for p, share in zip(parts, shares):
                value = value + share[:, j : j + 1] * p[:, j * 128 : j * 128 + 128].astype(F32)
            if more is not None:
                value = value + shares[-1][:, j : j + 1] * more[0][j * REQ : (j + 1) * REQ]
            values.append(value.astype(BF16))
        return values, peak + jnp.log(whole)

    def along_x(n):
        for i in (1, 3, 2):
            src = msg_ref.at[homes[n] * 4 + lax.rem(x + i, 4)]
            remote(src, got.at[n, i], ms.at[n, i], mr.at[n, i], other).wait()
        return [msg_ref[homes[n] * 4 + x]] + [got[n, i] for i in range(1, 4)]

    lane = lax.broadcasted_iota(jnp.int32, (REQ, 128), 1)

    def along_z(n):
        return remote(
            blended.at[n], got_z.at[n], gs.at[n], gr.at[n], dev(x, y, homes[n], zh, c)
        )

    for n in range(3):
        values, log_sum = blend(along_x(n))
        tail = pack_logs(jnp.where(lane < QT, log_sum, 0.0)).astype(BF16)
        blended[n] = jnp.concatenate(values + [tail], axis=1)
        along_z(n).start()

    experts = router_ref.shape[0]
    pairs = (zl // 2, 1 - zl // 2)
    picks, masks = [], []
    for q_ in range(2):
        routes = routes_ref[pl.ds(pairs[q_] * 4, 4)].reshape(32, 128)
        ids = lax.broadcasted_iota(jnp.int32, (32, experts), 1)
        chosen = jnp.zeros((32, experts), F32)
        for k in range(6):
            chosen = jnp.where(routes[:, k : k + 1] == ids, 1.0, chosen)
        ti = lax.broadcasted_iota(jnp.int32, (32, 32), 0)
        tj = lax.broadcasted_iota(jnp.int32, (32, 32), 1)
        before = flag((ti // 8 == tj // 8) & (tj < ti))
        rank = jnp.where(chosen > 0.0, dot(before, chosen.astype(BF16)), -1.0)
        col = lax.broadcasted_iota(jnp.int32, (experts, 128), 1)
        spread = flag(lax.broadcasted_iota(jnp.int32, (experts, 128), 0) == zl * 16 + col // 8)
        spread_rank = dot(rank.astype(BF16), spread)
        ct = lax.broadcasted_iota(jnp.int32, (32, 128), 1)
        rt = lax.broadcasted_iota(jnp.int32, (32, 128), 0)
        pick = jnp.where(
            (spread_rank == (ct % 2).astype(F32)) & (rt // 8 == (ct // 2) % 4), 1.0, 0.0
        )
        picks.append(pick)
        masks.append(chosen)

    here = along_x(3)
    logs = jnp.zeros((REQ, 128), F32)
    for j in range(QT):
        logs = jnp.where(lane == j, new_log[j * REQ : (j + 1) * REQ], logs)
    for n in (2, 0, 1):
        along_z(n).wait()
    pieces, _ = blend(here + [got_z[n] for n in range(3)], (new_valued, logs))
    valued = jnp.concatenate(pieces, axis=0)
    di = lax.broadcasted_iota(jnp.int32, (rows, rows), 0)
    si = lax.broadcasted_iota(jnp.int32, (rows, rows), 1)
    req = ((di % 64) // 16) * 4 + ((di % 16) // 8) * 2 + di // 64
    perm = flag(si == (di % 8) * REQ + req)
    valued_s[...] = dot(perm, valued).astype(BF16).reshape(2, 64, 128)
    csend[...] = dot(valued_s[1 - c], outw_ref[...]).astype(BF16)
    remote(csend, crecv, cs, cr, other).start()
    own = dot(valued_s[c], outw_ref[...])
    remote(csend, crecv, cs, cr, other).wait()
    acc[...] = (own + crecv[...].astype(F32)).reshape(4, 16, 2048)
    ysend[...] = acc[...].astype(BF16)
    for i in (2, 1, 3):
        peer = lax.rem(y + i, 4)
        remote(ysend.at[peer], yrecv.at[i], ys.at[i], yr.at[i], dev(x, peer, zl, zh, c)).start()
    total_row = acc[y]
    for i in (1, 3, 2):
        remote(ysend.at[0], yrecv.at[i], ys.at[i], yr.at[i], other).wait()
        total_row = total_row + yrecv[i].astype(F32)
    own_8 = lax.broadcasted_iota(jnp.int32, (16, 1), 0) // 8 == zh
    resid = resid_ref[...].astype(F32)
    total_row = total_row + jnp.where(own_8, jnp.concatenate([resid, resid], axis=0), 0.0)
    zsend[...] = total_row.astype(BF16)
    for d in (1, 3, 2, 5, 7, 4, 6):
        remote(zsend, zrecv.at[d], ns.at[d], nr.at[d], line(d)).start()

    def column(d):
        remote(zsend, zrecv.at[d], ns.at[d], nr.at[d], other).wait()
        return zrecv[d].astype(F32)

    gain = gain_ref[...].reshape(1, gain_ref.shape[0]).astype(F32)

    def norm(hidden):
        square = jnp.mean(hidden * hidden, axis=1, keepdims=True)
        return (hidden * lax.rsqrt(square + EPSILON) * gain).astype(BF16)

    hidden = total_row + column(1)
    hidden_s[...] = hidden.reshape(2, 8, 2048)
    normed[zl] = norm(hidden)
    share_in[x, zl] = normed[zl].reshape(2, 8, 2048)[0]

    @pl.when(zh == 1)
    def _():
        share_in[x, zl] = normed[zl].reshape(2, 8, 2048)[1]

    for i in (2, 1, 3):
        block = share_in.at[x, zl]
        peer = dev(lax.rem(x + i, 4), y, zl, zh, c)
        remote(block, block, xs.at[0, i], xr.at[0, i], peer).start()

    def pack(chunk):
        tokens = normed[pl.ds(pairs[chunk] * 2, 2)].reshape(32, 2048)
        packed[chunk] = (
            lax.dot_general(
                picks[chunk].astype(BF16),
                tokens,
                (((0,), (0,)), ((), ())),
                preferred_element_type=F32,
            )
            .astype(BF16)
            .reshape(16, 8, 2048)
        )

        def send(i, carry):
            p = lax.rem(mine + i, 16)
            remote(
                packed.at[chunk, p],
                arrived.at[chunk, c, mine],
                ds.at[chunk, i],
                dr.at[chunk, i],
                plane(p),
            ).start()
            return carry

        lax.fori_loop(1, 16, send, 0)
        arrived[chunk, c, mine] = packed[chunk, mine]
        here = arrived.at[chunk, c, mine]
        remote(here, here, fs.at[chunk, 0], fr.at[chunk, 0], other).start()
        logits = dot_nt(tokens, router_ref[...])
        sigma = jax.nn.sigmoid(logits) * masks[chunk]
        route_w = ROUTE_SCALE * sigma / jnp.sum(sigma, axis=1, keepdims=True)
        col = lax.broadcasted_iota(jnp.int32, (experts, 128), 1)
        spread = flag(lax.broadcasted_iota(jnp.int32, (experts, 128), 0) == zl * 16 + col // 8)
        w_hi, w_mid, w_low = split3(route_w)
        return (
            dot(w_hi.astype(BF16), spread)
            + dot(w_mid.astype(BF16), spread)
            + dot(w_low.astype(BF16), spread)
        ) * picks[chunk]

    normed[lines[1]] = norm(column(2) + column(3))
    combine0 = pack(0)
    normed[lines[2]] = norm(column(4) + column(5))
    normed[lines[3]] = norm(column(6) + column(7))
    combine1 = pack(1)
    combines = (combine0, combine1)
    for d in range(1, 4):
        both = normed[lines[d]].reshape(2, 8, 2048)
        share_in[x, lines[d]] = jnp.where(zh == 0, both[0], both[1])
    for i in (1, 3, 2):
        block = share_in.at[lax.rem(x - i + 4, 4), zl]
        remote(share_in.at[x, zl], block, xs.at[0, i], xr.at[0, i], other).wait()
        for d in range(1, 4):
            remote(block, block, xs.at[d, i], xr.at[d, i], line(2 * d)).start()

    def forward(chunk):
        def step(i, carry):
            src = lax.rem(mine - i + 16, 16)
            block = arrived.at[chunk, c, src]
            remote(packed.at[chunk, src], block, ds.at[chunk, i], dr.at[chunk, i], other).wait()
            remote(block, block, fs.at[chunk, i], fr.at[chunk, i], other).start()
            return carry

        lax.fori_loop(1, 16, step, 0)

    def crossed(chunk):
        def step(i, carry):
            src = lax.rem(mine - i + 16, 16)
            block = arrived.at[chunk, c, src]
            remote(
                block, arrived.at[chunk, 1 - c, src], fs.at[chunk, i], fr.at[chunk, i], other
            ).wait()
            return carry

        lax.fori_loop(0, 16, step, 0)

    def ffn(rows_in, both_w, gap, units, down):
        val = dot_nt(rows_in, both_w[...])
        hidden = (jax.nn.silu(val[:, :units]) * val[:, gap : gap + units]).astype(BF16)
        return dot(hidden, down[...])

    def routed_ffn(chunk):
        out = ffn(arrived[chunk].reshape(256, 2048), gate_up, GAP, ff, down_w)
        first, second = out[:128], out[128:]
        own_out[chunk] = jnp.where(c == 0, first, second)
        cross_send[chunk] = jnp.where(c == 0, second, first).astype(BF16)
        remote(
            cross_send.at[chunk], cross_recv.at[chunk], os_.at[chunk], or_.at[chunk], other
        ).start()

    def give(chunk):
        remote(
            cross_send.at[chunk], cross_recv.at[chunk], os_.at[chunk], or_.at[chunk], other
        ).wait()
        ret_send[chunk] = (
            (own_out[chunk] + cross_recv[chunk].astype(F32)).astype(BF16).reshape(16, 8, 2048)
        )

        def step(i, carry):
            p = lax.rem(mine + i, 16)
            remote(
                ret_send.at[chunk, p],
                ret_recv.at[chunk, mine],
                rs.at[chunk, i],
                rr.at[chunk, i],
                plane(p),
            ).start()
            return carry

        lax.fori_loop(1, 16, step, 0)
        ret_recv[chunk, mine] = ret_send[chunk, mine]

    forward(0)
    for load in loads[6:9]:
        load.wait()
    crossed(0)
    routed_ffn(0)
    forward(1)
    give(0)
    crossed(1)
    routed_ffn(1)

    for load in loads[9:]:
        load.wait()
    for i in (1, 3, 2):
        src = lax.rem(x - i + 4, 4)
        for d in range(1, 4):
            remote(
                share_in.at[src, zl], share_in.at[src, lines[d]], xs.at[d, i], xr.at[d, i], other
            ).wait()
    shared = ffn(share_in[...].reshape(128, 2048), sgate_up, SGAP, sff, sdown_w)
    share_out[...] = shared.reshape(4, 4, 8, 2048)
    for z in range(4):
        share_send[z] = share_out[:, z].astype(BF16)
    for d in (2, 3, 1):
        remote(
            share_send.at[lines[d]], share_recv.at[d], bs.at[d], br.at[d], line(2 * d)
        ).start()
    give(1)
    def take(chunk):
        def step(i, carry):
            src = lax.rem(mine - i + 16, 16)
            remote(
                ret_send.at[chunk, src],
                ret_recv.at[chunk, src],
                rs.at[chunk, i],
                rr.at[chunk, i],
                other,
            ).wait()
            return carry

        lax.fori_loop(1, 16, step, 0)
        back = ret_recv[chunk].reshape(128, 2048)
        w_hi = combines[chunk].astype(BF16)
        w_low = (combines[chunk] - w_hi.astype(F32)).astype(BF16)
        routed = (dot(w_hi, back) + dot(w_low, back)).reshape(2, 2, 8, 2048)
        first = pl.ds(pairs[chunk] * 2, 2)
        part[first] = routed
        lsend[first] = routed.astype(BF16)

    def hand(d):
        block = lsend.at[lines[d // 2], halves[d % 2]]
        return remote(block, lrecv.at[d], ls.at[d], lr.at[d], line(d))

    take(0)
    for d in (1, 3, 2):
        hand(d).start()
    for d in (1, 2, 3):
        remote(share_send.at[lines[d]], share_recv.at[d], bs.at[d], br.at[d], other).wait()
    for n in range(4):
        both = share_out[n, zl]
        for d in range(1, 4):
            both = both + share_recv[d, n].astype(F32)
        share_sum[n] = both
        share_x[n] = both.astype(BF16)
    for i in (2, 1, 3):
        peer = lax.rem(x + i, 4)
        remote(
            share_x.at[peer], share_back.at[i], us.at[i], ur.at[i], dev(peer, y, zl, zh, c)
        ).start()
    take(1)
    for d in (5, 7, 4, 6):
        hand(d).start()
    result = hidden_s[zh] + part[zl, zh] + share_sum[x]
    for i in (1, 3, 2):
        remote(share_x.at[lax.rem(x + i, 4)], share_back.at[i], us.at[i], ur.at[i], other).wait()
        result = result + share_back[i].astype(F32)
    for d in (2, 1, 3, 4, 6, 5, 7):
        hand(d).wait()
        result = result + lrecv[d].astype(F32)
    out_ref[...] = result.astype(BF16)


def layer(vmem_args, more, weights):
    gate, up, down, sgate, sup, sdown = weights
    width = gate.shape[1]
    return pl.pallas_call(
        layer_kernel,
        name="layer",
        out_shape=jax.ShapeDtypeStruct((8, width), BF16),
        in_specs=[vmem_spec()] * len(vmem_args) + [hbm_spec()] * (len(more) + 6),
        out_specs=vmem_spec(),
        scratch_shapes=[VMEM(m.shape, BF16) for m in more]
        + [
            VMEM((GAP + gate.shape[0], width), BF16),
            VMEM(down.shape, BF16),
            VMEM((SGAP + sgate.shape[0], width), BF16),
            VMEM(sdown.shape, BF16),
            VMEM((4, 4, REQ, MSG), BF16),
            VMEM((3, REQ, MSG), BF16),
            VMEM((3, REQ, MSG), BF16),
            VMEM((2, 64, 128), BF16),
            VMEM((64, width), BF16),
            VMEM((64, width), BF16),
            VMEM((4, 16, width), F32),
            VMEM((4, 16, width), BF16),
            VMEM((4, 16, width), BF16),
            VMEM((16, width), BF16),
            VMEM((8, 16, width), BF16),
            VMEM((2, 8, width), F32),
            VMEM((4, 16, width), BF16),
            VMEM((2, 16, 8, width), BF16),
            VMEM((2, 2, 16, 8, width), BF16),
            VMEM((2, 128, width), F32),
            VMEM((2, 128, width), BF16),
            VMEM((2, 128, width), BF16),
            VMEM((2, 16, 8, width), BF16),
            VMEM((2, 16, 8, width), BF16),
            VMEM((4, 4, 8, width), BF16),
            VMEM((4, 4, 8, width), F32),
            VMEM((4, 4, 8, width), BF16),
            VMEM((4, 4, 8, width), BF16),
            VMEM((4, 8, width), F32),
            VMEM((4, 8, width), BF16),
            VMEM((4, 8, width), BF16),
            VMEM((4, 2, 8, width), F32),
            VMEM((4, 2, 8, width), BF16),
            VMEM((8, 8, width), BF16),
            DMA((12,)),
            DMA((4, 4)),
            DMA((4, 4)),
            DMA((3,)),
            DMA((3,)),
            DMA,
            DMA,
            DMA((4,)),
            DMA((4,)),
            DMA((8,)),
            DMA((8,)),
            DMA((2, 16)),
            DMA((2, 16)),
            DMA((2, 16)),
            DMA((2, 16)),
            DMA((2,)),
            DMA((2,)),
            DMA((2, 16)),
            DMA((2, 16)),
            DMA((4, 4)),
            DMA((4, 4)),
            DMA((4,)),
            DMA((4,)),
            DMA((4,)),
            DMA((4,)),
            DMA((8,)),
            DMA((8,)),
        ],
        compiler_params=pltpu.CompilerParams(
            collective_id=1, has_side_effects=True, vmem_limit_bytes=44 << 20
        ),
    )(*vmem_args, *map(stay, more), *map(stay, weights))


def on_device(
    query_nope,
    query_rope,
    absorb_weight,
    value_weight,
    output_weight,
    cache_latent,
    cache_rope,
    node_length,
    new_latent,
    new_rope,
    parent_node,
    leaf_node,
    residual,
    norm_gain,
    router_weight,
    routes,
    expert_gate,
    expert_up,
    expert_down,
    shared_gate,
    shared_up,
    shared_down,
):
    q_all, routes8, pick, place, lat, krope, absorb, value = gather(
        query_nope[:, 0, :],
        query_rope[:, 0, :].T,
        routes,
        leaf_node,
        parent_node,
        cache_latent,
        jnp.swapaxes(cache_rope, 1, 2),
        absorb_weight[0],
        value_weight[0],
    )
    msg = attend(
        node_length, q_all.reshape(16 * REQ, -1), pick, place, absorb, value, lat, krope
    )
    return layer(
        (msg.reshape(16, REQ, MSG), q_all, routes8, absorb, value),
        (norm_gain, new_latent, new_rope.T, residual, router_weight.T, output_weight),
        (
            expert_gate[0].T,
            expert_up[0].T,
            expert_down[0],
            shared_gate.T,
            shared_up.T,
            shared_down,
        ),
    )


def solution(mesh):
    in_specs = (
        P("group", "expert", None),
        P("group", "expert", None),
        P("expert", None, None),
        P("expert", None, None),
        P("expert", None),
        P("group", None, None),
        P("group", None, None),
        P("group"),
        P("group", None),
        P("group", None),
        P(),
        P(),
        P(("group", "expert"), None),
        P(),
        P(),
        P(("group", "expert"), None),
        P(("group", "expert"), None, None),
        P(("group", "expert"), None, None),
        P(("group", "expert"), None, None),
        P(None, "group"),
        P(None, "group"),
        P("group", None),
    )
    out_specs = P(("group", "expert"), None)
    return jax.shard_map(
        on_device, mesh=mesh, in_specs=in_specs, out_specs=out_specs, check_vma=False
    )
```

```python
import jax
import jax.numpy as jnp
from jax import lax
from jax.experimental import pallas as pl
from jax.experimental.pallas import tpu as pltpu
from jax.sharding import PartitionSpec as P

ROUTE_SCALE = 2.446
NEGATIVE = -1e30
EPSILON = 1e-06
MESH = pl.DeviceIdType.MESH
F32 = jnp.float32
BF16 = jnp.bfloat16
VMEM = pltpu.VMEM
DMA = pltpu.SemaphoreType.DMA

REQ = 16
QT = 8
MSG = 1024 + 128


def vmem_spec():
    return pl.BlockSpec(memory_space=pltpu.VMEM)


def hbm_spec():
    return pl.BlockSpec(memory_space=pltpu.HBM)


def stay(x):
    return pltpu.with_memory_space_constraint(x, pltpu.HBM)


def start_loads(pairs, sem):
    loads = [pltpu.make_async_copy(src, dst, sem.at[i]) for i, (src, dst) in enumerate(pairs)]
    for load in loads:
        load.start()
    return loads


def coords():
    g = lax.axis_index("group")
    e = lax.axis_index("expert")
    zl, x = g // 4, g % 4
    y, zh, c = e // 4, (e % 4) // 2, e % 2
    return g, e, x, y, zl, zh, c


def dev(x, y, zl, zh, c):
    return (zl * 4 + x, y * 4 + zh * 2 + c)


def remote(src, dst, send, recv, device):
    return pltpu.make_async_remote_copy(
        src_ref=src,
        dst_ref=dst,
        send_sem=send,
        recv_sem=recv,
        device_id=device,
        device_id_type=MESH,
    )


def greet(barrier, device):
    pl.semaphore_signal(barrier, inc=1, device_id=device, device_id_type=MESH)


def dot(a, b):
    return jnp.dot(a, b, preferred_element_type=F32)


def eye_column(row):
    n = row.shape[1]
    same = lax.broadcasted_iota(jnp.int32, (n, n), 0) == lax.broadcasted_iota(jnp.int32, (n, n), 1)
    return jnp.sum(jnp.where(same, row, 0), axis=1, keepdims=True)


def flag(condition):
    return jnp.where(condition, 1.0, 0.0).astype(BF16)


def dot_nt(a, b):
    return lax.dot_general(a, b, (((1,), (1,)), ((), ())), preferred_element_type=F32)


def on_path(leaf_row, parent_col, node):
    nodes = parent_col.shape[0]
    ids = lax.broadcasted_iota(jnp.int32, (nodes, leaf_row.shape[1]), 0)
    mid = jnp.sum(jnp.where(leaf_row == ids, parent_col, 0), axis=0, keepdims=True)
    top = jnp.sum(jnp.where(mid == ids, parent_col, 0), axis=0, keepdims=True)
    return (leaf_row == node) | (mid == node) | (top == node)


def gather_kernel(
    nope_hbm,
    rope_hbm,
    routes_hbm,
    leaf_hbm,
    parent_hbm,
    lat_hbm,
    krope_hbm,
    absorb_hbm,
    value_hbm,
    qall,
    routes8,
    pick_ref,
    place_ref,
    lat_ref,
    krope_ref,
    absorb_ref,
    value_ref,
    nope_v,
    rope_v,
    routes_v,
    leaf_v,
    parent_v,
    mine,
    wsem,
    zq,
    zqr,
    xq,
    xqr,
    rs,
    rr,
):
    g, e, x, y, zl, zh, c = coords()
    loads = start_loads(
        [
            (nope_hbm, nope_v),
            (rope_hbm, rope_v),
            (routes_hbm, routes_v),
            (leaf_hbm, leaf_v),
            (parent_hbm, parent_v),
            (lat_hbm, lat_ref),
            (krope_hbm, krope_ref),
            (absorb_hbm, absorb_ref),
            (value_hbm, value_ref),
        ],
        wsem,
    )
    barrier = pltpu.get_barrier_semaphore()
    partner = dev(x, y, zl, 1 - zh, c)
    me = zl * 2 + zh
    for i in range(1, 4):
        greet(barrier, dev(lax.rem(x + i, 4), y, zl, zh, c))
        greet(barrier, dev(x, y, lax.rem(zl + i, 4), zh, c))
    for k in (1, 3, 5, 7):
        s = lax.rem(me + k, 8)
        greet(barrier, dev(x, y, s // 2, s % 2, c))

    rows = REQ * QT
    di = lax.broadcasted_iota(jnp.int32, (rows, rows), 0)
    si = lax.broadcasted_iota(jnp.int32, (rows, rows), 1)
    perm = flag(si == (di % REQ) * QT + di // REQ)
    for load in loads[:3]:
        load.wait()
    nope = dot(perm, nope_v[...]).astype(BF16)
    rope = dot_nt(perm, rope_v[...]).astype(BF16)
    qall[g] = jnp.concatenate(
        [nope[j * REQ : (j + 1) * REQ] for j in range(QT)]
        + [rope[j * REQ : (j + 1) * REQ] for j in range(QT)],
        axis=1,
    )
    mine[...] = jnp.zeros_like(mine)
    mine[:, 0 : routes_v.shape[1]] = routes_v[...]
    routes8[me] = mine[...]
    pl.semaphore_wait(barrier, 10)

    own = qall.at[g]
    for i in (1, 3, 2):
        remote(own, own, zq.at[i], zqr.at[i], dev(x, y, lax.rem(zl + i, 4), zh, c)).start()
    for k in (1, 3, 2):
        remote(own, own, xq.at[0, k], xqr.at[0, k], dev(lax.rem(x + k, 4), y, zl, zh, c)).start()
    for k in range(1, 8):
        s = lax.rem(me + k, 8)
        remote(mine, routes8.at[me], rs.at[k], rr.at[k], dev(x, y, s // 2, s % 2, c)).start()

    def pass_on(i):
        block = qall.at[lax.rem(zl - i + 4, 4) * 4 + x]
        remote(own, block, zq.at[i], zqr.at[i], partner).wait()
        for k in (1, 3, 2):
            remote(
                block, block, xq.at[i, k], xqr.at[i, k], dev(lax.rem(x + k, 4), y, zl, zh, c)
            ).start()

    pass_on(1)
    pass_on(3)
    pass_on(2)

    for load in loads[3:5]:
        load.wait()
    slots, _, requests = pick_ref.shape
    ids_0 = lax.broadcasted_iota(jnp.int32, (requests, requests), 0)
    ids_1 = lax.broadcasted_iota(jnp.int32, (requests, requests), 1)
    earlier = flag(ids_0 < ids_1)
    parent_col = eye_column(parent_v[...])
    for slot in range(slots):
        on_row = on_path(leaf_v[...], parent_col, g * slots + slot)
        row_f = jnp.where(on_row, 1.0, 0.0)
        rank_row = dot(jnp.broadcast_to(row_f, (8, requests)).astype(BF16), earlier)[0:1]
        rank_row = jnp.where(on_row, rank_row, -1.0)
        pick_ref[slot] = flag(rank_row.astype(jnp.int32) == ids_0)
        place_ref[slot] = flag(eye_column(rank_row).astype(jnp.int32) == ids_1)

    for load in loads[5:]:
        load.wait()
    for k in range(1, 8):
        s = lax.rem(me - k + 8, 8)
        remote(mine, routes8.at[s], rs.at[k], rr.at[k], partner).wait()
    for i in range(4):
        for k in (1, 3, 2):
            block = qall.at[lax.rem(zl - i + 4, 4) * 4 + lax.rem(x - k + 4, 4)]
            remote(own, block, xq.at[i, k], xqr.at[i, k], partner).wait()


def gather(nope, rope_t, routes, leaf, parent, lat, krope_t, absorb, value):
    requests = leaf.shape[0]
    slots = lat.shape[0]
    return pl.pallas_call(
        gather_kernel,
        name="gather_queries",
        out_shape=(
            jax.ShapeDtypeStruct((16, REQ, QT * 192), BF16),
            jax.ShapeDtypeStruct((8, 8, 128), jnp.int32),
            jax.ShapeDtypeStruct((slots, requests, requests), BF16),
            jax.ShapeDtypeStruct((slots, requests, requests), BF16),
            jax.ShapeDtypeStruct(lat.shape, BF16),
            jax.ShapeDtypeStruct(krope_t.shape, BF16),
            jax.ShapeDtypeStruct(absorb.shape, BF16),
            jax.ShapeDtypeStruct(value.shape, BF16),
        ),
        in_specs=[hbm_spec()] * 9,
        out_specs=(vmem_spec(),) * 8,
        scratch_shapes=[
            VMEM(nope.shape, BF16),
            VMEM(rope_t.shape, BF16),
            VMEM(routes.shape, jnp.int32),
            VMEM((1, requests), jnp.int32),
            VMEM((1, parent.shape[0]), jnp.int32),
            VMEM((8, 128), jnp.int32),
            DMA((9,)),
            DMA((4,)),
            DMA((4,)),
            DMA((4, 4)),
            DMA((4, 4)),
            DMA((8,)),
            DMA((8,)),
        ],
        compiler_params=pltpu.CompilerParams(
            collective_id=0, has_side_effects=True, vmem_limit_bytes=24 << 20
        ),
    )(
        *map(
            stay,
            (nope, rope_t, routes, leaf[None, :], parent[None, :], lat, krope_t, absorb, value),
        )
    )


TILE = 32
KEYS = 256


def split3(v):
    hi = v.astype(BF16)
    rest = v - hi.astype(F32)
    mid = rest.astype(BF16)
    low = (rest - mid.astype(F32)).astype(BF16)
    return hi.astype(F32), mid.astype(F32), low.astype(F32)


def pack_logs(logs):
    hi, mid, low = split3(logs)
    return hi + pltpu.roll(mid, 8, 1) + pltpu.roll(low, 16, 1)


def join_logs(tail):
    return tail + pltpu.roll(tail, 120, 1) + pltpu.roll(tail, 112, 1)


def attn_kernel(
    q_ref,
    pick_ref,
    place_ref,
    absorb_ref,
    value_ref,
    lat_ref,
    rope_ref,
    len_hbm,
    out_ref,
    len_ref,
    picked,
    done,
    wsem,
):
    (load,) = start_loads([(len_hbm, len_ref)], wsem)
    requests = q_ref.shape[0]
    slots, most = lat_ref.shape[0], lat_ref.shape[1]
    scaling = float(128 + 64) ** (-0.5)
    done[...] = jnp.zeros_like(done)
    lane = lax.broadcasted_iota(jnp.int32, (TILE, 128), 1)
    counts = []
    for slot in range(slots):
        picked[slot] = dot(pick_ref[slot], q_ref[...]).astype(BF16)
        counts.append(jnp.sum(pick_ref[slot].astype(F32)).astype(jnp.int32))
    load.wait()

    for slot in range(slots):
        length = len_ref[slot]

        def tile(keys, step, carry):
            here = pl.ds(pl.multiple_of(step * TILE, TILE), TILE)
            qt = picked[slot, here]
            nope = jnp.concatenate([qt[:, j * 128 : j * 128 + 128] for j in range(QT)], axis=0)
            rot = jnp.concatenate(
                [qt[:, 1024 + j * 64 : 1024 + j * 64 + 64] for j in range(QT)], axis=0
            )
            lat = dot(nope, absorb_ref[...]).astype(BF16)
            scores = dot_nt(lat, lat_ref[slot, :keys]) + dot(rot, rope_ref[slot, :, :keys])
            positions = lax.broadcasted_iota(jnp.int32, (1, keys), 1)
            scores = jnp.where(positions < length, scores * scaling, NEGATIVE)
            top = jnp.max(scores, axis=1, keepdims=True)
            weights = jnp.exp(scores - top).astype(BF16)
            total = jnp.sum(weights.astype(F32), axis=1, keepdims=True)
            summed = dot(weights, lat_ref[slot, :keys])
            attended = (summed / total).astype(BF16)
            valued = dot(attended, value_ref[...]).astype(BF16)
            log_sum = top + jnp.log(total)
            logs = jnp.zeros((TILE, 128), F32)
            for j in range(QT):
                logs = jnp.where(lane == j, log_sum[j * TILE : (j + 1) * TILE], logs)
            tail = jnp.where((lane >= 24) & (lane < 32), 1.0, pack_logs(logs))
            done[slot, here] = jnp.concatenate(
                [valued[j * TILE : (j + 1) * TILE] for j in range(QT)] + [tail.astype(BF16)],
                axis=1,
            )
            return carry

        tiles = (counts[slot] + TILE - 1) // TILE
        for keys in range(KEYS, most + 1, KEYS):

            @pl.when((length > keys - KEYS) & (length <= keys))
            def _():
                lax.fori_loop(0, tiles, lambda step, carry: tile(keys, step, carry), 0)

    acc = [dot(place_ref[s], done[s]) for s in range(slots)]
    tails = [a[:, 1024:] for a in acc]
    logs = [jnp.where(pltpu.roll(t, 104, 1) > 0.5, join_logs(t), NEGATIVE) for t in tails]
    top = logs[0]
    for s in range(1, slots):
        top = jnp.maximum(top, logs[s])
    shares = [jnp.exp(v - top) for v in logs]
    total = shares[0]
    for s in range(1, slots):
        total = total + shares[s]
    shares = [v / total for v in shares]
    for j in range(QT):
        out = 0.0
        for s in range(slots):
            out = out + shares[s][:, j : j + 1] * acc[s][:, j * 128 : j * 128 + 128]
        out_ref[:, j * 128 : j * 128 + 128] = out.astype(BF16)
    lanes = lax.broadcasted_iota(jnp.int32, (requests, 128), 1)
    log_sum = jnp.where(lanes < QT, top + jnp.log(total), 0.0)
    out_ref[:, 1024:] = pack_logs(log_sum).astype(BF16)


def attend(node_length, q_all, pick, place, absorb, value, lat, rope_t):
    requests = q_all.shape[0]
    slots = lat.shape[0]
    return pl.pallas_call(
        attn_kernel,
        name="attend_nodes",
        out_shape=jax.ShapeDtypeStruct((requests, MSG), BF16),
        in_specs=[vmem_spec()] * 7 + [hbm_spec()],
        out_specs=vmem_spec(),
        scratch_shapes=[
            pltpu.SMEM(node_length.shape, jnp.int32),
            VMEM((slots, requests, q_all.shape[1]), BF16),
            VMEM((slots, requests, MSG), BF16),
            DMA((1,)),
        ],
        compiler_params=pltpu.CompilerParams(vmem_limit_bytes=32 << 20),
    )(q_all, pick, place, absorb, value, lat, rope_t, stay(node_length))


OFFSETS = sorted(
    [(i, j) for i in range(4) for j in range(4) if i or j],
    key=lambda o: -min(o[0], 4 - o[0]) - min(o[1], 4 - o[1]),
)

GAP = 384
SGAP = 256


def layer_kernel(
    msg_ref,
    q_ref,
    routes_ref,
    absorb_ref,
    value_ref,
    gain_hbm,
    newlat_hbm,
    newrope_hbm,
    resid_hbm,
    router_hbm,
    outw_hbm,
    gate_hbm,
    up_hbm,
    down_hbm,
    sgate_hbm,
    sup_hbm,
    sdown_hbm,
    out_ref,
    gain_ref,
    newlat_ref,
    newrope_ref,
    resid_ref,
    router_ref,
    outw_ref,
    gate_up,
    down_w,
    sgate_up,
    sdown_w,
    got,
    got_z,
    blended,
    valued_s,
    csend,
    crecv,
    acc,
    ysend,
    yrecv,
    zsend,
    zrecv,
    hidden_s,
    normed,
    packed,
    arrived,
    own_out,
    cross_send,
    cross_recv,
    ret_send,
    ret_recv,
    share_in,
    share_out,
    share_send,
    share_recv,
    share_sum,
    share_x,
    share_back,
    part,
    lsend,
    lrecv,
    wsem,
    ms,
    mr,
    gs,
    gr,
    cs,
    cr,
    ys,
    yr,
    ns,
    nr,
    ds,
    dr,
    fs,
    fr,
    os_,
    or_,
    rs,
    rr,
    xs,
    xr,
    bs,
    br,
    us,
    ur,
    ls,
    lr,
):
    g, e, x, y, zl, zh, c = coords()
    mine = x * 4 + y
    ff = gate_hbm.shape[0]
    sff = sgate_hbm.shape[0]
    barrier = pltpu.get_barrier_semaphore()

    def source(i):
        return lax.rem(x - i // 4 + 4, 4) * 4 + lax.rem(y - i % 4 + 4, 4)

    other = dev(x, y, zl, zh, 1 - c)
    partner = dev(x, y, zl, 1 - zh, c)
    greet(barrier, other)
    greet(barrier, partner)
    for i in range(4):
        for k in range(1, 4):
            greet(barrier, dev(lax.rem(x + i, 4), lax.rem(y + k, 4), zl, zh, c))
    lines = (zl, zl + 1 - 2 * (zl % 2), zl + 2 - 4 * (zl // 2), 3 - zl)
    halves = (zh, 1 - zh)

    def line(d):
        return dev(x, y, lines[d // 2], halves[d % 2], c)

    for d in range(2, 8):
        greet(barrier, line(d))
    for i in range(1, 4):
        greet(barrier, dev(lax.rem(x + i, 4), y, zl, zh, c))
    loads = start_loads(
        [
            (gain_hbm, gain_ref),
            (newlat_hbm, newlat_ref),
            (newrope_hbm, newrope_ref),
            (resid_hbm, resid_ref),
            (router_hbm, router_ref),
            (outw_hbm, outw_ref),
            (gate_hbm, gate_up.at[pl.ds(0, ff)]),
            (up_hbm, gate_up.at[pl.ds(GAP, ff)]),
            (down_hbm, down_w),
            (sgate_hbm, sgate_up.at[pl.ds(0, sff)]),
            (sup_hbm, sgate_up.at[pl.ds(SGAP, sff)]),
            (sdown_hbm, sdown_w),
        ],
        wsem,
    )
    gate_up[ff:GAP] = jnp.zeros((GAP - ff, gate_up.shape[1]), BF16)
    sgate_up[sff:SGAP] = jnp.zeros((SGAP - sff, sgate_up.shape[1]), BF16)

    pl.semaphore_wait(barrier, 23)

    homes = (lines[2], lines[3], lines[1], zl)
    for n in range(4):
        for i in (2, 1, 3):
            peer = lax.rem(x + i, 4)
            remote(
                msg_ref.at[homes[n] * 4 + peer],
                got.at[n, i],
                ms.at[n, i],
                mr.at[n, i],
                dev(peer, y, zl, zh, c),
            ).start()

    scaling = float(128 + 64) ** (-0.5)
    for load in loads[:6]:
        load.wait()
    q = q_ref[g]
    nope = jnp.concatenate([q[:, j * 128 : j * 128 + 128] for j in range(QT)], axis=0)
    rot = jnp.concatenate([q[:, 1024 + j * 64 : 1024 + j * 64 + 64] for j in range(QT)], axis=0)
    lat = dot(nope, absorb_ref[...]).astype(BF16)
    scores = dot_nt(lat, newlat_ref[...]) + dot(rot, newrope_ref[...])
    rows = REQ * QT
    qi = lax.broadcasted_iota(jnp.int32, (rows, rows), 0)
    ki = lax.broadcasted_iota(jnp.int32, (rows, rows), 1)
    usable = ((qi % REQ) == (ki // QT)) & ((ki % QT) <= (qi // REQ))
    scores = jnp.where(usable, scores * scaling, NEGATIVE)
    top = jnp.max(scores, axis=1, keepdims=True)
    weights = jnp.where(usable, jnp.exp(scores - top), 0.0).astype(BF16)
    total = jnp.sum(weights.astype(F32), axis=1, keepdims=True)
    summed = dot(weights, newlat_ref[...]) / total
    new_valued = dot(summed.astype(BF16), value_ref[...])
    new_log = top + jnp.log(total)

    def blend(parts, more=None):
        logs = [join_logs(p[:, 1024:].astype(F32)) for p in parts]
        if more is not None:
            logs.append(more[1])
        peak = logs[0]
        for v in logs[1:]:
            peak = jnp.maximum(peak, v)
        shares = [jnp.exp(v - peak) for v in logs]
        whole = shares[0]
        for v in shares[1:]:
            whole = whole + v
        shares = [v / whole for v in shares]
        values = []
        for j in range(QT):
            value = 0.0
            for p, share in zip(parts, shares):
                value = value + share[:, j : j + 1] * p[:, j * 128 : j * 128 + 128].astype(F32)
            if more is not None:
                value = value + shares[-1][:, j : j + 1] * more[0][j * REQ : (j + 1) * REQ]
            values.append(value.astype(BF16))
        return values, peak + jnp.log(whole)

    def along_x(n):
        for i in (1, 3, 2):
            src = msg_ref.at[homes[n] * 4 + lax.rem(x + i, 4)]
            remote(src, got.at[n, i], ms.at[n, i], mr.at[n, i], other).wait()
        return [msg_ref[homes[n] * 4 + x]] + [got[n, i] for i in range(1, 4)]

    lane = lax.broadcasted_iota(jnp.int32, (REQ, 128), 1)

    def along_z(n):
        return remote(
            blended.at[n], got_z.at[n], gs.at[n], gr.at[n], dev(x, y, homes[n], zh, c)
        )

    for n in range(3):
        values, log_sum = blend(along_x(n))
        tail = pack_logs(jnp.where(lane < QT, log_sum, 0.0)).astype(BF16)
        blended[n] = jnp.concatenate(values + [tail], axis=1)
        along_z(n).start()

    experts = router_ref.shape[0]
    pairs = (zl // 2, 1 - zl // 2)
    picks, masks = [], []
    for q_ in range(2):
        routes = routes_ref[pl.ds(pairs[q_] * 4, 4)].reshape(32, 128)
        ids = lax.broadcasted_iota(jnp.int32, (32, experts), 1)
        chosen = jnp.zeros((32, experts), F32)
        for k in range(6):
            chosen = jnp.where(routes[:, k : k + 1] == ids, 1.0, chosen)
        ti = lax.broadcasted_iota(jnp.int32, (32, 32), 0)
        tj = lax.broadcasted_iota(jnp.int32, (32, 32), 1)
        before = flag((ti // 8 == tj // 8) & (tj < ti))
        rank = jnp.where(chosen > 0.0, dot(before, chosen.astype(BF16)), -1.0)
        col = lax.broadcasted_iota(jnp.int32, (experts, 128), 1)
        spread = flag(lax.broadcasted_iota(jnp.int32, (experts, 128), 0) == zl * 16 + col // 8)
        spread_rank = dot(rank.astype(BF16), spread)
        ct = lax.broadcasted_iota(jnp.int32, (32, 128), 1)
        rt = lax.broadcasted_iota(jnp.int32, (32, 128), 0)
        pick = jnp.where(
            (spread_rank == (ct % 2).astype(F32)) & (rt // 8 == (ct // 2) % 4), 1.0, 0.0
        )
        picks.append(pick)
        masks.append(chosen)

    here = along_x(3)
    logs = jnp.zeros((REQ, 128), F32)
    for j in range(QT):
        logs = jnp.where(lane == j, new_log[j * REQ : (j + 1) * REQ], logs)
    for n in (2, 0, 1):
        along_z(n).wait()
    pieces, _ = blend(here + [got_z[n] for n in range(3)], (new_valued, logs))
    valued = jnp.concatenate(pieces, axis=0)
    di = lax.broadcasted_iota(jnp.int32, (rows, rows), 0)
    si = lax.broadcasted_iota(jnp.int32, (rows, rows), 1)
    req = ((di % 64) // 16) * 4 + ((di % 16) // 8) * 2 + di // 64
    perm = flag(si == (di % 8) * REQ + req)
    valued_s[...] = dot(perm, valued).astype(BF16).reshape(2, 64, 128)
    half = outw_ref.shape[1] // 2
    cols = [pl.ds(h * half, half) for h in range(2)]
    own_8 = lax.broadcasted_iota(jnp.int32, (16, 1), 0) // 8 == zh
    for h in range(2):
        csend[h] = dot(valued_s[1 - c], outw_ref[:, cols[h]]).astype(BF16)
        remote(csend.at[h], crecv.at[h], cs.at[h], cr.at[h], other).start()
    own = [dot(valued_s[c], outw_ref[:, cols[h]]) for h in range(2)]
    for h in range(2):
        remote(csend.at[h], crecv.at[h], cs.at[h], cr.at[h], other).wait()
        acc[h] = (own[h] + crecv[h].astype(F32)).reshape(4, 16, half)
        ysend[h] = acc[h].astype(BF16)
        for i in (2, 1, 3):
            peer = lax.rem(y + i, 4)
            remote(
                ysend.at[h, peer],
                yrecv.at[h, i],
                ys.at[h, i],
                yr.at[h, i],
                dev(x, peer, zl, zh, c),
            ).start()
    sums = []
    for h in range(2):
        row = acc[h, y]
        for i in (1, 3, 2):
            remote(ysend.at[h, 0], yrecv.at[h, i], ys.at[h, i], yr.at[h, i], other).wait()
            row = row + yrecv[h, i].astype(F32)
        resid = resid_ref[:, cols[h]].astype(F32)
        row = row + jnp.where(own_8, jnp.concatenate([resid, resid], axis=0), 0.0)
        zsend[h] = row.astype(BF16)
        sums.append(row)
        for d in (1, 3, 2):
            remote(zsend.at[h], zrecv.at[d, h], ns.at[d, h], nr.at[d, h], line(d)).start()
    for h in range(2):
        for d in (5, 7, 4, 6):
            remote(zsend.at[h], zrecv.at[d, h], ns.at[d, h], nr.at[d, h], line(d)).start()
    total_row = jnp.concatenate(sums, axis=1)

    def column(d):
        for h in range(2):
            remote(zsend.at[h], zrecv.at[d, h], ns.at[d, h], nr.at[d, h], other).wait()
        return jnp.concatenate([zrecv[d, 0], zrecv[d, 1]], axis=1).astype(F32)

    gain = gain_ref[...].reshape(1, gain_ref.shape[0]).astype(F32)

    def norm(hidden):
        square = jnp.mean(hidden * hidden, axis=1, keepdims=True)
        return (hidden * lax.rsqrt(square + EPSILON) * gain).astype(BF16)

    hidden = total_row + column(1)
    hidden_s[...] = hidden.reshape(2, 8, 2048)
    normed[zl] = norm(hidden)
    share_in[x, zl] = normed[zl].reshape(2, 8, 2048)[0]

    @pl.when(zh == 1)
    def _():
        share_in[x, zl] = normed[zl].reshape(2, 8, 2048)[1]

    for i in (2, 1, 3):
        block = share_in.at[x, zl]
        peer = dev(lax.rem(x + i, 4), y, zl, zh, c)
        remote(block, block, xs.at[0, i], xr.at[0, i], peer).start()

    def pack(chunk):
        tokens = normed[pl.ds(pairs[chunk] * 2, 2)].reshape(32, 2048)
        packed[chunk] = (
            lax.dot_general(
                picks[chunk].astype(BF16),
                tokens,
                (((0,), (0,)), ((), ())),
                preferred_element_type=F32,
            )
            .astype(BF16)
            .reshape(16, 8, 2048)
        )

        for dx, dy in OFFSETS:
            to_x, to_y = lax.rem(x + dx, 4), lax.rem(y + dy, 4)
            remote(
                packed.at[chunk, to_x * 4 + to_y],
                arrived.at[chunk, c, mine],
                ds.at[chunk, dx * 4 + dy],
                dr.at[chunk, dx * 4 + dy],
                dev(to_x, to_y, zl, zh, c),
            ).start()
        arrived[chunk, c, mine] = packed[chunk, mine]
        here = arrived.at[chunk, c, mine]
        remote(here, here, fs.at[chunk, 0], fr.at[chunk, 0], other).start()
        logits = dot_nt(tokens, router_ref[...])
        sigma = jax.nn.sigmoid(logits) * masks[chunk]
        route_w = ROUTE_SCALE * sigma / jnp.sum(sigma, axis=1, keepdims=True)
        col = lax.broadcasted_iota(jnp.int32, (experts, 128), 1)
        spread = flag(lax.broadcasted_iota(jnp.int32, (experts, 128), 0) == zl * 16 + col // 8)
        w_hi, w_mid, w_low = split3(route_w)
        return (
            dot(w_hi.astype(BF16), spread)
            + dot(w_mid.astype(BF16), spread)
            + dot(w_low.astype(BF16), spread)
        ) * picks[chunk]

    normed[lines[1]] = norm(column(2) + column(3))
    combine0 = pack(0)
    normed[lines[2]] = norm(column(4) + column(5))
    normed[lines[3]] = norm(column(6) + column(7))
    combine1 = pack(1)
    combines = (combine0, combine1)
    for d in range(1, 4):
        both = normed[lines[d]].reshape(2, 8, 2048)
        share_in[x, lines[d]] = jnp.where(zh == 0, both[0], both[1])
    for i in (1, 3, 2):
        block = share_in.at[lax.rem(x - i + 4, 4), zl]
        remote(share_in.at[x, zl], block, xs.at[0, i], xr.at[0, i], other).wait()
        for d in range(1, 4):
            remote(block, block, xs.at[d, i], xr.at[d, i], line(2 * d)).start()

    def forward(chunk):
        def step(i, carry):
            src = source(i)
            block = arrived.at[chunk, c, src]
            remote(packed.at[chunk, src], block, ds.at[chunk, i], dr.at[chunk, i], other).wait()
            remote(block, block, fs.at[chunk, i], fr.at[chunk, i], other).start()
            return carry

        lax.fori_loop(1, 16, step, 0)

    def crossed(chunk):
        def step(i, carry):
            src = source(i)
            block = arrived.at[chunk, c, src]
            remote(
                block, arrived.at[chunk, 1 - c, src], fs.at[chunk, i], fr.at[chunk, i], other
            ).wait()
            return carry

        lax.fori_loop(0, 16, step, 0)

    def ffn(rows_in, both_w, gap, units, down):
        val = dot_nt(rows_in, both_w[...])
        hidden = (jax.nn.silu(val[:, :units]) * val[:, gap : gap + units]).astype(BF16)
        return dot(hidden, down[...])

    def routed_ffn(chunk):
        out = ffn(arrived[chunk].reshape(256, 2048), gate_up, GAP, ff, down_w)
        first, second = out[:128], out[128:]
        own_out[chunk] = jnp.where(c == 0, first, second)
        cross_send[chunk] = jnp.where(c == 0, second, first).astype(BF16)
        remote(
            cross_send.at[chunk], cross_recv.at[chunk], os_.at[chunk], or_.at[chunk], other
        ).start()

    def give(chunk):
        remote(
            cross_send.at[chunk], cross_recv.at[chunk], os_.at[chunk], or_.at[chunk], other
        ).wait()
        ret_send[chunk] = (
            (own_out[chunk] + cross_recv[chunk].astype(F32)).astype(BF16).reshape(16, 8, 2048)
        )

        for dx, dy in OFFSETS:
            to_x, to_y = lax.rem(x + dx, 4), lax.rem(y + dy, 4)
            remote(
                ret_send.at[chunk, to_x * 4 + to_y],
                ret_recv.at[chunk, mine],
                rs.at[chunk, dx * 4 + dy],
                rr.at[chunk, dx * 4 + dy],
                dev(to_x, to_y, zl, zh, c),
            ).start()
        ret_recv[chunk, mine] = ret_send[chunk, mine]

    forward(0)
    for load in loads[6:9]:
        load.wait()
    crossed(0)
    routed_ffn(0)
    forward(1)
    give(0)
    crossed(1)
    routed_ffn(1)

    give(1)

    for load in loads[9:]:
        load.wait()
    for i in (1, 3, 2):
        src = lax.rem(x - i + 4, 4)
        for d in range(1, 4):
            remote(
                share_in.at[src, zl], share_in.at[src, lines[d]], xs.at[d, i], xr.at[d, i], other
            ).wait()
    shared = ffn(share_in[...].reshape(128, 2048), sgate_up, SGAP, sff, sdown_w)
    share_out[...] = shared.reshape(4, 4, 8, 2048)
    for z in range(4):
        share_send[z] = share_out[:, z].astype(BF16)
    for d in (2, 3, 1):
        remote(
            share_send.at[lines[d]], share_recv.at[d], bs.at[d], br.at[d], line(2 * d)
        ).start()
    def take(chunk):
        def step(i, carry):
            src = source(i)
            remote(
                ret_send.at[chunk, src],
                ret_recv.at[chunk, src],
                rs.at[chunk, i],
                rr.at[chunk, i],
                other,
            ).wait()
            return carry

        lax.fori_loop(1, 16, step, 0)
        back = ret_recv[chunk].reshape(128, 2048)
        w_hi = combines[chunk].astype(BF16)
        w_low = (combines[chunk] - w_hi.astype(F32)).astype(BF16)
        routed = (dot(w_hi, back) + dot(w_low, back)).reshape(2, 2, 8, 2048)
        first = pl.ds(pairs[chunk] * 2, 2)
        part[first] = routed
        lsend[first] = routed.astype(BF16)

    def hand(d):
        block = lsend.at[lines[d // 2], halves[d % 2]]
        return remote(block, lrecv.at[d], ls.at[d], lr.at[d], line(d))

    take(0)
    for d in (1, 3, 2):
        hand(d).start()
    take(1)
    for d in (5, 7, 4, 6):
        hand(d).start()
    for d in (1, 2, 3):
        remote(share_send.at[lines[d]], share_recv.at[d], bs.at[d], br.at[d], other).wait()
    for n in range(4):
        both = share_out[n, zl]
        for d in range(1, 4):
            both = both + share_recv[d, n].astype(F32)
        share_sum[n] = both
        share_x[n] = both.astype(BF16)
    for i in (2, 1, 3):
        peer = lax.rem(x + i, 4)
        remote(
            share_x.at[peer], share_back.at[i], us.at[i], ur.at[i], dev(peer, y, zl, zh, c)
        ).start()
    result = hidden_s[zh] + part[zl, zh] + share_sum[x]
    for d in (2, 1, 3, 4, 6, 5, 7):
        hand(d).wait()
        result = result + lrecv[d].astype(F32)
    for i in (1, 3, 2):
        remote(share_x.at[lax.rem(x + i, 4)], share_back.at[i], us.at[i], ur.at[i], other).wait()
        result = result + share_back[i].astype(F32)
    out_ref[...] = result.astype(BF16)


def layer(vmem_args, more, weights):
    gate, up, down, sgate, sup, sdown = weights
    width = gate.shape[1]
    return pl.pallas_call(
        layer_kernel,
        name="layer",
        out_shape=jax.ShapeDtypeStruct((8, width), BF16),
        in_specs=[vmem_spec()] * len(vmem_args) + [hbm_spec()] * (len(more) + 6),
        out_specs=vmem_spec(),
        scratch_shapes=[VMEM(m.shape, BF16) for m in more]
        + [
            VMEM((GAP + gate.shape[0], width), BF16),
            VMEM(down.shape, BF16),
            VMEM((SGAP + sgate.shape[0], width), BF16),
            VMEM(sdown.shape, BF16),
            VMEM((4, 4, REQ, MSG), BF16),
            VMEM((3, REQ, MSG), BF16),
            VMEM((3, REQ, MSG), BF16),
            VMEM((2, 64, 128), BF16),
            VMEM((2, 64, width // 2), BF16),
            VMEM((2, 64, width // 2), BF16),
            VMEM((2, 4, 16, width // 2), F32),
            VMEM((2, 4, 16, width // 2), BF16),
            VMEM((2, 4, 16, width // 2), BF16),
            VMEM((2, 16, width // 2), BF16),
            VMEM((8, 2, 16, width // 2), BF16),
            VMEM((2, 8, width), F32),
            VMEM((4, 16, width), BF16),
            VMEM((2, 16, 8, width), BF16),
            VMEM((2, 2, 16, 8, width), BF16),
            VMEM((2, 128, width), F32),
            VMEM((2, 128, width), BF16),
            VMEM((2, 128, width), BF16),
            VMEM((2, 16, 8, width), BF16),
            VMEM((2, 16, 8, width), BF16),
            VMEM((4, 4, 8, width), BF16),
            VMEM((4, 4, 8, width), F32),
            VMEM((4, 4, 8, width), BF16),
            VMEM((4, 4, 8, width), BF16),
            VMEM((4, 8, width), F32),
            VMEM((4, 8, width), BF16),
            VMEM((4, 8, width), BF16),
            VMEM((4, 2, 8, width), F32),
            VMEM((4, 2, 8, width), BF16),
            VMEM((8, 8, width), BF16),
            DMA((12,)),
            DMA((4, 4)),
            DMA((4, 4)),
            DMA((3,)),
            DMA((3,)),
            DMA((2,)),
            DMA((2,)),
            DMA((2, 4)),
            DMA((2, 4)),
            DMA((8, 2)),
            DMA((8, 2)),
            DMA((2, 16)),
            DMA((2, 16)),
            DMA((2, 16)),
            DMA((2, 16)),
            DMA((2,)),
            DMA((2,)),
            DMA((2, 16)),
            DMA((2, 16)),
            DMA((4, 4)),
            DMA((4, 4)),
            DMA((4,)),
            DMA((4,)),
            DMA((4,)),
            DMA((4,)),
            DMA((8,)),
            DMA((8,)),
        ],
        compiler_params=pltpu.CompilerParams(
            collective_id=1, has_side_effects=True, vmem_limit_bytes=44 << 20
        ),
    )(*vmem_args, *map(stay, more), *map(stay, weights))


def on_device(
    query_nope,
    query_rope,
    absorb_weight,
    value_weight,
    output_weight,
    cache_latent,
    cache_rope,
    node_length,
    new_latent,
    new_rope,
    parent_node,
    leaf_node,
    residual,
    norm_gain,
    router_weight,
    routes,
    expert_gate,
    expert_up,
    expert_down,
    shared_gate,
    shared_up,
    shared_down,
):
    q_all, routes8, pick, place, lat, krope, absorb, value = gather(
        query_nope[:, 0, :],
        query_rope[:, 0, :].T,
        routes,
        leaf_node,
        parent_node,
        cache_latent,
        jnp.swapaxes(cache_rope, 1, 2),
        absorb_weight[0],
        value_weight[0],
    )
    msg = attend(
        node_length, q_all.reshape(16 * REQ, -1), pick, place, absorb, value, lat, krope
    )
    return layer(
        (msg.reshape(16, REQ, MSG), q_all, routes8, absorb, value),
        (norm_gain, new_latent, new_rope.T, residual, router_weight.T, output_weight),
        (
            expert_gate[0].T,
            expert_up[0].T,
            expert_down[0],
            shared_gate.T,
            shared_up.T,
            shared_down,
        ),
    )


def solution(mesh):
    in_specs = (
        P("group", "expert", None),
        P("group", "expert", None),
        P("expert", None, None),
        P("expert", None, None),
        P("expert", None),
        P("group", None, None),
        P("group", None, None),
        P("group"),
        P("group", None),
        P("group", None),
        P(),
        P(),
        P(("group", "expert"), None),
        P(),
        P(),
        P(("group", "expert"), None),
        P(("group", "expert"), None, None),
        P(("group", "expert"), None, None),
        P(("group", "expert"), None, None),
        P(None, "group"),
        P(None, "group"),
        P("group", None),
    )
    out_specs = P(("group", "expert"), None)
    return jax.shard_map(
        on_device, mesh=mesh, in_specs=in_specs, out_specs=out_specs, check_vma=False
    )
```

```python
import jax
import jax.numpy as jnp
from jax import lax
from jax.experimental import pallas as pl
from jax.experimental.pallas import tpu as pltpu
from jax.sharding import PartitionSpec as P

ROUTE_SCALE = 2.446
NEGATIVE = -1e30
EPSILON = 1e-06
MESH = pl.DeviceIdType.MESH
F32 = jnp.float32
BF16 = jnp.bfloat16
VMEM = pltpu.VMEM
DMA = pltpu.SemaphoreType.DMA

REQ = 16
QT = 8
MSG = 1024 + 128


def vmem_spec():
    return pl.BlockSpec(memory_space=pltpu.VMEM)


def hbm_spec():
    return pl.BlockSpec(memory_space=pltpu.HBM)


def stay(x):
    return pltpu.with_memory_space_constraint(x, pltpu.HBM)


def start_loads(pairs, sem):
    loads = [pltpu.make_async_copy(src, dst, sem.at[i]) for i, (src, dst) in enumerate(pairs)]
    for load in loads:
        load.start()
    return loads


def coords():
    g = lax.axis_index("group")
    e = lax.axis_index("expert")
    zl, x = g // 4, g % 4
    y, zh, c = e // 4, (e % 4) // 2, e % 2
    return g, e, x, y, zl, zh, c


def dev(x, y, zl, zh, c):
    return (zl * 4 + x, y * 4 + zh * 2 + c)


def remote(src, dst, send, recv, device):
    return pltpu.make_async_remote_copy(
        src_ref=src,
        dst_ref=dst,
        send_sem=send,
        recv_sem=recv,
        device_id=device,
        device_id_type=MESH,
    )


def greet(barrier, device):
    pl.semaphore_signal(barrier, inc=1, device_id=device, device_id_type=MESH)


def dot(a, b):
    return jnp.dot(a, b, preferred_element_type=F32)


def eye_column(row):
    n = row.shape[1]
    same = lax.broadcasted_iota(jnp.int32, (n, n), 0) == lax.broadcasted_iota(jnp.int32, (n, n), 1)
    return jnp.sum(jnp.where(same, row, 0), axis=1, keepdims=True)


def flag(condition):
    return jnp.where(condition, 1.0, 0.0).astype(BF16)


def dot_nt(a, b):
    return lax.dot_general(a, b, (((1,), (1,)), ((), ())), preferred_element_type=F32)


def on_path(leaf_row, parent_col, node):
    nodes = parent_col.shape[0]
    ids = lax.broadcasted_iota(jnp.int32, (nodes, leaf_row.shape[1]), 0)
    mid = jnp.sum(jnp.where(leaf_row == ids, parent_col, 0), axis=0, keepdims=True)
    top = jnp.sum(jnp.where(mid == ids, parent_col, 0), axis=0, keepdims=True)
    return (leaf_row == node) | (mid == node) | (top == node)


def gather_kernel(
    nope_hbm,
    rope_hbm,
    routes_hbm,
    leaf_hbm,
    parent_hbm,
    lat_hbm,
    krope_hbm,
    absorb_hbm,
    value_hbm,
    qall,
    routes8,
    pick_ref,
    place_ref,
    lat_ref,
    krope_ref,
    absorb_ref,
    value_ref,
    nope_v,
    rope_v,
    routes_v,
    leaf_v,
    parent_v,
    mine,
    wsem,
    zq,
    zqr,
    xq,
    xqr,
    rs,
    rr,
):
    g, e, x, y, zl, zh, c = coords()
    loads = start_loads(
        [
            (nope_hbm, nope_v),
            (rope_hbm, rope_v),
            (routes_hbm, routes_v),
            (leaf_hbm, leaf_v),
            (parent_hbm, parent_v),
            (lat_hbm, lat_ref),
            (krope_hbm, krope_ref),
            (absorb_hbm, absorb_ref),
            (value_hbm, value_ref),
        ],
        wsem,
    )
    barrier = pltpu.get_barrier_semaphore()
    partner = dev(x, y, zl, 1 - zh, c)
    me = zl * 2 + zh
    for i in range(1, 4):
        greet(barrier, dev(lax.rem(x + i, 4), y, zl, zh, c))
        greet(barrier, dev(x, y, lax.rem(zl + i, 4), zh, c))
    for k in (1, 3, 5, 7):
        s = lax.rem(me + k, 8)
        greet(barrier, dev(x, y, s // 2, s % 2, c))

    rows = REQ * QT
    di = lax.broadcasted_iota(jnp.int32, (rows, rows), 0)
    si = lax.broadcasted_iota(jnp.int32, (rows, rows), 1)
    perm = flag(si == (di % REQ) * QT + di // REQ)
    for load in loads[:3]:
        load.wait()
    nope = dot(perm, nope_v[...]).astype(BF16)
    rope = dot_nt(perm, rope_v[...]).astype(BF16)
    qall[g] = jnp.concatenate(
        [nope[j * REQ : (j + 1) * REQ] for j in range(QT)]
        + [rope[j * REQ : (j + 1) * REQ] for j in range(QT)],
        axis=1,
    )
    mine[...] = jnp.zeros_like(mine)
    mine[:, 0 : routes_v.shape[1]] = routes_v[...]
    routes8[me] = mine[...]
    pl.semaphore_wait(barrier, 10)

    own = qall.at[g]
    for i in (1, 3, 2):
        remote(own, own, zq.at[i], zqr.at[i], dev(x, y, lax.rem(zl + i, 4), zh, c)).start()
    for k in (2, 1, 3):
        remote(own, own, xq.at[0, k], xqr.at[0, k], dev(lax.rem(x + k, 4), y, zl, zh, c)).start()
    for k in range(1, 8):
        s = lax.rem(me + k, 8)
        remote(mine, routes8.at[me], rs.at[k], rr.at[k], dev(x, y, s // 2, s % 2, c)).start()

    def pass_on(i):
        block = qall.at[lax.rem(zl - i + 4, 4) * 4 + x]
        remote(own, block, zq.at[i], zqr.at[i], partner).wait()
        for k in (2, 1, 3):
            remote(
                block, block, xq.at[i, k], xqr.at[i, k], dev(lax.rem(x + k, 4), y, zl, zh, c)
            ).start()

    pass_on(1)
    pass_on(3)
    pass_on(2)

    for load in loads[3:5]:
        load.wait()
    slots, _, requests = pick_ref.shape
    ids_0 = lax.broadcasted_iota(jnp.int32, (requests, requests), 0)
    ids_1 = lax.broadcasted_iota(jnp.int32, (requests, requests), 1)
    earlier = flag(ids_0 < ids_1)
    parent_col = eye_column(parent_v[...])
    for slot in range(slots):
        on_row = on_path(leaf_v[...], parent_col, g * slots + slot)
        row_f = jnp.where(on_row, 1.0, 0.0)
        rank_row = dot(jnp.broadcast_to(row_f, (8, requests)).astype(BF16), earlier)[0:1]
        rank_row = jnp.where(on_row, rank_row, -1.0)
        pick_ref[slot] = flag(rank_row.astype(jnp.int32) == ids_0)
        place_ref[slot] = flag(eye_column(rank_row).astype(jnp.int32) == ids_1)

    for load in loads[5:]:
        load.wait()
    for k in range(1, 8):
        s = lax.rem(me - k + 8, 8)
        remote(mine, routes8.at[s], rs.at[k], rr.at[k], partner).wait()
    for i in range(4):
        for k in (1, 3, 2):
            block = qall.at[lax.rem(zl - i + 4, 4) * 4 + lax.rem(x - k + 4, 4)]
            remote(own, block, xq.at[i, k], xqr.at[i, k], partner).wait()


def gather(nope, rope_t, routes, leaf, parent, lat, krope_t, absorb, value):
    requests = leaf.shape[0]
    slots = lat.shape[0]
    return pl.pallas_call(
        gather_kernel,
        name="gather_queries",
        out_shape=(
            jax.ShapeDtypeStruct((16, REQ, QT * 192), BF16),
            jax.ShapeDtypeStruct((8, 8, 128), jnp.int32),
            jax.ShapeDtypeStruct((slots, requests, requests), BF16),
            jax.ShapeDtypeStruct((slots, requests, requests), BF16),
            jax.ShapeDtypeStruct(lat.shape, BF16),
            jax.ShapeDtypeStruct(krope_t.shape, BF16),
            jax.ShapeDtypeStruct(absorb.shape, BF16),
            jax.ShapeDtypeStruct(value.shape, BF16),
        ),
        in_specs=[hbm_spec()] * 9,
        out_specs=(vmem_spec(),) * 8,
        scratch_shapes=[
            VMEM(nope.shape, BF16),
            VMEM(rope_t.shape, BF16),
            VMEM(routes.shape, jnp.int32),
            VMEM((1, requests), jnp.int32),
            VMEM((1, parent.shape[0]), jnp.int32),
            VMEM((8, 128), jnp.int32),
            DMA((9,)),
            DMA((4,)),
            DMA((4,)),
            DMA((4, 4)),
            DMA((4, 4)),
            DMA((8,)),
            DMA((8,)),
        ],
        compiler_params=pltpu.CompilerParams(
            collective_id=0, has_side_effects=True, vmem_limit_bytes=24 << 20
        ),
    )(
        *map(
            stay,
            (nope, rope_t, routes, leaf[None, :], parent[None, :], lat, krope_t, absorb, value),
        )
    )


TILE = 32
KEYS = 256


def split3(v):
    hi = v.astype(BF16)
    rest = v - hi.astype(F32)
    mid = rest.astype(BF16)
    low = (rest - mid.astype(F32)).astype(BF16)
    return hi.astype(F32), mid.astype(F32), low.astype(F32)


def pack_logs(logs):
    hi, mid, low = split3(logs)
    return hi + pltpu.roll(mid, 8, 1) + pltpu.roll(low, 16, 1)


def join_logs(tail):
    return tail + pltpu.roll(tail, 120, 1) + pltpu.roll(tail, 112, 1)


def attn_kernel(
    q_ref,
    pick_ref,
    place_ref,
    absorb_ref,
    value_ref,
    lat_ref,
    rope_ref,
    len_hbm,
    out_ref,
    len_ref,
    picked,
    done,
    wsem,
):
    (load,) = start_loads([(len_hbm, len_ref)], wsem)
    requests = q_ref.shape[0]
    slots, most = lat_ref.shape[0], lat_ref.shape[1]
    scaling = float(128 + 64) ** (-0.5)
    done[...] = jnp.zeros_like(done)
    lane = lax.broadcasted_iota(jnp.int32, (TILE, 128), 1)
    counts = []
    for slot in range(slots):
        picked[slot] = dot(pick_ref[slot], q_ref[...]).astype(BF16)
        counts.append(jnp.sum(pick_ref[slot].astype(F32)).astype(jnp.int32))
    load.wait()

    for slot in range(slots):
        length = len_ref[slot]

        def tile(keys, step, carry):
            here = pl.ds(pl.multiple_of(step * TILE, TILE), TILE)
            qt = picked[slot, here]
            nope = jnp.concatenate([qt[:, j * 128 : j * 128 + 128] for j in range(QT)], axis=0)
            rot = jnp.concatenate(
                [qt[:, 1024 + j * 64 : 1024 + j * 64 + 64] for j in range(QT)], axis=0
            )
            lat = dot(nope, absorb_ref[...]).astype(BF16)
            scores = dot_nt(lat, lat_ref[slot, :keys]) + dot(rot, rope_ref[slot, :, :keys])
            positions = lax.broadcasted_iota(jnp.int32, (1, keys), 1)
            scores = jnp.where(positions < length, scores * scaling, NEGATIVE)
            top = jnp.max(scores, axis=1, keepdims=True)
            weights = jnp.exp(scores - top).astype(BF16)
            total = jnp.sum(weights.astype(F32), axis=1, keepdims=True)
            summed = dot(weights, lat_ref[slot, :keys])
            attended = (summed / total).astype(BF16)
            valued = dot(attended, value_ref[...]).astype(BF16)
            log_sum = top + jnp.log(total)
            logs = jnp.zeros((TILE, 128), F32)
            for j in range(QT):
                logs = jnp.where(lane == j, log_sum[j * TILE : (j + 1) * TILE], logs)
            tail = jnp.where((lane >= 24) & (lane < 32), 1.0, pack_logs(logs))
            done[slot, here] = jnp.concatenate(
                [valued[j * TILE : (j + 1) * TILE] for j in range(QT)] + [tail.astype(BF16)],
                axis=1,
            )
            return carry

        tiles = (counts[slot] + TILE - 1) // TILE
        for keys in range(KEYS, most + 1, KEYS):

            @pl.when((length > keys - KEYS) & (length <= keys))
            def _():
                lax.fori_loop(0, tiles, lambda step, carry: tile(keys, step, carry), 0)

    acc = [dot(place_ref[s], done[s]) for s in range(slots)]
    tails = [a[:, 1024:] for a in acc]
    logs = [jnp.where(pltpu.roll(t, 104, 1) > 0.5, join_logs(t), NEGATIVE) for t in tails]
    top = logs[0]
    for s in range(1, slots):
        top = jnp.maximum(top, logs[s])
    shares = [jnp.exp(v - top) for v in logs]
    total = shares[0]
    for s in range(1, slots):
        total = total + shares[s]
    shares = [v / total for v in shares]
    for j in range(QT):
        out = 0.0
        for s in range(slots):
            out = out + shares[s][:, j : j + 1] * acc[s][:, j * 128 : j * 128 + 128]
        out_ref[:, j * 128 : j * 128 + 128] = out.astype(BF16)
    lanes = lax.broadcasted_iota(jnp.int32, (requests, 128), 1)
    log_sum = jnp.where(lanes < QT, top + jnp.log(total), 0.0)
    out_ref[:, 1024:] = pack_logs(log_sum).astype(BF16)


def attend(node_length, q_all, pick, place, absorb, value, lat, rope_t):
    requests = q_all.shape[0]
    slots = lat.shape[0]
    return pl.pallas_call(
        attn_kernel,
        name="attend_nodes",
        out_shape=jax.ShapeDtypeStruct((requests, MSG), BF16),
        in_specs=[vmem_spec()] * 7 + [hbm_spec()],
        out_specs=vmem_spec(),
        scratch_shapes=[
            pltpu.SMEM(node_length.shape, jnp.int32),
            VMEM((slots, requests, q_all.shape[1]), BF16),
            VMEM((slots, requests, MSG), BF16),
            DMA((1,)),
        ],
        compiler_params=pltpu.CompilerParams(vmem_limit_bytes=32 << 20),
    )(q_all, pick, place, absorb, value, lat, rope_t, stay(node_length))


OFFSETS = sorted(
    [(i, j) for i in range(4) for j in range(4) if i or j],
    key=lambda o: -min(o[0], 4 - o[0]) - min(o[1], 4 - o[1]),
)

GAP = 384
SGAP = 256


def layer_kernel(
    msg_ref,
    q_ref,
    routes_ref,
    absorb_ref,
    value_ref,
    gain_hbm,
    newlat_hbm,
    newrope_hbm,
    resid_hbm,
    router_hbm,
    outw_hbm,
    gate_hbm,
    up_hbm,
    down_hbm,
    sgate_hbm,
    sup_hbm,
    sdown_hbm,
    out_ref,
    gain_ref,
    newlat_ref,
    newrope_ref,
    resid_ref,
    router_ref,
    outw_ref,
    gate_up,
    down_w,
    sgate_up,
    sdown_w,
    got,
    got_z,
    blended,
    valued_s,
    csend,
    crecv,
    acc,
    ysend,
    yrecv,
    zsend,
    zrecv,
    hidden_s,
    normed,
    packed,
    arrived,
    own_out,
    cross_send,
    cross_recv,
    ret_send,
    ret_recv,
    share_in,
    share_out,
    share_send,
    share_recv,
    share_sum,
    share_x,
    share_back,
    part,
    lsend,
    lrecv,
    wsem,
    ms,
    mr,
    gs,
    gr,
    cs,
    cr,
    ys,
    yr,
    ns,
    nr,
    ds,
    dr,
    fs,
    fr,
    os_,
    or_,
    rs,
    rr,
    xs,
    xr,
    bs,
    br,
    us,
    ur,
    ls,
    lr,
):
    g, e, x, y, zl, zh, c = coords()
    mine = x * 4 + y
    ff = gate_hbm.shape[0]
    sff = sgate_hbm.shape[0]
    barrier = pltpu.get_barrier_semaphore()

    def source(i):
        return lax.rem(x - i // 4 + 4, 4) * 4 + lax.rem(y - i % 4 + 4, 4)

    other = dev(x, y, zl, zh, 1 - c)
    partner = dev(x, y, zl, 1 - zh, c)
    greet(barrier, other)
    greet(barrier, partner)
    for i in range(4):
        for k in range(1, 4):
            greet(barrier, dev(lax.rem(x + i, 4), lax.rem(y + k, 4), zl, zh, c))
    lines = (zl, zl + 1 - 2 * (zl % 2), zl + 2 - 4 * (zl // 2), 3 - zl)
    halves = (zh, 1 - zh)

    def line(d):
        return dev(x, y, lines[d // 2], halves[d % 2], c)

    for d in range(2, 8):
        greet(barrier, line(d))
    for i in range(1, 4):
        greet(barrier, dev(lax.rem(x + i, 4), y, zl, zh, c))
    loads = start_loads(
        [
            (gain_hbm, gain_ref),
            (newlat_hbm, newlat_ref),
            (newrope_hbm, newrope_ref),
            (resid_hbm, resid_ref),
            (router_hbm, router_ref),
            (outw_hbm, outw_ref),
            (gate_hbm, gate_up.at[pl.ds(0, ff)]),
            (up_hbm, gate_up.at[pl.ds(GAP, ff)]),
            (down_hbm, down_w),
            (sgate_hbm, sgate_up.at[pl.ds(0, sff)]),
            (sup_hbm, sgate_up.at[pl.ds(SGAP, sff)]),
            (sdown_hbm, sdown_w),
        ],
        wsem,
    )
    gate_up[ff:GAP] = jnp.zeros((GAP - ff, gate_up.shape[1]), BF16)
    sgate_up[sff:SGAP] = jnp.zeros((SGAP - sff, sgate_up.shape[1]), BF16)

    pl.semaphore_wait(barrier, 23)

    homes = (lines[2], lines[3], lines[1], zl)
    for n in range(4):
        for i in (2, 1, 3):
            peer = lax.rem(x + i, 4)
            remote(
                msg_ref.at[homes[n] * 4 + peer],
                got.at[n, i],
                ms.at[n, i],
                mr.at[n, i],
                dev(peer, y, zl, zh, c),
            ).start()

    scaling = float(128 + 64) ** (-0.5)
    for load in loads[:6]:
        load.wait()
    q = q_ref[g]
    nope = jnp.concatenate([q[:, j * 128 : j * 128 + 128] for j in range(QT)], axis=0)
    rot = jnp.concatenate([q[:, 1024 + j * 64 : 1024 + j * 64 + 64] for j in range(QT)], axis=0)
    lat = dot(nope, absorb_ref[...]).astype(BF16)
    scores = dot_nt(lat, newlat_ref[...]) + dot(rot, newrope_ref[...])
    rows = REQ * QT
    qi = lax.broadcasted_iota(jnp.int32, (rows, rows), 0)
    ki = lax.broadcasted_iota(jnp.int32, (rows, rows), 1)
    usable = ((qi % REQ) == (ki // QT)) & ((ki % QT) <= (qi // REQ))
    scores = jnp.where(usable, scores * scaling, NEGATIVE)
    top = jnp.max(scores, axis=1, keepdims=True)
    weights = jnp.where(usable, jnp.exp(scores - top), 0.0).astype(BF16)
    total = jnp.sum(weights.astype(F32), axis=1, keepdims=True)
    summed = dot(weights, newlat_ref[...]) / total
    new_valued = dot(summed.astype(BF16), value_ref[...])
    new_log = top + jnp.log(total)

    def blend(parts, more=None):
        logs = [join_logs(p[:, 1024:].astype(F32)) for p in parts]
        if more is not None:
            logs.append(more[1])
        peak = logs[0]
        for v in logs[1:]:
            peak = jnp.maximum(peak, v)
        shares = [jnp.exp(v - peak) for v in logs]
        whole = shares[0]
        for v in shares[1:]:
            whole = whole + v
        shares = [v / whole for v in shares]
        values = []
        for j in range(QT):
            value = 0.0
            for p, share in zip(parts, shares):
                value = value + share[:, j : j + 1] * p[:, j * 128 : j * 128 + 128].astype(F32)
            if more is not None:
                value = value + shares[-1][:, j : j + 1] * more[0][j * REQ : (j + 1) * REQ]
            values.append(value.astype(BF16))
        return values, peak + jnp.log(whole)

    def along_x(n):
        for i in (1, 3, 2):
            src = msg_ref.at[homes[n] * 4 + lax.rem(x + i, 4)]
            remote(src, got.at[n, i], ms.at[n, i], mr.at[n, i], other).wait()
        return [msg_ref[homes[n] * 4 + x]] + [got[n, i] for i in range(1, 4)]

    lane = lax.broadcasted_iota(jnp.int32, (REQ, 128), 1)

    def along_z(n):
        return remote(
            blended.at[n], got_z.at[n], gs.at[n], gr.at[n], dev(x, y, homes[n], zh, c)
        )

    for n in range(3):
        values, log_sum = blend(along_x(n))
        tail = pack_logs(jnp.where(lane < QT, log_sum, 0.0)).astype(BF16)
        blended[n] = jnp.concatenate(values + [tail], axis=1)
        along_z(n).start()

    experts = router_ref.shape[0]
    pairs = (zl // 2, 1 - zl // 2)
    picks, masks = [], []
    for q_ in range(2):
        routes = routes_ref[pl.ds(pairs[q_] * 4, 4)].reshape(32, 128)
        ids = lax.broadcasted_iota(jnp.int32, (32, experts), 1)
        chosen = jnp.zeros((32, experts), F32)
        for k in range(6):
            chosen = jnp.where(routes[:, k : k + 1] == ids, 1.0, chosen)
        ti = lax.broadcasted_iota(jnp.int32, (32, 32), 0)
        tj = lax.broadcasted_iota(jnp.int32, (32, 32), 1)
        before = flag((ti // 8 == tj // 8) & (tj < ti))
        rank = jnp.where(chosen > 0.0, dot(before, chosen.astype(BF16)), -1.0)
        col = lax.broadcasted_iota(jnp.int32, (experts, 128), 1)
        spread = flag(lax.broadcasted_iota(jnp.int32, (experts, 128), 0) == zl * 16 + col // 8)
        spread_rank = dot(rank.astype(BF16), spread)
        ct = lax.broadcasted_iota(jnp.int32, (32, 128), 1)
        rt = lax.broadcasted_iota(jnp.int32, (32, 128), 0)
        pick = jnp.where(
            (spread_rank == (ct % 2).astype(F32)) & (rt // 8 == (ct // 2) % 4), 1.0, 0.0
        )
        picks.append(pick)
        masks.append(chosen)

    here = along_x(3)
    logs = jnp.zeros((REQ, 128), F32)
    for j in range(QT):
        logs = jnp.where(lane == j, new_log[j * REQ : (j + 1) * REQ], logs)
    for n in (2, 0, 1):
        along_z(n).wait()
    pieces, _ = blend(here + [got_z[n] for n in range(3)], (new_valued, logs))
    valued = jnp.concatenate(pieces, axis=0)
    di = lax.broadcasted_iota(jnp.int32, (rows, rows), 0)
    si = lax.broadcasted_iota(jnp.int32, (rows, rows), 1)
    req = ((di % 64) // 16) * 4 + ((di % 16) // 8) * 2 + di // 64
    perm = flag(si == (di % 8) * REQ + req)
    valued_s[...] = dot(perm, valued).astype(BF16).reshape(2, 64, 128)
    half = outw_ref.shape[1] // 2
    cols = [pl.ds(h * half, half) for h in range(2)]
    own_8 = lax.broadcasted_iota(jnp.int32, (16, 1), 0) // 8 == zh
    for h in range(2):
        csend[h] = dot(valued_s[1 - c], outw_ref[:, cols[h]]).astype(BF16)
        remote(csend.at[h], crecv.at[h], cs.at[h], cr.at[h], other).start()
    own = [dot(valued_s[c], outw_ref[:, cols[h]]) for h in range(2)]
    for h in range(2):
        remote(csend.at[h], crecv.at[h], cs.at[h], cr.at[h], other).wait()
        acc[h] = (own[h] + crecv[h].astype(F32)).reshape(4, 16, half)
        ysend[h] = acc[h].astype(BF16)
        for i in (2, 1, 3):
            peer = lax.rem(y + i, 4)
            remote(
                ysend.at[h, peer],
                yrecv.at[h, i],
                ys.at[h, i],
                yr.at[h, i],
                dev(x, peer, zl, zh, c),
            ).start()
    sums = []
    for h in range(2):
        row = acc[h, y]
        for i in (1, 3, 2):
            remote(ysend.at[h, 0], yrecv.at[h, i], ys.at[h, i], yr.at[h, i], other).wait()
            row = row + yrecv[h, i].astype(F32)
        resid = resid_ref[:, cols[h]].astype(F32)
        row = row + jnp.where(own_8, jnp.concatenate([resid, resid], axis=0), 0.0)
        zsend[h] = row.astype(BF16)
        sums.append(row)
        for d in (1, 3, 2):
            remote(zsend.at[h], zrecv.at[d, h], ns.at[d, h], nr.at[d, h], line(d)).start()
    for h in range(2):
        for d in (5, 7, 4, 6):
            remote(zsend.at[h], zrecv.at[d, h], ns.at[d, h], nr.at[d, h], line(d)).start()
    total_row = jnp.concatenate(sums, axis=1)

    def column(d):
        for h in range(2):
            remote(zsend.at[h], zrecv.at[d, h], ns.at[d, h], nr.at[d, h], other).wait()
        return jnp.concatenate([zrecv[d, 0], zrecv[d, 1]], axis=1).astype(F32)

    gain = gain_ref[...].reshape(1, gain_ref.shape[0]).astype(F32)

    def norm(hidden):
        square = jnp.mean(hidden * hidden, axis=1, keepdims=True)
        return (hidden * lax.rsqrt(square + EPSILON) * gain).astype(BF16)

    hidden = total_row + column(1)
    hidden_s[...] = hidden.reshape(2, 8, 2048)
    normed[zl] = norm(hidden)
    share_in[x, zl] = normed[zl].reshape(2, 8, 2048)[0]

    @pl.when(zh == 1)
    def _():
        share_in[x, zl] = normed[zl].reshape(2, 8, 2048)[1]

    for i in (2, 1, 3):
        block = share_in.at[x, zl]
        peer = dev(lax.rem(x + i, 4), y, zl, zh, c)
        remote(block, block, xs.at[0, i], xr.at[0, i], peer).start()

    def pack(chunk):
        tokens = normed[pl.ds(pairs[chunk] * 2, 2)].reshape(32, 2048)
        packed[chunk] = (
            lax.dot_general(
                picks[chunk].astype(BF16),
                tokens,
                (((0,), (0,)), ((), ())),
                preferred_element_type=F32,
            )
            .astype(BF16)
            .reshape(16, 8, 2048)
        )

        for dx, dy in OFFSETS:
            to_x, to_y = lax.rem(x + dx, 4), lax.rem(y + dy, 4)
            remote(
                packed.at[chunk, to_x * 4 + to_y],
                arrived.at[chunk, c, mine],
                ds.at[chunk, dx * 4 + dy],
                dr.at[chunk, dx * 4 + dy],
                dev(to_x, to_y, zl, zh, c),
            ).start()
        arrived[chunk, c, mine] = packed[chunk, mine]
        here = arrived.at[chunk, c, mine]
        remote(here, here, fs.at[chunk, 0], fr.at[chunk, 0], other).start()

    def weigh(chunk):
        tokens = normed[pl.ds(pairs[chunk] * 2, 2)].reshape(32, 2048)
        logits = dot_nt(tokens, router_ref[...])
        sigma = jax.nn.sigmoid(logits) * masks[chunk]
        route_w = ROUTE_SCALE * sigma / jnp.sum(sigma, axis=1, keepdims=True)
        col = lax.broadcasted_iota(jnp.int32, (experts, 128), 1)
        spread = flag(lax.broadcasted_iota(jnp.int32, (experts, 128), 0) == zl * 16 + col // 8)
        w_hi, w_mid, w_low = split3(route_w)
        return (
            dot(w_hi.astype(BF16), spread)
            + dot(w_mid.astype(BF16), spread)
            + dot(w_low.astype(BF16), spread)
        ) * picks[chunk]

    normed[lines[1]] = norm(column(2) + column(3))
    pack(0)
    normed[lines[2]] = norm(column(4) + column(5))
    normed[lines[3]] = norm(column(6) + column(7))
    pack(1)
    for d in range(1, 4):
        both = normed[lines[d]].reshape(2, 8, 2048)
        share_in[x, lines[d]] = jnp.where(zh == 0, both[0], both[1])
    for i in (1, 3, 2):
        block = share_in.at[lax.rem(x - i + 4, 4), zl]
        remote(share_in.at[x, zl], block, xs.at[0, i], xr.at[0, i], other).wait()
        for d in range(1, 4):
            remote(block, block, xs.at[d, i], xr.at[d, i], line(2 * d)).start()

    def forward(chunk):
        def step(i, carry):
            src = source(i)
            block = arrived.at[chunk, c, src]
            remote(packed.at[chunk, src], block, ds.at[chunk, i], dr.at[chunk, i], other).wait()
            remote(block, block, fs.at[chunk, i], fr.at[chunk, i], other).start()
            return carry

        lax.fori_loop(1, 16, step, 0)

    def crossed(chunk):
        def step(i, carry):
            src = source(i)
            block = arrived.at[chunk, c, src]
            remote(
                block, arrived.at[chunk, 1 - c, src], fs.at[chunk, i], fr.at[chunk, i], other
            ).wait()
            return carry

        lax.fori_loop(0, 16, step, 0)

    def ffn(rows_in, both_w, gap, units, down):
        val = dot_nt(rows_in, both_w[...])
        hidden = (jax.nn.silu(val[:, :units]) * val[:, gap : gap + units]).astype(BF16)
        return dot(hidden, down[...])

    def routed_ffn(chunk):
        out = ffn(arrived[chunk].reshape(256, 2048), gate_up, GAP, ff, down_w)
        first, second = out[:128], out[128:]
        own_out[chunk] = jnp.where(c == 0, first, second)
        cross_send[chunk] = jnp.where(c == 0, second, first).astype(BF16)
        remote(
            cross_send.at[chunk], cross_recv.at[chunk], os_.at[chunk], or_.at[chunk], other
        ).start()

    def give(chunk):
        remote(
            cross_send.at[chunk], cross_recv.at[chunk], os_.at[chunk], or_.at[chunk], other
        ).wait()
        ret_send[chunk] = (
            (own_out[chunk] + cross_recv[chunk].astype(F32)).astype(BF16).reshape(16, 8, 2048)
        )

        for dx, dy in OFFSETS:
            to_x, to_y = lax.rem(x + dx, 4), lax.rem(y + dy, 4)
            remote(
                ret_send.at[chunk, to_x * 4 + to_y],
                ret_recv.at[chunk, mine],
                rs.at[chunk, dx * 4 + dy],
                rr.at[chunk, dx * 4 + dy],
                dev(to_x, to_y, zl, zh, c),
            ).start()
        ret_recv[chunk, mine] = ret_send[chunk, mine]

    forward(0)
    for load in loads[6:9]:
        load.wait()
    crossed(0)
    routed_ffn(0)
    give(0)
    forward(1)
    crossed(1)
    routed_ffn(1)

    give(1)

    for load in loads[9:]:
        load.wait()
    for i in (1, 3, 2):
        src = lax.rem(x - i + 4, 4)
        for d in range(1, 4):
            remote(
                share_in.at[src, zl], share_in.at[src, lines[d]], xs.at[d, i], xr.at[d, i], other
            ).wait()
    shared = ffn(share_in[...].reshape(128, 2048), sgate_up, SGAP, sff, sdown_w)
    share_out[...] = shared.reshape(4, 4, 8, 2048)
    for z in range(4):
        share_send[z] = share_out[:, z].astype(BF16)
    for d in (2, 3, 1):
        remote(
            share_send.at[lines[d]], share_recv.at[d], bs.at[d], br.at[d], line(2 * d)
        ).start()
    combines = [weigh(chunk) for chunk in range(2)]

    def take(chunk):
        def step(i, carry):
            src = source(i)
            remote(
                ret_send.at[chunk, src],
                ret_recv.at[chunk, src],
                rs.at[chunk, i],
                rr.at[chunk, i],
                other,
            ).wait()
            return carry

        lax.fori_loop(1, 16, step, 0)
        back = ret_recv[chunk].reshape(128, 2048)
        w_hi = combines[chunk].astype(BF16)
        w_low = (combines[chunk] - w_hi.astype(F32)).astype(BF16)
        routed = (dot(w_hi, back) + dot(w_low, back)).reshape(2, 2, 8, 2048)
        first = pl.ds(pairs[chunk] * 2, 2)
        part[first] = routed
        lsend[first] = routed.astype(BF16)

    def hand(d):
        block = lsend.at[lines[d // 2], halves[d % 2]]
        return remote(block, lrecv.at[d], ls.at[d], lr.at[d], line(d))

    take(0)
    for d in (1, 3, 2):
        hand(d).start()
    take(1)
    for d in (5, 7, 4, 6):
        hand(d).start()
    for d in (1, 2, 3):
        remote(share_send.at[lines[d]], share_recv.at[d], bs.at[d], br.at[d], other).wait()
    for n in range(4):
        both = share_out[n, zl]
        for d in range(1, 4):
            both = both + share_recv[d, n].astype(F32)
        share_sum[n] = both
        share_x[n] = both.astype(BF16)
    for i in (2, 1, 3):
        peer = lax.rem(x + i, 4)
        remote(
            share_x.at[peer], share_back.at[i], us.at[i], ur.at[i], dev(peer, y, zl, zh, c)
        ).start()
    result = hidden_s[zh] + part[zl, zh] + share_sum[x]
    for d in (2, 1, 3, 4, 6, 5, 7):
        hand(d).wait()
        result = result + lrecv[d].astype(F32)
    for i in (1, 3, 2):
        remote(share_x.at[lax.rem(x + i, 4)], share_back.at[i], us.at[i], ur.at[i], other).wait()
        result = result + share_back[i].astype(F32)
    out_ref[...] = result.astype(BF16)


def layer(vmem_args, more, weights):
    gate, up, down, sgate, sup, sdown = weights
    width = gate.shape[1]
    return pl.pallas_call(
        layer_kernel,
        name="layer",
        out_shape=jax.ShapeDtypeStruct((8, width), BF16),
        in_specs=[vmem_spec()] * len(vmem_args) + [hbm_spec()] * (len(more) + 6),
        out_specs=vmem_spec(),
        scratch_shapes=[VMEM(m.shape, BF16) for m in more]
        + [
            VMEM((GAP + gate.shape[0], width), BF16),
            VMEM(down.shape, BF16),
            VMEM((SGAP + sgate.shape[0], width), BF16),
            VMEM(sdown.shape, BF16),
            VMEM((4, 4, REQ, MSG), BF16),
            VMEM((3, REQ, MSG), BF16),
            VMEM((3, REQ, MSG), BF16),
            VMEM((2, 64, 128), BF16),
            VMEM((2, 64, width // 2), BF16),
            VMEM((2, 64, width // 2), BF16),
            VMEM((2, 4, 16, width // 2), F32),
            VMEM((2, 4, 16, width // 2), BF16),
            VMEM((2, 4, 16, width // 2), BF16),
            VMEM((2, 16, width // 2), BF16),
            VMEM((8, 2, 16, width // 2), BF16),
            VMEM((2, 8, width), F32),
            VMEM((4, 16, width), BF16),
            VMEM((2, 16, 8, width), BF16),
            VMEM((2, 2, 16, 8, width), BF16),
            VMEM((2, 128, width), F32),
            VMEM((2, 128, width), BF16),
            VMEM((2, 128, width), BF16),
            VMEM((2, 16, 8, width), BF16),
            VMEM((2, 16, 8, width), BF16),
            VMEM((4, 4, 8, width), BF16),
            VMEM((4, 4, 8, width), F32),
            VMEM((4, 4, 8, width), BF16),
            VMEM((4, 4, 8, width), BF16),
            VMEM((4, 8, width), F32),
            VMEM((4, 8, width), BF16),
            VMEM((4, 8, width), BF16),
            VMEM((4, 2, 8, width), F32),
            VMEM((4, 2, 8, width), BF16),
            VMEM((8, 8, width), BF16),
            DMA((12,)),
            DMA((4, 4)),
            DMA((4, 4)),
            DMA((3,)),
            DMA((3,)),
            DMA((2,)),
            DMA((2,)),
            DMA((2, 4)),
            DMA((2, 4)),
            DMA((8, 2)),
            DMA((8, 2)),
            DMA((2, 16)),
            DMA((2, 16)),
            DMA((2, 16)),
            DMA((2, 16)),
            DMA((2,)),
            DMA((2,)),
            DMA((2, 16)),
            DMA((2, 16)),
            DMA((4, 4)),
            DMA((4, 4)),
            DMA((4,)),
            DMA((4,)),
            DMA((4,)),
            DMA((4,)),
            DMA((8,)),
            DMA((8,)),
        ],
        compiler_params=pltpu.CompilerParams(
            collective_id=1, has_side_effects=True, vmem_limit_bytes=44 << 20
        ),
    )(*vmem_args, *map(stay, more), *map(stay, weights))


def on_device(
    query_nope,
    query_rope,
    absorb_weight,
    value_weight,
    output_weight,
    cache_latent,
    cache_rope,
    node_length,
    new_latent,
    new_rope,
    parent_node,
    leaf_node,
    residual,
    norm_gain,
    router_weight,
    routes,
    expert_gate,
    expert_up,
    expert_down,
    shared_gate,
    shared_up,
    shared_down,
):
    q_all, routes8, pick, place, lat, krope, absorb, value = gather(
        query_nope[:, 0, :],
        query_rope[:, 0, :].T,
        routes,
        leaf_node,
        parent_node,
        cache_latent,
        jnp.swapaxes(cache_rope, 1, 2),
        absorb_weight[0],
        value_weight[0],
    )
    msg = attend(
        node_length, q_all.reshape(16 * REQ, -1), pick, place, absorb, value, lat, krope
    )
    return layer(
        (msg.reshape(16, REQ, MSG), q_all, routes8, absorb, value),
        (norm_gain, new_latent, new_rope.T, residual, router_weight.T, output_weight),
        (
            expert_gate[0].T,
            expert_up[0].T,
            expert_down[0],
            shared_gate.T,
            shared_up.T,
            shared_down,
        ),
    )


def solution(mesh):
    in_specs = (
        P("group", "expert", None),
        P("group", "expert", None),
        P("expert", None, None),
        P("expert", None, None),
        P("expert", None),
        P("group", None, None),
        P("group", None, None),
        P("group"),
        P("group", None),
        P("group", None),
        P(),
        P(),
        P(("group", "expert"), None),
        P(),
        P(),
        P(("group", "expert"), None),
        P(("group", "expert"), None, None),
        P(("group", "expert"), None, None),
        P(("group", "expert"), None, None),
        P(None, "group"),
        P(None, "group"),
        P("group", None),
    )
    out_specs = P(("group", "expert"), None)
    return jax.shard_map(
        on_device, mesh=mesh, in_specs=in_specs, out_specs=out_specs, check_vma=False
    )
```

```python
import jax
import jax.numpy as jnp
from jax import lax
from jax.experimental import pallas as pl
from jax.experimental.pallas import tpu as pltpu
from jax.sharding import PartitionSpec as P

ROUTE_SCALE = 2.446
NEGATIVE = -1e30
EPSILON = 1e-06
MESH = pl.DeviceIdType.MESH
F32 = jnp.float32
BF16 = jnp.bfloat16
VMEM = pltpu.VMEM
DMA = pltpu.SemaphoreType.DMA

REQ = 16
QT = 8
MSG = 1024 + 128


def vmem_spec():
    return pl.BlockSpec(memory_space=pltpu.VMEM)


def hbm_spec():
    return pl.BlockSpec(memory_space=pltpu.HBM)


def stay(x):
    return pltpu.with_memory_space_constraint(x, pltpu.HBM)


def start_loads(pairs, sem):
    loads = [pltpu.make_async_copy(src, dst, sem.at[i]) for i, (src, dst) in enumerate(pairs)]
    for load in loads:
        load.start()
    return loads


def coords():
    g = lax.axis_index("group")
    e = lax.axis_index("expert")
    zl, x = g // 4, g % 4
    y, zh, c = e // 4, (e % 4) // 2, e % 2
    return g, e, x, y, zl, zh, c


def dev(x, y, zl, zh, c):
    return (zl * 4 + x, y * 4 + zh * 2 + c)


def remote(src, dst, send, recv, device):
    return pltpu.make_async_remote_copy(
        src_ref=src,
        dst_ref=dst,
        send_sem=send,
        recv_sem=recv,
        device_id=device,
        device_id_type=MESH,
    )


def greet(barrier, device):
    pl.semaphore_signal(barrier, inc=1, device_id=device, device_id_type=MESH)


def dot(a, b):
    return jnp.dot(a, b, preferred_element_type=F32)


def eye_column(row):
    n = row.shape[1]
    same = lax.broadcasted_iota(jnp.int32, (n, n), 0) == lax.broadcasted_iota(jnp.int32, (n, n), 1)
    return jnp.sum(jnp.where(same, row, 0), axis=1, keepdims=True)


def flag(condition):
    return jnp.where(condition, 1.0, 0.0).astype(BF16)


def dot_nt(a, b):
    return lax.dot_general(a, b, (((1,), (1,)), ((), ())), preferred_element_type=F32)


def on_path(leaf_row, parent_col, node):
    nodes = parent_col.shape[0]
    ids = lax.broadcasted_iota(jnp.int32, (nodes, leaf_row.shape[1]), 0)
    mid = jnp.sum(jnp.where(leaf_row == ids, parent_col, 0), axis=0, keepdims=True)
    top = jnp.sum(jnp.where(mid == ids, parent_col, 0), axis=0, keepdims=True)
    return (leaf_row == node) | (mid == node) | (top == node)


def gather_kernel(
    nope_hbm,
    rope_hbm,
    routes_hbm,
    leaf_hbm,
    parent_hbm,
    lat_hbm,
    krope_hbm,
    absorb_hbm,
    value_hbm,
    qall,
    routes8,
    pick_ref,
    place_ref,
    lat_ref,
    krope_ref,
    absorb_ref,
    value_ref,
    nope_v,
    rope_v,
    routes_v,
    leaf_v,
    parent_v,
    mine,
    wsem,
    zq,
    zqr,
    xq,
    xqr,
    rs,
    rr,
):
    g, e, x, y, zl, zh, c = coords()
    loads = start_loads(
        [
            (nope_hbm, nope_v),
            (rope_hbm, rope_v),
            (routes_hbm, routes_v),
            (leaf_hbm, leaf_v),
            (parent_hbm, parent_v),
            (lat_hbm, lat_ref),
            (krope_hbm, krope_ref),
            (absorb_hbm, absorb_ref),
            (value_hbm, value_ref),
        ],
        wsem,
    )
    barrier = pltpu.get_barrier_semaphore()
    partner = dev(x, y, zl, 1 - zh, c)
    me = zl * 2 + zh
    for i in range(1, 4):
        greet(barrier, dev(lax.rem(x + i, 4), y, zl, zh, c))
        greet(barrier, dev(x, y, lax.rem(zl + i, 4), zh, c))
    for k in (1, 3, 5, 7):
        s = lax.rem(me + k, 8)
        greet(barrier, dev(x, y, s // 2, s % 2, c))

    rows = REQ * QT
    di = lax.broadcasted_iota(jnp.int32, (rows, rows), 0)
    si = lax.broadcasted_iota(jnp.int32, (rows, rows), 1)
    perm = flag(si == (di % REQ) * QT + di // REQ)
    for load in loads[:3]:
        load.wait()
    nope = dot(perm, nope_v[...]).astype(BF16)
    rope = dot_nt(perm, rope_v[...]).astype(BF16)
    qall[g] = jnp.concatenate(
        [nope[j * REQ : (j + 1) * REQ] for j in range(QT)]
        + [rope[j * REQ : (j + 1) * REQ] for j in range(QT)],
        axis=1,
    )
    mine[...] = jnp.zeros_like(mine)
    mine[:, 0 : routes_v.shape[1]] = routes_v[...]
    routes8[me] = mine[...]
    pl.semaphore_wait(barrier, 10)

    own = qall.at[g]
    for i in (1, 3, 2):
        remote(own, own, zq.at[i], zqr.at[i], dev(x, y, lax.rem(zl + i, 4), zh, c)).start()
    for k in (2, 1, 3):
        remote(own, own, xq.at[0, k], xqr.at[0, k], dev(lax.rem(x + k, 4), y, zl, zh, c)).start()
    for k in range(1, 8):
        s = lax.rem(me + k, 8)
        remote(mine, routes8.at[me], rs.at[k], rr.at[k], dev(x, y, s // 2, s % 2, c)).start()

    def pass_on(i):
        block = qall.at[lax.rem(zl - i + 4, 4) * 4 + x]
        remote(own, block, zq.at[i], zqr.at[i], partner).wait()
        for k in (2, 1, 3):
            remote(
                block, block, xq.at[i, k], xqr.at[i, k], dev(lax.rem(x + k, 4), y, zl, zh, c)
            ).start()

    pass_on(1)
    pass_on(3)
    pass_on(2)

    for load in loads[3:5]:
        load.wait()
    slots, _, requests = pick_ref.shape
    ids_0 = lax.broadcasted_iota(jnp.int32, (requests, requests), 0)
    ids_1 = lax.broadcasted_iota(jnp.int32, (requests, requests), 1)
    earlier = flag(ids_0 < ids_1)
    parent_col = eye_column(parent_v[...])
    for slot in range(slots):
        on_row = on_path(leaf_v[...], parent_col, g * slots + slot)
        row_f = jnp.where(on_row, 1.0, 0.0)
        rank_row = dot(jnp.broadcast_to(row_f, (8, requests)).astype(BF16), earlier)[0:1]
        rank_row = jnp.where(on_row, rank_row, -1.0)
        pick_ref[slot] = flag(rank_row.astype(jnp.int32) == ids_0)
        place_ref[slot] = flag(eye_column(rank_row).astype(jnp.int32) == ids_1)

    for load in loads[5:]:
        load.wait()
    for k in range(1, 8):
        s = lax.rem(me - k + 8, 8)
        remote(mine, routes8.at[s], rs.at[k], rr.at[k], partner).wait()
    for i in range(4):
        for k in (1, 3, 2):
            block = qall.at[lax.rem(zl - i + 4, 4) * 4 + lax.rem(x - k + 4, 4)]
            remote(own, block, xq.at[i, k], xqr.at[i, k], partner).wait()


def gather(nope, rope_t, routes, leaf, parent, lat, krope_t, absorb, value):
    requests = leaf.shape[0]
    slots = lat.shape[0]
    return pl.pallas_call(
        gather_kernel,
        name="gather_queries",
        out_shape=(
            jax.ShapeDtypeStruct((16, REQ, QT * 192), BF16),
            jax.ShapeDtypeStruct((8, 8, 128), jnp.int32),
            jax.ShapeDtypeStruct((slots, requests, requests), BF16),
            jax.ShapeDtypeStruct((slots, requests, requests), BF16),
            jax.ShapeDtypeStruct(lat.shape, BF16),
            jax.ShapeDtypeStruct(krope_t.shape, BF16),
            jax.ShapeDtypeStruct(absorb.shape, BF16),
            jax.ShapeDtypeStruct(value.shape, BF16),
        ),
        in_specs=[hbm_spec()] * 9,
        out_specs=(vmem_spec(),) * 8,
        scratch_shapes=[
            VMEM(nope.shape, BF16),
            VMEM(rope_t.shape, BF16),
            VMEM(routes.shape, jnp.int32),
            VMEM((1, requests), jnp.int32),
            VMEM((1, parent.shape[0]), jnp.int32),
            VMEM((8, 128), jnp.int32),
            DMA((9,)),
            DMA((4,)),
            DMA((4,)),
            DMA((4, 4)),
            DMA((4, 4)),
            DMA((8,)),
            DMA((8,)),
        ],
        compiler_params=pltpu.CompilerParams(
            collective_id=0, has_side_effects=True, vmem_limit_bytes=24 << 20
        ),
    )(
        *map(
            stay,
            (nope, rope_t, routes, leaf[None, :], parent[None, :], lat, krope_t, absorb, value),
        )
    )


TILE = 32
KEYS = 256


def split3(v):
    hi = v.astype(BF16)
    rest = v - hi.astype(F32)
    mid = rest.astype(BF16)
    low = (rest - mid.astype(F32)).astype(BF16)
    return hi.astype(F32), mid.astype(F32), low.astype(F32)


def pack_logs(logs):
    hi, mid, low = split3(logs)
    return hi + pltpu.roll(mid, 8, 1) + pltpu.roll(low, 16, 1)


def join_logs(tail):
    return tail + pltpu.roll(tail, 120, 1) + pltpu.roll(tail, 112, 1)


def attn_kernel(
    q_ref,
    pick_ref,
    place_ref,
    absorb_ref,
    value_ref,
    lat_ref,
    rope_ref,
    len_hbm,
    out_ref,
    len_ref,
    picked,
    done,
    wsem,
):
    (load,) = start_loads([(len_hbm, len_ref)], wsem)
    requests = q_ref.shape[0]
    slots, most = lat_ref.shape[0], lat_ref.shape[1]
    scaling = float(128 + 64) ** (-0.5)
    done[...] = jnp.zeros_like(done)
    lane = lax.broadcasted_iota(jnp.int32, (TILE, 128), 1)
    counts = []
    for slot in range(slots):
        picked[slot] = dot(pick_ref[slot], q_ref[...]).astype(BF16)
        counts.append(jnp.sum(pick_ref[slot].astype(F32)).astype(jnp.int32))
    load.wait()

    for slot in range(slots):
        length = len_ref[slot]

        def tile(keys, step, carry):
            here = pl.ds(pl.multiple_of(step * TILE, TILE), TILE)
            qt = picked[slot, here]
            nope = jnp.concatenate([qt[:, j * 128 : j * 128 + 128] for j in range(QT)], axis=0)
            rot = jnp.concatenate(
                [qt[:, 1024 + j * 64 : 1024 + j * 64 + 64] for j in range(QT)], axis=0
            )
            lat = dot(nope, absorb_ref[...]).astype(BF16)
            scores = dot_nt(lat, lat_ref[slot, :keys]) + dot(rot, rope_ref[slot, :, :keys])
            positions = lax.broadcasted_iota(jnp.int32, (1, keys), 1)
            scores = jnp.where(positions < length, scores * scaling, NEGATIVE)
            top = jnp.max(scores, axis=1, keepdims=True)
            weights = jnp.exp(scores - top).astype(BF16)
            total = jnp.sum(weights.astype(F32), axis=1, keepdims=True)
            summed = dot(weights, lat_ref[slot, :keys])
            attended = (summed / total).astype(BF16)
            valued = dot(attended, value_ref[...]).astype(BF16)
            log_sum = top + jnp.log(total)
            logs = jnp.zeros((TILE, 128), F32)
            for j in range(QT):
                logs = jnp.where(lane == j, log_sum[j * TILE : (j + 1) * TILE], logs)
            tail = jnp.where((lane >= 24) & (lane < 32), 1.0, pack_logs(logs))
            done[slot, here] = jnp.concatenate(
                [valued[j * TILE : (j + 1) * TILE] for j in range(QT)] + [tail.astype(BF16)],
                axis=1,
            )
            return carry

        tiles = (counts[slot] + TILE - 1) // TILE
        for keys in range(KEYS, most + 1, KEYS):

            @pl.when((length > keys - KEYS) & (length <= keys))
            def _():
                lax.fori_loop(0, tiles, lambda step, carry: tile(keys, step, carry), 0)

    acc = [dot(place_ref[s], done[s]) for s in range(slots)]
    tails = [a[:, 1024:] for a in acc]
    logs = [jnp.where(pltpu.roll(t, 104, 1) > 0.5, join_logs(t), NEGATIVE) for t in tails]
    top = logs[0]
    for s in range(1, slots):
        top = jnp.maximum(top, logs[s])
    shares = [jnp.exp(v - top) for v in logs]
    total = shares[0]
    for s in range(1, slots):
        total = total + shares[s]
    shares = [v / total for v in shares]
    for j in range(QT):
        out = 0.0
        for s in range(slots):
            out = out + shares[s][:, j : j + 1] * acc[s][:, j * 128 : j * 128 + 128]
        out_ref[:, j * 128 : j * 128 + 128] = out.astype(BF16)
    lanes = lax.broadcasted_iota(jnp.int32, (requests, 128), 1)
    log_sum = jnp.where(lanes < QT, top + jnp.log(total), 0.0)
    out_ref[:, 1024:] = pack_logs(log_sum).astype(BF16)


def attend(node_length, q_all, pick, place, absorb, value, lat, rope_t):
    requests = q_all.shape[0]
    slots = lat.shape[0]
    return pl.pallas_call(
        attn_kernel,
        name="attend_nodes",
        out_shape=jax.ShapeDtypeStruct((requests, MSG), BF16),
        in_specs=[vmem_spec()] * 7 + [hbm_spec()],
        out_specs=vmem_spec(),
        scratch_shapes=[
            pltpu.SMEM(node_length.shape, jnp.int32),
            VMEM((slots, requests, q_all.shape[1]), BF16),
            VMEM((slots, requests, MSG), BF16),
            DMA((1,)),
        ],
        compiler_params=pltpu.CompilerParams(vmem_limit_bytes=32 << 20),
    )(q_all, pick, place, absorb, value, lat, rope_t, stay(node_length))


OFFSETS = sorted(
    [(i, j) for i in range(4) for j in range(4) if i or j],
    key=lambda o: -min(o[0], 4 - o[0]) - min(o[1], 4 - o[1]),
)

GAP = 384
SGAP = 256


def layer_kernel(
    msg_ref,
    q_ref,
    routes_ref,
    absorb_ref,
    value_ref,
    gain_hbm,
    newlat_hbm,
    newrope_hbm,
    resid_hbm,
    router_hbm,
    outw_hbm,
    gate_hbm,
    up_hbm,
    down_hbm,
    sgate_hbm,
    sup_hbm,
    sdown_hbm,
    out_ref,
    gain_ref,
    newlat_ref,
    newrope_ref,
    resid_ref,
    router_ref,
    outw_ref,
    gate_up,
    down_w,
    sgate_up,
    sdown_w,
    got,
    got_z,
    blended,
    valued_s,
    csend,
    crecv,
    acc,
    ysend,
    yrecv,
    zsend,
    zrecv,
    hidden_s,
    normed,
    packed,
    arrived,
    own_out,
    cross_send,
    cross_recv,
    ret_send,
    ret_recv,
    share_in,
    share_out,
    share_near,
    near_recv,
    share_send,
    share_recv,
    share_sum,
    share_x,
    share_back,
    part,
    lsend,
    lrecv,
    wsem,
    ms,
    mr,
    gs,
    gr,
    cs,
    cr,
    ys,
    yr,
    ns,
    nr,
    ds,
    dr,
    fs,
    fr,
    os_,
    or_,
    rs,
    rr,
    xs,
    xr,
    bs,
    br,
    us,
    ur,
    ls,
    lr,
):
    g, e, x, y, zl, zh, c = coords()
    mine = x * 4 + y
    ff = gate_hbm.shape[0]
    sff = sgate_hbm.shape[0]
    barrier = pltpu.get_barrier_semaphore()

    def source(i):
        return lax.rem(x - i // 4 + 4, 4) * 4 + lax.rem(y - i % 4 + 4, 4)

    other = dev(x, y, zl, zh, 1 - c)
    partner = dev(x, y, zl, 1 - zh, c)
    greet(barrier, other)
    greet(barrier, partner)
    for i in range(4):
        for k in range(1, 4):
            greet(barrier, dev(lax.rem(x + i, 4), lax.rem(y + k, 4), zl, zh, c))
    lines = (zl, zl + 1 - 2 * (zl % 2), zl + 2 - 4 * (zl // 2), 3 - zl)
    halves = (zh, 1 - zh)

    def line(d):
        return dev(x, y, lines[d // 2], halves[d % 2], c)

    for d in range(2, 8):
        greet(barrier, line(d))
    for i in range(1, 4):
        greet(barrier, dev(lax.rem(x + i, 4), y, zl, zh, c))
    loads = start_loads(
        [
            (gain_hbm, gain_ref),
            (newlat_hbm, newlat_ref),
            (newrope_hbm, newrope_ref),
            (resid_hbm, resid_ref),
            (router_hbm, router_ref),
            (outw_hbm, outw_ref),
            (gate_hbm, gate_up.at[pl.ds(0, ff)]),
            (up_hbm, gate_up.at[pl.ds(GAP, ff)]),
            (down_hbm, down_w),
            (sgate_hbm, sgate_up.at[pl.ds(0, sff)]),
            (sup_hbm, sgate_up.at[pl.ds(SGAP, sff)]),
            (sdown_hbm, sdown_w),
        ],
        wsem,
    )
    gate_up[ff:GAP] = jnp.zeros((GAP - ff, gate_up.shape[1]), BF16)
    sgate_up[sff:SGAP] = jnp.zeros((SGAP - sff, sgate_up.shape[1]), BF16)

    pl.semaphore_wait(barrier, 23)

    homes = (lines[2], lines[3], lines[1], zl)
    for n in range(4):
        for i in (2, 1, 3):
            peer = lax.rem(x + i, 4)
            remote(
                msg_ref.at[homes[n] * 4 + peer],
                got.at[n, i],
                ms.at[n, i],
                mr.at[n, i],
                dev(peer, y, zl, zh, c),
            ).start()

    scaling = float(128 + 64) ** (-0.5)
    for load in loads[:6]:
        load.wait()
    q = q_ref[g]
    nope = jnp.concatenate([q[:, j * 128 : j * 128 + 128] for j in range(QT)], axis=0)
    rot = jnp.concatenate([q[:, 1024 + j * 64 : 1024 + j * 64 + 64] for j in range(QT)], axis=0)
    lat = dot(nope, absorb_ref[...]).astype(BF16)
    scores = dot_nt(lat, newlat_ref[...]) + dot(rot, newrope_ref[...])
    rows = REQ * QT
    qi = lax.broadcasted_iota(jnp.int32, (rows, rows), 0)
    ki = lax.broadcasted_iota(jnp.int32, (rows, rows), 1)
    usable = ((qi % REQ) == (ki // QT)) & ((ki % QT) <= (qi // REQ))
    scores = jnp.where(usable, scores * scaling, NEGATIVE)
    top = jnp.max(scores, axis=1, keepdims=True)
    weights = jnp.where(usable, jnp.exp(scores - top), 0.0).astype(BF16)
    total = jnp.sum(weights.astype(F32), axis=1, keepdims=True)
    summed = dot(weights, newlat_ref[...]) / total
    new_valued = dot(summed.astype(BF16), value_ref[...])
    new_log = top + jnp.log(total)

    def blend(parts, more=None):
        logs = [join_logs(p[:, 1024:].astype(F32)) for p in parts]
        if more is not None:
            logs.append(more[1])
        peak = logs[0]
        for v in logs[1:]:
            peak = jnp.maximum(peak, v)
        shares = [jnp.exp(v - peak) for v in logs]
        whole = shares[0]
        for v in shares[1:]:
            whole = whole + v
        shares = [v / whole for v in shares]
        values = []
        for j in range(QT):
            value = 0.0
            for p, share in zip(parts, shares):
                value = value + share[:, j : j + 1] * p[:, j * 128 : j * 128 + 128].astype(F32)
            if more is not None:
                value = value + shares[-1][:, j : j + 1] * more[0][j * REQ : (j + 1) * REQ]
            values.append(value.astype(BF16))
        return values, peak + jnp.log(whole)

    def along_x(n):
        for i in (1, 3, 2):
            src = msg_ref.at[homes[n] * 4 + lax.rem(x + i, 4)]
            remote(src, got.at[n, i], ms.at[n, i], mr.at[n, i], other).wait()
        return [msg_ref[homes[n] * 4 + x]] + [got[n, i] for i in range(1, 4)]

    lane = lax.broadcasted_iota(jnp.int32, (REQ, 128), 1)

    def along_z(n):
        return remote(
            blended.at[n], got_z.at[n], gs.at[n], gr.at[n], dev(x, y, homes[n], zh, c)
        )

    for n in range(3):
        values, log_sum = blend(along_x(n))
        tail = pack_logs(jnp.where(lane < QT, log_sum, 0.0)).astype(BF16)
        blended[n] = jnp.concatenate(values + [tail], axis=1)
        along_z(n).start()

    experts = router_ref.shape[0]
    pairs = (zl // 2, 1 - zl // 2)
    picks, masks = [], []
    for q_ in range(2):
        routes = routes_ref[pl.ds(pairs[q_] * 4, 4)].reshape(32, 128)
        ids = lax.broadcasted_iota(jnp.int32, (32, experts), 1)
        chosen = jnp.zeros((32, experts), F32)
        for k in range(6):
            chosen = jnp.where(routes[:, k : k + 1] == ids, 1.0, chosen)
        ti = lax.broadcasted_iota(jnp.int32, (32, 32), 0)
        tj = lax.broadcasted_iota(jnp.int32, (32, 32), 1)
        before = flag((ti // 8 == tj // 8) & (tj < ti))
        rank = jnp.where(chosen > 0.0, dot(before, chosen.astype(BF16)), -1.0)
        col = lax.broadcasted_iota(jnp.int32, (experts, 128), 1)
        spread = flag(lax.broadcasted_iota(jnp.int32, (experts, 128), 0) == zl * 16 + col // 8)
        spread_rank = dot(rank.astype(BF16), spread)
        ct = lax.broadcasted_iota(jnp.int32, (32, 128), 1)
        rt = lax.broadcasted_iota(jnp.int32, (32, 128), 0)
        pick = jnp.where(
            (spread_rank == (ct % 2).astype(F32)) & (rt // 8 == (ct // 2) % 4), 1.0, 0.0
        )
        picks.append(pick)
        masks.append(chosen)

    here = along_x(3)
    logs = jnp.zeros((REQ, 128), F32)
    for j in range(QT):
        logs = jnp.where(lane == j, new_log[j * REQ : (j + 1) * REQ], logs)
    for n in (2, 0, 1):
        along_z(n).wait()
    pieces, _ = blend(here + [got_z[n] for n in range(3)], (new_valued, logs))
    valued = jnp.concatenate(pieces, axis=0)
    di = lax.broadcasted_iota(jnp.int32, (rows, rows), 0)
    si = lax.broadcasted_iota(jnp.int32, (rows, rows), 1)
    req = ((di % 64) // 16) * 4 + ((di % 16) // 8) * 2 + di // 64
    perm = flag(si == (di % 8) * REQ + req)
    valued_s[...] = dot(perm, valued).astype(BF16).reshape(2, 64, 128)
    half = outw_ref.shape[1] // 2
    cols = [pl.ds(h * half, half) for h in range(2)]
    own_8 = lax.broadcasted_iota(jnp.int32, (16, 1), 0) // 8 == zh
    for h in range(2):
        csend[h] = dot(valued_s[1 - c], outw_ref[:, cols[h]]).astype(BF16)
        remote(csend.at[h], crecv.at[h], cs.at[h], cr.at[h], other).start()
    own = [dot(valued_s[c], outw_ref[:, cols[h]]) for h in range(2)]
    for h in range(2):
        remote(csend.at[h], crecv.at[h], cs.at[h], cr.at[h], other).wait()
        acc[h] = (own[h] + crecv[h].astype(F32)).reshape(4, 16, half)
        ysend[h] = acc[h].astype(BF16)
        for i in (2, 1, 3):
            peer = lax.rem(y + i, 4)
            remote(
                ysend.at[h, peer],
                yrecv.at[h, i],
                ys.at[h, i],
                yr.at[h, i],
                dev(x, peer, zl, zh, c),
            ).start()
    sums = []
    for h in range(2):
        row = acc[h, y]
        for i in (1, 3, 2):
            remote(ysend.at[h, 0], yrecv.at[h, i], ys.at[h, i], yr.at[h, i], other).wait()
            row = row + yrecv[h, i].astype(F32)
        resid = resid_ref[:, cols[h]].astype(F32)
        row = row + jnp.where(own_8, jnp.concatenate([resid, resid], axis=0), 0.0)
        zsend[h] = row.astype(BF16)
        sums.append(row)
        for d in (1, 3, 2):
            remote(zsend.at[h], zrecv.at[d, h], ns.at[d, h], nr.at[d, h], line(d)).start()
    for h in range(2):
        for d in (5, 7, 4, 6):
            remote(zsend.at[h], zrecv.at[d, h], ns.at[d, h], nr.at[d, h], line(d)).start()
    total_row = jnp.concatenate(sums, axis=1)

    def column(d):
        for h in range(2):
            remote(zsend.at[h], zrecv.at[d, h], ns.at[d, h], nr.at[d, h], other).wait()
        return jnp.concatenate([zrecv[d, 0], zrecv[d, 1]], axis=1).astype(F32)

    gain = gain_ref[...].reshape(1, gain_ref.shape[0]).astype(F32)

    def norm(hidden):
        square = jnp.mean(hidden * hidden, axis=1, keepdims=True)
        return (hidden * lax.rsqrt(square + EPSILON) * gain).astype(BF16)

    hidden = total_row + column(1)
    hidden_s[...] = hidden.reshape(2, 8, 2048)
    normed[zl] = norm(hidden)
    share_in[x, zl] = normed[zl].reshape(2, 8, 2048)[0]

    @pl.when(zh == 1)
    def _():
        share_in[x, zl] = normed[zl].reshape(2, 8, 2048)[1]

    for i in (2, 1, 3):
        block = share_in.at[x, zl]
        peer = dev(lax.rem(x + i, 4), y, zl, zh, c)
        remote(block, block, xs.at[0, i], xr.at[0, i], peer).start()

    def pack(chunk):
        tokens = normed[pl.ds(pairs[chunk] * 2, 2)].reshape(32, 2048)
        packed[chunk] = (
            lax.dot_general(
                picks[chunk].astype(BF16),
                tokens,
                (((0,), (0,)), ((), ())),
                preferred_element_type=F32,
            )
            .astype(BF16)
            .reshape(16, 8, 2048)
        )

        for dx, dy in OFFSETS:
            to_x, to_y = lax.rem(x + dx, 4), lax.rem(y + dy, 4)
            remote(
                packed.at[chunk, to_x * 4 + to_y],
                arrived.at[chunk, c, mine],
                ds.at[chunk, dx * 4 + dy],
                dr.at[chunk, dx * 4 + dy],
                dev(to_x, to_y, zl, zh, c),
            ).start()
        arrived[chunk, c, mine] = packed[chunk, mine]
        here = arrived.at[chunk, c, mine]
        remote(here, here, fs.at[chunk, 0], fr.at[chunk, 0], other).start()

    def weigh(chunk):
        tokens = normed[pl.ds(pairs[chunk] * 2, 2)].reshape(32, 2048)
        logits = dot_nt(tokens, router_ref[...])
        sigma = jax.nn.sigmoid(logits) * masks[chunk]
        route_w = ROUTE_SCALE * sigma / jnp.sum(sigma, axis=1, keepdims=True)
        col = lax.broadcasted_iota(jnp.int32, (experts, 128), 1)
        spread = flag(lax.broadcasted_iota(jnp.int32, (experts, 128), 0) == zl * 16 + col // 8)
        w_hi, w_mid, w_low = split3(route_w)
        return (
            dot(w_hi.astype(BF16), spread)
            + dot(w_mid.astype(BF16), spread)
            + dot(w_low.astype(BF16), spread)
        ) * picks[chunk]

    normed[lines[1]] = norm(column(2) + column(3))
    pack(0)
    normed[lines[2]] = norm(column(4) + column(5))
    normed[lines[3]] = norm(column(6) + column(7))
    pack(1)
    for d in range(1, 4):
        both = normed[lines[d]].reshape(2, 8, 2048)
        share_in[x, lines[d]] = jnp.where(zh == 0, both[0], both[1])
    for i in (1, 3, 2):
        block = share_in.at[lax.rem(x - i + 4, 4), zl]
        remote(share_in.at[x, zl], block, xs.at[0, i], xr.at[0, i], other).wait()
        for d in range(1, 4):
            remote(block, block, xs.at[d, i], xr.at[d, i], line(2 * d)).start()

    def forward(chunk):
        def step(i, carry):
            src = source(i)
            block = arrived.at[chunk, c, src]
            remote(packed.at[chunk, src], block, ds.at[chunk, i], dr.at[chunk, i], other).wait()
            remote(block, block, fs.at[chunk, i], fr.at[chunk, i], other).start()
            return carry

        lax.fori_loop(1, 16, step, 0)

    def crossed(chunk):
        def step(i, carry):
            src = source(i)
            block = arrived.at[chunk, c, src]
            remote(
                block, arrived.at[chunk, 1 - c, src], fs.at[chunk, i], fr.at[chunk, i], other
            ).wait()
            return carry

        lax.fori_loop(0, 16, step, 0)

    def ffn(rows_in, both_w, gap, units, down):
        val = dot_nt(rows_in, both_w[...])
        hidden = (jax.nn.silu(val[:, :units]) * val[:, gap : gap + units]).astype(BF16)
        return dot(hidden, down[...])

    def routed_ffn(chunk):
        out = ffn(arrived[chunk].reshape(256, 2048), gate_up, GAP, ff, down_w)
        first, second = out[:128], out[128:]
        own_out[chunk] = jnp.where(c == 0, first, second)
        cross_send[chunk] = jnp.where(c == 0, second, first).astype(BF16)
        remote(
            cross_send.at[chunk], cross_recv.at[chunk], os_.at[chunk], or_.at[chunk], other
        ).start()

    def give(chunk):
        remote(
            cross_send.at[chunk], cross_recv.at[chunk], os_.at[chunk], or_.at[chunk], other
        ).wait()
        ret_send[chunk] = (
            (own_out[chunk] + cross_recv[chunk].astype(F32)).astype(BF16).reshape(16, 8, 2048)
        )

        for dx, dy in OFFSETS:
            to_x, to_y = lax.rem(x + dx, 4), lax.rem(y + dy, 4)
            remote(
                ret_send.at[chunk, to_x * 4 + to_y],
                ret_recv.at[chunk, mine],
                rs.at[chunk, dx * 4 + dy],
                rr.at[chunk, dx * 4 + dy],
                dev(to_x, to_y, zl, zh, c),
            ).start()
        ret_recv[chunk, mine] = ret_send[chunk, mine]

    forward(0)
    for load in loads[6:9]:
        load.wait()
    crossed(0)
    routed_ffn(0)
    give(0)
    forward(1)
    crossed(1)
    routed_ffn(1)

    give(1)

    for load in loads[9:]:
        load.wait()
    for i in (1, 3, 2):
        src = lax.rem(x - i + 4, 4)
        for d in range(1, 4):
            remote(
                share_in.at[src, zl], share_in.at[src, lines[d]], xs.at[d, i], xr.at[d, i], other
            ).wait()
    shared = ffn(share_in[...].reshape(128, 2048), sgate_up, SGAP, sff, sdown_w)
    share_out[...] = shared.reshape(4, 4, 8, 2048)
    for n in range(4):
        share_near[n] = share_out[n, lines[1]].astype(BF16)
        share_send[n] = share_out[n, pl.ds(pairs[1] * 2, 2)].astype(BF16)
    remote(share_near, near_recv, bs.at[0], br.at[0], line(2)).start()
    for i in (2, 1, 3):
        peer = lax.rem(x + i, 4)
        remote(
            share_send.at[peer], share_recv.at[i], bs.at[i], br.at[i], dev(peer, y, zl, zh, c)
        ).start()

    combines = [weigh(chunk) for chunk in range(2)]

    is_own = lax.broadcasted_iota(jnp.int32, (2, 2, 8, 2048), 1) == zh

    def take(chunk):
        def step(i, carry):
            src = source(i)
            remote(
                ret_send.at[chunk, src],
                ret_recv.at[chunk, src],
                rs.at[chunk, i],
                rr.at[chunk, i],
                other,
            ).wait()
            return carry

        lax.fori_loop(1, 16, step, 0)
        back = ret_recv[chunk].reshape(128, 2048)
        w_hi = combines[chunk].astype(BF16)
        w_low = (combines[chunk] - w_hi.astype(F32)).astype(BF16)
        routed = (dot(w_hi, back) + dot(w_low, back)).reshape(2, 2, 8, 2048)
        if chunk == 1:
            shared_far = share_out[x, pl.ds(pairs[1] * 2, 2)]
            for i in (1, 3, 2):
                remote(share_send.at[0], share_recv.at[i], bs.at[i], br.at[i], other).wait()
                shared_far = shared_far + share_recv[i].astype(F32)
            routed = routed + jnp.where(is_own, shared_far[:, None], 0.0)
        first = pl.ds(pairs[chunk] * 2, 2)
        part[first] = routed
        lsend[first] = routed.astype(BF16)

    def hand(d):
        block = lsend.at[lines[d // 2], halves[d % 2]]
        return remote(block, lrecv.at[d], ls.at[d], lr.at[d], line(d))

    take(0)
    for d in (1, 3, 2):
        hand(d).start()
    remote(share_near, near_recv, bs.at[0], br.at[0], other).wait()
    for n in range(4):
        both = share_out[n, zl] + near_recv[n].astype(F32)
        share_sum[n] = both
        share_x[n] = both.astype(BF16)
    for i in (2, 1, 3):
        peer = lax.rem(x + i, 4)
        remote(
            share_x.at[peer], share_back.at[i], us.at[i], ur.at[i], dev(peer, y, zl, zh, c)
        ).start()
    take(1)
    for d in (5, 7, 4, 6):
        hand(d).start()
    result = hidden_s[zh] + part[zl, zh] + share_sum[x]
    for d in (2, 1, 3, 4, 6, 5, 7):
        hand(d).wait()
        result = result + lrecv[d].astype(F32)
    for i in (1, 3, 2):
        remote(share_x.at[lax.rem(x + i, 4)], share_back.at[i], us.at[i], ur.at[i], other).wait()
        result = result + share_back[i].astype(F32)
    out_ref[...] = result.astype(BF16)


def layer(vmem_args, more, weights):
    gate, up, down, sgate, sup, sdown = weights
    width = gate.shape[1]
    return pl.pallas_call(
        layer_kernel,
        name="layer",
        out_shape=jax.ShapeDtypeStruct((8, width), BF16),
        in_specs=[vmem_spec()] * len(vmem_args) + [hbm_spec()] * (len(more) + 6),
        out_specs=vmem_spec(),
        scratch_shapes=[VMEM(m.shape, BF16) for m in more]
        + [
            VMEM((GAP + gate.shape[0], width), BF16),
            VMEM(down.shape, BF16),
            VMEM((SGAP + sgate.shape[0], width), BF16),
            VMEM(sdown.shape, BF16),
            VMEM((4, 4, REQ, MSG), BF16),
            VMEM((3, REQ, MSG), BF16),
            VMEM((3, REQ, MSG), BF16),
            VMEM((2, 64, 128), BF16),
            VMEM((2, 64, width // 2), BF16),
            VMEM((2, 64, width // 2), BF16),
            VMEM((2, 4, 16, width // 2), F32),
            VMEM((2, 4, 16, width // 2), BF16),
            VMEM((2, 4, 16, width // 2), BF16),
            VMEM((2, 16, width // 2), BF16),
            VMEM((8, 2, 16, width // 2), BF16),
            VMEM((2, 8, width), F32),
            VMEM((4, 16, width), BF16),
            VMEM((2, 16, 8, width), BF16),
            VMEM((2, 2, 16, 8, width), BF16),
            VMEM((2, 128, width), F32),
            VMEM((2, 128, width), BF16),
            VMEM((2, 128, width), BF16),
            VMEM((2, 16, 8, width), BF16),
            VMEM((2, 16, 8, width), BF16),
            VMEM((4, 4, 8, width), BF16),
            VMEM((4, 4, 8, width), F32),
            VMEM((4, 8, width), BF16),
            VMEM((4, 8, width), BF16),
            VMEM((4, 2, 8, width), BF16),
            VMEM((4, 2, 8, width), BF16),
            VMEM((4, 8, width), F32),
            VMEM((4, 8, width), BF16),
            VMEM((4, 8, width), BF16),
            VMEM((4, 2, 8, width), F32),
            VMEM((4, 2, 8, width), BF16),
            VMEM((8, 8, width), BF16),
            DMA((12,)),
            DMA((4, 4)),
            DMA((4, 4)),
            DMA((3,)),
            DMA((3,)),
            DMA((2,)),
            DMA((2,)),
            DMA((2, 4)),
            DMA((2, 4)),
            DMA((8, 2)),
            DMA((8, 2)),
            DMA((2, 16)),
            DMA((2, 16)),
            DMA((2, 16)),
            DMA((2, 16)),
            DMA((2,)),
            DMA((2,)),
            DMA((2, 16)),
            DMA((2, 16)),
            DMA((4, 4)),
            DMA((4, 4)),
            DMA((4,)),
            DMA((4,)),
            DMA((4,)),
            DMA((4,)),
            DMA((8,)),
            DMA((8,)),
        ],
        compiler_params=pltpu.CompilerParams(
            collective_id=1, has_side_effects=True, vmem_limit_bytes=44 << 20
        ),
    )(*vmem_args, *map(stay, more), *map(stay, weights))


def on_device(
    query_nope,
    query_rope,
    absorb_weight,
    value_weight,
    output_weight,
    cache_latent,
    cache_rope,
    node_length,
    new_latent,
    new_rope,
    parent_node,
    leaf_node,
    residual,
    norm_gain,
    router_weight,
    routes,
    expert_gate,
    expert_up,
    expert_down,
    shared_gate,
    shared_up,
    shared_down,
):
    q_all, routes8, pick, place, lat, krope, absorb, value = gather(
        query_nope[:, 0, :],
        query_rope[:, 0, :].T,
        routes,
        leaf_node,
        parent_node,
        cache_latent,
        jnp.swapaxes(cache_rope, 1, 2),
        absorb_weight[0],
        value_weight[0],
    )
    msg = attend(
        node_length, q_all.reshape(16 * REQ, -1), pick, place, absorb, value, lat, krope
    )
    return layer(
        (msg.reshape(16, REQ, MSG), q_all, routes8, absorb, value),
        (norm_gain, new_latent, new_rope.T, residual, router_weight.T, output_weight),
        (
            expert_gate[0].T,
            expert_up[0].T,
            expert_down[0],
            shared_gate.T,
            shared_up.T,
            shared_down,
        ),
    )


def solution(mesh):
    in_specs = (
        P("group", "expert", None),
        P("group", "expert", None),
        P("expert", None, None),
        P("expert", None, None),
        P("expert", None),
        P("group", None, None),
        P("group", None, None),
        P("group"),
        P("group", None),
        P("group", None),
        P(),
        P(),
        P(("group", "expert"), None),
        P(),
        P(),
        P(("group", "expert"), None),
        P(("group", "expert"), None, None),
        P(("group", "expert"), None, None),
        P(("group", "expert"), None, None),
        P(None, "group"),
        P(None, "group"),
        P("group", None),
    )
    out_specs = P(("group", "expert"), None)
    return jax.shard_map(
        on_device, mesh=mesh, in_specs=in_specs, out_specs=out_specs, check_vma=False
    )
```

```python
import jax
import jax.numpy as jnp
from jax import lax
from jax.experimental import pallas as pl
from jax.experimental.pallas import tpu as pltpu
from jax.sharding import PartitionSpec as P

ROUTE_SCALE = 2.446
NEGATIVE = -1e30
EPSILON = 1e-06
LOG2_E = 1.4426950408889634
MESH = pl.DeviceIdType.MESH
F32 = jnp.float32
BF16 = jnp.bfloat16
VMEM = pltpu.VMEM
DMA = pltpu.SemaphoreType.DMA

REQ = 16
QT = 8
MSG = 1024 + 128


def vmem_spec():
    return pl.BlockSpec(memory_space=pltpu.VMEM)


def hbm_spec():
    return pl.BlockSpec(memory_space=pltpu.HBM)


def stay(x):
    return pltpu.with_memory_space_constraint(x, pltpu.HBM)


def start_loads(pairs, sem):
    loads = [pltpu.make_async_copy(src, dst, sem.at[i]) for i, (src, dst) in enumerate(pairs)]
    for load in loads:
        load.start()
    return loads


def coords():
    g = lax.axis_index("group")
    e = lax.axis_index("expert")
    zl, x = g // 4, g % 4
    y, zh, c = e // 4, (e % 4) // 2, e % 2
    return g, e, x, y, zl, zh, c


def dev(x, y, zl, zh, c):
    return (zl * 4 + x, y * 4 + zh * 2 + c)


def remote(src, dst, send, recv, device):
    return pltpu.make_async_remote_copy(
        src_ref=src,
        dst_ref=dst,
        send_sem=send,
        recv_sem=recv,
        device_id=device,
        device_id_type=MESH,
    )


def greet(barrier, device):
    pl.semaphore_signal(barrier, inc=1, device_id=device, device_id_type=MESH)


def dot(a, b):
    return jnp.dot(a, b, preferred_element_type=F32)


def eye_column(row):
    n = row.shape[1]
    same = lax.broadcasted_iota(jnp.int32, (n, n), 0) == lax.broadcasted_iota(jnp.int32, (n, n), 1)
    return jnp.sum(jnp.where(same, row, 0), axis=1, keepdims=True)


def flag(condition):
    return jnp.where(condition, 1.0, 0.0).astype(BF16)


def dot_nt(a, b):
    return lax.dot_general(a, b, (((1,), (1,)), ((), ())), preferred_element_type=F32)


def on_path(leaf_row, parent_col, node):
    nodes = parent_col.shape[0]
    ids = lax.broadcasted_iota(jnp.int32, (nodes, leaf_row.shape[1]), 0)
    mid = jnp.sum(jnp.where(leaf_row == ids, parent_col, 0), axis=0, keepdims=True)
    top = jnp.sum(jnp.where(mid == ids, parent_col, 0), axis=0, keepdims=True)
    return (leaf_row == node) | (mid == node) | (top == node)


def gather_kernel(
    nope_hbm,
    rope_hbm,
    routes_hbm,
    leaf_hbm,
    parent_hbm,
    lat_hbm,
    krope_hbm,
    absorb_hbm,
    value_hbm,
    qall,
    routes8,
    pick_ref,
    place_ref,
    lat_ref,
    krope_ref,
    absorb_ref,
    value_ref,
    nope_v,
    rope_v,
    routes_v,
    leaf_v,
    parent_v,
    mine,
    wsem,
    zq,
    zqr,
    xq,
    xqr,
    rs,
    rr,
):
    g, e, x, y, zl, zh, c = coords()
    loads = start_loads(
        [
            (nope_hbm, nope_v),
            (rope_hbm, rope_v),
            (routes_hbm, routes_v),
            (leaf_hbm, leaf_v),
            (parent_hbm, parent_v),
            (lat_hbm, lat_ref),
            (krope_hbm, krope_ref),
            (absorb_hbm, absorb_ref),
            (value_hbm, value_ref),
        ],
        wsem,
    )
    barrier = pltpu.get_barrier_semaphore()
    partner = dev(x, y, zl, 1 - zh, c)
    me = zl * 2 + zh
    for i in range(1, 4):
        greet(barrier, dev(lax.rem(x + i, 4), y, zl, zh, c))
        greet(barrier, dev(x, y, lax.rem(zl + i, 4), zh, c))
    for k in (1, 3, 5, 7):
        s = lax.rem(me + k, 8)
        greet(barrier, dev(x, y, s // 2, s % 2, c))

    rows = REQ * QT
    di = lax.broadcasted_iota(jnp.int32, (rows, rows), 0)
    si = lax.broadcasted_iota(jnp.int32, (rows, rows), 1)
    perm = flag(si == (di % REQ) * QT + di // REQ)
    for load in loads[:3]:
        load.wait()
    nope = dot(perm, nope_v[...]).astype(BF16)
    rope = dot_nt(perm, rope_v[...]).astype(BF16)
    qall[g] = jnp.concatenate(
        [nope[j * REQ : (j + 1) * REQ] for j in range(QT)]
        + [rope[j * REQ : (j + 1) * REQ] for j in range(QT)],
        axis=1,
    )
    mine[...] = jnp.zeros_like(mine)
    mine[:, 0 : routes_v.shape[1]] = routes_v[...]
    routes8[me] = mine[...]
    pl.semaphore_wait(barrier, 10)

    own = qall.at[g]
    for i in (1, 3, 2):
        remote(own, own, zq.at[i], zqr.at[i], dev(x, y, lax.rem(zl + i, 4), zh, c)).start()
    for k in (2, 1, 3):
        remote(own, own, xq.at[0, k], xqr.at[0, k], dev(lax.rem(x + k, 4), y, zl, zh, c)).start()
    for k in range(1, 8):
        s = lax.rem(me + k, 8)
        remote(mine, routes8.at[me], rs.at[k], rr.at[k], dev(x, y, s // 2, s % 2, c)).start()

    def pass_on(i):
        block = qall.at[lax.rem(zl - i + 4, 4) * 4 + x]
        remote(own, block, zq.at[i], zqr.at[i], partner).wait()
        for k in (2, 1, 3):
            remote(
                block, block, xq.at[i, k], xqr.at[i, k], dev(lax.rem(x + k, 4), y, zl, zh, c)
            ).start()

    pass_on(1)
    pass_on(3)
    pass_on(2)

    for load in loads[3:5]:
        load.wait()
    slots, _, requests = pick_ref.shape
    ids_0 = lax.broadcasted_iota(jnp.int32, (requests, requests), 0)
    ids_1 = lax.broadcasted_iota(jnp.int32, (requests, requests), 1)
    earlier = flag(ids_0 < ids_1)
    parent_col = eye_column(parent_v[...])
    for slot in range(slots):
        on_row = on_path(leaf_v[...], parent_col, g * slots + slot)
        row_f = jnp.where(on_row, 1.0, 0.0)
        rank_row = dot(jnp.broadcast_to(row_f, (8, requests)).astype(BF16), earlier)[0:1]
        rank_row = jnp.where(on_row, rank_row, -1.0)
        pick_ref[slot] = flag(rank_row.astype(jnp.int32) == ids_0)
        place_ref[slot] = flag(eye_column(rank_row).astype(jnp.int32) == ids_1)

    for load in loads[5:]:
        load.wait()
    for k in range(1, 8):
        s = lax.rem(me - k + 8, 8)
        remote(mine, routes8.at[s], rs.at[k], rr.at[k], partner).wait()
    for i in range(4):
        for k in (1, 3, 2):
            block = qall.at[lax.rem(zl - i + 4, 4) * 4 + lax.rem(x - k + 4, 4)]
            remote(own, block, xq.at[i, k], xqr.at[i, k], partner).wait()


def gather(nope, rope_t, routes, leaf, parent, lat, krope_t, absorb, value):
    requests = leaf.shape[0]
    slots = lat.shape[0]
    return pl.pallas_call(
        gather_kernel,
        name="gather_queries",
        out_shape=(
            jax.ShapeDtypeStruct((16, REQ, QT * 192), BF16),
            jax.ShapeDtypeStruct((8, 8, 128), jnp.int32),
            jax.ShapeDtypeStruct((slots, requests, requests), BF16),
            jax.ShapeDtypeStruct((slots, requests, requests), BF16),
            jax.ShapeDtypeStruct(lat.shape, BF16),
            jax.ShapeDtypeStruct(krope_t.shape, BF16),
            jax.ShapeDtypeStruct(absorb.shape, BF16),
            jax.ShapeDtypeStruct(value.shape, BF16),
        ),
        in_specs=[hbm_spec()] * 9,
        out_specs=(vmem_spec(),) * 8,
        scratch_shapes=[
            VMEM(nope.shape, BF16),
            VMEM(rope_t.shape, BF16),
            VMEM(routes.shape, jnp.int32),
            VMEM((1, requests), jnp.int32),
            VMEM((1, parent.shape[0]), jnp.int32),
            VMEM((8, 128), jnp.int32),
            DMA((9,)),
            DMA((4,)),
            DMA((4,)),
            DMA((4, 4)),
            DMA((4, 4)),
            DMA((8,)),
            DMA((8,)),
        ],
        compiler_params=pltpu.CompilerParams(
            collective_id=0, has_side_effects=True, vmem_limit_bytes=24 << 20
        ),
    )(
        *map(
            stay,
            (nope, rope_t, routes, leaf[None, :], parent[None, :], lat, krope_t, absorb, value),
        )
    )


TILE = 32
KEYS = 256


def split3(v):
    hi = v.astype(BF16)
    rest = v - hi.astype(F32)
    mid = rest.astype(BF16)
    low = (rest - mid.astype(F32)).astype(BF16)
    return hi.astype(F32), mid.astype(F32), low.astype(F32)


def pack_logs(logs):
    hi, mid, low = split3(logs)
    return hi + pltpu.roll(mid, 8, 1) + pltpu.roll(low, 16, 1)


def join_logs(tail):
    return tail + pltpu.roll(tail, 120, 1) + pltpu.roll(tail, 112, 1)


def attn_kernel(
    q_ref,
    pick_ref,
    place_ref,
    absorb_ref,
    value_ref,
    lat_ref,
    rope_ref,
    len_hbm,
    out_ref,
    len_ref,
    picked,
    done,
    wsem,
):
    (load,) = start_loads([(len_hbm, len_ref)], wsem)
    requests = q_ref.shape[0]
    slots, most = lat_ref.shape[0], lat_ref.shape[1]
    scaling = float(128 + 64) ** (-0.5)
    done[...] = jnp.zeros_like(done)
    lane = lax.broadcasted_iota(jnp.int32, (TILE, 128), 1)
    counts = []
    for slot in range(slots):
        picked[slot] = dot(pick_ref[slot], q_ref[...]).astype(BF16)
        counts.append(jnp.sum(pick_ref[slot].astype(F32)).astype(jnp.int32))
    load.wait()

    for slot in range(slots):
        length = len_ref[slot]

        def tile(keys, step, carry):
            here = pl.ds(pl.multiple_of(step * TILE, TILE), TILE)
            qt = picked[slot, here]
            nope = jnp.concatenate([qt[:, j * 128 : j * 128 + 128] for j in range(QT)], axis=0)
            rot = jnp.concatenate(
                [qt[:, 1024 + j * 64 : 1024 + j * 64 + 64] for j in range(QT)], axis=0
            )
            lat = dot(nope, absorb_ref[...]).astype(BF16)
            scores = dot_nt(lat, lat_ref[slot, :keys]) + dot(rot, rope_ref[slot, :, :keys])
            scores = scores * (scaling * LOG2_E)
            inside = keys - KEYS
            positions = lax.broadcasted_iota(jnp.int32, (1, KEYS), 1) + inside
            last = jnp.where(positions < length, scores[:, inside:], NEGATIVE)
            if inside:
                scores = jnp.concatenate([scores[:, :inside], last], axis=1)
            else:
                scores = last
            top = jnp.max(scores, axis=1, keepdims=True)
            weights = jnp.exp2(scores - top).astype(BF16)
            total = jnp.sum(weights.astype(F32), axis=1, keepdims=True)
            summed = dot(weights, lat_ref[slot, :keys])
            attended = (summed / total).astype(BF16)
            valued = dot(attended, value_ref[...]).astype(BF16)
            log_sum = top * (1.0 / LOG2_E) + jnp.log(total)
            logs = jnp.zeros((TILE, 128), F32)
            for j in range(QT):
                logs = jnp.where(lane == j, log_sum[j * TILE : (j + 1) * TILE], logs)
            tail = jnp.where((lane >= 24) & (lane < 32), 1.0, pack_logs(logs))
            done[slot, here] = jnp.concatenate(
                [valued[j * TILE : (j + 1) * TILE] for j in range(QT)] + [tail.astype(BF16)],
                axis=1,
            )
            return carry

        tiles = (counts[slot] + TILE - 1) // TILE
        for keys in range(KEYS, most + 1, KEYS):

            @pl.when((length > keys - KEYS) & (length <= keys))
            def _():
                lax.fori_loop(0, tiles, lambda step, carry: tile(keys, step, carry), 0)

    acc = [dot(place_ref[s], done[s]) for s in range(slots)]
    tails = [a[:, 1024:] for a in acc]
    logs = [jnp.where(pltpu.roll(t, 104, 1) > 0.5, join_logs(t), NEGATIVE) for t in tails]
    top = logs[0]
    for s in range(1, slots):
        top = jnp.maximum(top, logs[s])
    shares = [jnp.exp(v - top) for v in logs]
    total = shares[0]
    for s in range(1, slots):
        total = total + shares[s]
    shares = [v / total for v in shares]
    for j in range(QT):
        out = 0.0
        for s in range(slots):
            out = out + shares[s][:, j : j + 1] * acc[s][:, j * 128 : j * 128 + 128]
        out_ref[:, j * 128 : j * 128 + 128] = out.astype(BF16)
    lanes = lax.broadcasted_iota(jnp.int32, (requests, 128), 1)
    log_sum = jnp.where(lanes < QT, top + jnp.log(total), 0.0)
    out_ref[:, 1024:] = pack_logs(log_sum).astype(BF16)


def attend(node_length, q_all, pick, place, absorb, value, lat, rope_t):
    requests = q_all.shape[0]
    slots = lat.shape[0]
    return pl.pallas_call(
        attn_kernel,
        name="attend_nodes",
        out_shape=jax.ShapeDtypeStruct((requests, MSG), BF16),
        in_specs=[vmem_spec()] * 7 + [hbm_spec()],
        out_specs=vmem_spec(),
        scratch_shapes=[
            pltpu.SMEM(node_length.shape, jnp.int32),
            VMEM((slots, requests, q_all.shape[1]), BF16),
            VMEM((slots, requests, MSG), BF16),
            DMA((1,)),
        ],
        compiler_params=pltpu.CompilerParams(vmem_limit_bytes=32 << 20),
    )(q_all, pick, place, absorb, value, lat, rope_t, stay(node_length))


OFFSETS = sorted(
    [(i, j) for i in range(4) for j in range(4) if i or j],
    key=lambda o: -min(o[0], 4 - o[0]) - min(o[1], 4 - o[1]),
)

GAP = 384
SGAP = 256


def layer_kernel(
    msg_ref,
    q_ref,
    routes_ref,
    absorb_ref,
    value_ref,
    gain_hbm,
    newlat_hbm,
    newrope_hbm,
    resid_hbm,
    router_hbm,
    outw_hbm,
    gate_hbm,
    up_hbm,
    down_hbm,
    sgate_hbm,
    sup_hbm,
    sdown_hbm,
    out_ref,
    gain_ref,
    newlat_ref,
    newrope_ref,
    resid_ref,
    router_ref,
    outw_ref,
    gate_up,
    down_w,
    sgate_up,
    sdown_w,
    got,
    got_z,
    blended,
    valued_s,
    csend,
    crecv,
    acc,
    ysend,
    yrecv,
    zsend,
    zrecv,
    hidden_s,
    normed,
    packed,
    arrived,
    own_out,
    cross_send,
    cross_recv,
    ret_send,
    ret_recv,
    share_in,
    share_out,
    share_near,
    near_recv,
    share_send,
    share_recv,
    share_sum,
    share_x,
    share_back,
    part,
    lsend,
    lrecv,
    wsem,
    ms,
    mr,
    gs,
    gr,
    cs,
    cr,
    ys,
    yr,
    ns,
    nr,
    ds,
    dr,
    fs,
    fr,
    os_,
    or_,
    rs,
    rr,
    xs,
    xr,
    bs,
    br,
    us,
    ur,
    ls,
    lr,
):
    g, e, x, y, zl, zh, c = coords()
    mine = x * 4 + y
    ff = gate_hbm.shape[0]
    sff = sgate_hbm.shape[0]
    barrier = pltpu.get_barrier_semaphore()

    def source(i):
        return lax.rem(x - i // 4 + 4, 4) * 4 + lax.rem(y - i % 4 + 4, 4)

    other = dev(x, y, zl, zh, 1 - c)
    partner = dev(x, y, zl, 1 - zh, c)
    greet(barrier, other)
    greet(barrier, partner)
    for i in range(4):
        for k in range(1, 4):
            greet(barrier, dev(lax.rem(x + i, 4), lax.rem(y + k, 4), zl, zh, c))
    lines = (zl, zl + 1 - 2 * (zl % 2), zl + 2 - 4 * (zl // 2), 3 - zl)
    halves = (zh, 1 - zh)

    def line(d):
        return dev(x, y, lines[d // 2], halves[d % 2], c)

    for d in range(2, 8):
        greet(barrier, line(d))
    for i in range(1, 4):
        greet(barrier, dev(lax.rem(x + i, 4), y, zl, zh, c))
    loads = start_loads(
        [
            (gain_hbm, gain_ref),
            (newlat_hbm, newlat_ref),
            (newrope_hbm, newrope_ref),
            (resid_hbm, resid_ref),
            (router_hbm, router_ref),
            (outw_hbm, outw_ref),
            (gate_hbm, gate_up.at[pl.ds(0, ff)]),
            (up_hbm, gate_up.at[pl.ds(GAP, ff)]),
            (down_hbm, down_w),
            (sgate_hbm, sgate_up.at[pl.ds(0, sff)]),
            (sup_hbm, sgate_up.at[pl.ds(SGAP, sff)]),
            (sdown_hbm, sdown_w),
        ],
        wsem,
    )
    gate_up[ff:GAP] = jnp.zeros((GAP - ff, gate_up.shape[1]), BF16)
    sgate_up[sff:SGAP] = jnp.zeros((SGAP - sff, sgate_up.shape[1]), BF16)

    pl.semaphore_wait(barrier, 23)

    homes = (lines[2], lines[3], lines[1], zl)
    for n in range(4):
        for i in (2, 1, 3):
            peer = lax.rem(x + i, 4)
            remote(
                msg_ref.at[homes[n] * 4 + peer],
                got.at[n, i],
                ms.at[n, i],
                mr.at[n, i],
                dev(peer, y, zl, zh, c),
            ).start()

    scaling = float(128 + 64) ** (-0.5)
    for load in loads[:6]:
        load.wait()
    q = q_ref[g]
    nope = jnp.concatenate([q[:, j * 128 : j * 128 + 128] for j in range(QT)], axis=0)
    rot = jnp.concatenate([q[:, 1024 + j * 64 : 1024 + j * 64 + 64] for j in range(QT)], axis=0)
    lat = dot(nope, absorb_ref[...]).astype(BF16)
    scores = dot_nt(lat, newlat_ref[...]) + dot(rot, newrope_ref[...])
    rows = REQ * QT
    qi = lax.broadcasted_iota(jnp.int32, (rows, rows), 0)
    ki = lax.broadcasted_iota(jnp.int32, (rows, rows), 1)
    usable = ((qi % REQ) == (ki // QT)) & ((ki % QT) <= (qi // REQ))
    scores = jnp.where(usable, scores * scaling, NEGATIVE)
    top = jnp.max(scores, axis=1, keepdims=True)
    weights = jnp.where(usable, jnp.exp(scores - top), 0.0).astype(BF16)
    total = jnp.sum(weights.astype(F32), axis=1, keepdims=True)
    summed = dot(weights, newlat_ref[...]) / total
    new_valued = dot(summed.astype(BF16), value_ref[...])
    new_log = top + jnp.log(total)

    def blend(parts, more=None):
        logs = [join_logs(p[:, 1024:].astype(F32)) for p in parts]
        if more is not None:
            logs.append(more[1])
        peak = logs[0]
        for v in logs[1:]:
            peak = jnp.maximum(peak, v)
        shares = [jnp.exp(v - peak) for v in logs]
        whole = shares[0]
        for v in shares[1:]:
            whole = whole + v
        shares = [v / whole for v in shares]
        values = []
        for j in range(QT):
            value = 0.0
            for p, share in zip(parts, shares):
                value = value + share[:, j : j + 1] * p[:, j * 128 : j * 128 + 128].astype(F32)
            if more is not None:
                value = value + shares[-1][:, j : j + 1] * more[0][j * REQ : (j + 1) * REQ]
            values.append(value.astype(BF16))
        return values, peak + jnp.log(whole)

    def along_x(n):
        for i in (1, 3, 2):
            src = msg_ref.at[homes[n] * 4 + lax.rem(x + i, 4)]
            remote(src, got.at[n, i], ms.at[n, i], mr.at[n, i], other).wait()
        return [msg_ref[homes[n] * 4 + x]] + [got[n, i] for i in range(1, 4)]

    lane = lax.broadcasted_iota(jnp.int32, (REQ, 128), 1)

    def along_z(n):
        return remote(
            blended.at[n], got_z.at[n], gs.at[n], gr.at[n], dev(x, y, homes[n], zh, c)
        )

    for n in range(3):
        values, log_sum = blend(along_x(n))
        tail = pack_logs(jnp.where(lane < QT, log_sum, 0.0)).astype(BF16)
        blended[n] = jnp.concatenate(values + [tail], axis=1)
        along_z(n).start()

    experts = router_ref.shape[0]
    pairs = (zl // 2, 1 - zl // 2)
    picks, masks = [], []
    for q_ in range(2):
        routes = routes_ref[pl.ds(pairs[q_] * 4, 4)].reshape(32, 128)
        ids = lax.broadcasted_iota(jnp.int32, (32, experts), 1)
        chosen = jnp.zeros((32, experts), F32)
        for k in range(6):
            chosen = jnp.where(routes[:, k : k + 1] == ids, 1.0, chosen)
        ti = lax.broadcasted_iota(jnp.int32, (32, 32), 0)
        tj = lax.broadcasted_iota(jnp.int32, (32, 32), 1)
        before = flag((ti // 8 == tj // 8) & (tj < ti))
        rank = jnp.where(chosen > 0.0, dot(before, chosen.astype(BF16)), -1.0)
        col = lax.broadcasted_iota(jnp.int32, (experts, 128), 1)
        spread = flag(lax.broadcasted_iota(jnp.int32, (experts, 128), 0) == zl * 16 + col // 8)
        spread_rank = dot(rank.astype(BF16), spread)
        ct = lax.broadcasted_iota(jnp.int32, (32, 128), 1)
        rt = lax.broadcasted_iota(jnp.int32, (32, 128), 0)
        pick = jnp.where(
            (spread_rank == (ct % 2).astype(F32)) & (rt // 8 == (ct // 2) % 4), 1.0, 0.0
        )
        picks.append(pick)
        masks.append(chosen)

    here = along_x(3)
    logs = jnp.zeros((REQ, 128), F32)
    for j in range(QT):
        logs = jnp.where(lane == j, new_log[j * REQ : (j + 1) * REQ], logs)
    for n in (2, 0, 1):
        along_z(n).wait()
    pieces, _ = blend(here + [got_z[n] for n in range(3)], (new_valued, logs))
    valued = jnp.concatenate(pieces, axis=0)
    di = lax.broadcasted_iota(jnp.int32, (rows, rows), 0)
    si = lax.broadcasted_iota(jnp.int32, (rows, rows), 1)
    req = ((di % 64) // 16) * 4 + ((di % 16) // 8) * 2 + di // 64
    perm = flag(si == (di % 8) * REQ + req)
    valued_s[...] = dot(perm, valued).astype(BF16).reshape(2, 64, 128)
    half = outw_ref.shape[1] // 2
    cols = [pl.ds(h * half, half) for h in range(2)]
    own_8 = lax.broadcasted_iota(jnp.int32, (16, 1), 0) // 8 == zh
    for h in range(2):
        csend[h] = dot(valued_s[1 - c], outw_ref[:, cols[h]]).astype(BF16)
        remote(csend.at[h], crecv.at[h], cs.at[h], cr.at[h], other).start()
    own = [dot(valued_s[c], outw_ref[:, cols[h]]) for h in range(2)]
    for h in range(2):
        remote(csend.at[h], crecv.at[h], cs.at[h], cr.at[h], other).wait()
        acc[h] = (own[h] + crecv[h].astype(F32)).reshape(4, 16, half)
        ysend[h] = acc[h].astype(BF16)
        for i in (2, 1, 3):
            peer = lax.rem(y + i, 4)
            remote(
                ysend.at[h, peer],
                yrecv.at[h, i],
                ys.at[h, i],
                yr.at[h, i],
                dev(x, peer, zl, zh, c),
            ).start()
    sums = []
    for h in range(2):
        row = acc[h, y]
        for i in (1, 3, 2):
            remote(ysend.at[h, 0], yrecv.at[h, i], ys.at[h, i], yr.at[h, i], other).wait()
            row = row + yrecv[h, i].astype(F32)
        resid = resid_ref[:, cols[h]].astype(F32)
        row = row + jnp.where(own_8, jnp.concatenate([resid, resid], axis=0), 0.0)
        zsend[h] = row.astype(BF16)
        sums.append(row)
        for d in (1, 3, 2):
            remote(zsend.at[h], zrecv.at[d, h], ns.at[d, h], nr.at[d, h], line(d)).start()
    for h in range(2):
        for d in (5, 7, 4, 6):
            remote(zsend.at[h], zrecv.at[d, h], ns.at[d, h], nr.at[d, h], line(d)).start()
    total_row = jnp.concatenate(sums, axis=1)

    def column(d):
        for h in range(2):
            remote(zsend.at[h], zrecv.at[d, h], ns.at[d, h], nr.at[d, h], other).wait()
        return jnp.concatenate([zrecv[d, 0], zrecv[d, 1]], axis=1).astype(F32)

    gain = gain_ref[...].reshape(1, gain_ref.shape[0]).astype(F32)

    def norm(hidden):
        square = jnp.mean(hidden * hidden, axis=1, keepdims=True)
        return (hidden * lax.rsqrt(square + EPSILON) * gain).astype(BF16)

    hidden = total_row + column(1)
    hidden_s[...] = hidden.reshape(2, 8, 2048)
    normed[zl] = norm(hidden)
    share_in[x, zl] = normed[zl].reshape(2, 8, 2048)[0]

    @pl.when(zh == 1)
    def _():
        share_in[x, zl] = normed[zl].reshape(2, 8, 2048)[1]

    for i in (2, 1, 3):
        block = share_in.at[x, zl]
        peer = dev(lax.rem(x + i, 4), y, zl, zh, c)
        remote(block, block, xs.at[0, i], xr.at[0, i], peer).start()

    def pack(chunk):
        tokens = normed[pl.ds(pairs[chunk] * 2, 2)].reshape(32, 2048)
        packed[chunk] = (
            lax.dot_general(
                picks[chunk].astype(BF16),
                tokens,
                (((0,), (0,)), ((), ())),
                preferred_element_type=F32,
            )
            .astype(BF16)
            .reshape(16, 8, 2048)
        )

        for dx, dy in OFFSETS:
            to_x, to_y = lax.rem(x + dx, 4), lax.rem(y + dy, 4)
            remote(
                packed.at[chunk, to_x * 4 + to_y],
                arrived.at[chunk, c, mine],
                ds.at[chunk, dx * 4 + dy],
                dr.at[chunk, dx * 4 + dy],
                dev(to_x, to_y, zl, zh, c),
            ).start()
        arrived[chunk, c, mine] = packed[chunk, mine]
        here = arrived.at[chunk, c, mine]
        remote(here, here, fs.at[chunk, 0], fr.at[chunk, 0], other).start()

    def weigh(chunk):
        tokens = normed[pl.ds(pairs[chunk] * 2, 2)].reshape(32, 2048)
        logits = dot_nt(tokens, router_ref[...])
        sigma = jax.nn.sigmoid(logits) * masks[chunk]
        route_w = ROUTE_SCALE * sigma / jnp.sum(sigma, axis=1, keepdims=True)
        col = lax.broadcasted_iota(jnp.int32, (experts, 128), 1)
        spread = flag(lax.broadcasted_iota(jnp.int32, (experts, 128), 0) == zl * 16 + col // 8)
        w_hi, w_mid, w_low = split3(route_w)
        return (
            dot(w_hi.astype(BF16), spread)
            + dot(w_mid.astype(BF16), spread)
            + dot(w_low.astype(BF16), spread)
        ) * picks[chunk]

    normed[lines[1]] = norm(column(2) + column(3))
    pack(0)
    normed[lines[2]] = norm(column(4) + column(5))
    normed[lines[3]] = norm(column(6) + column(7))
    pack(1)
    for d in range(1, 4):
        both = normed[lines[d]].reshape(2, 8, 2048)
        share_in[x, lines[d]] = jnp.where(zh == 0, both[0], both[1])
    for i in (1, 3, 2):
        block = share_in.at[lax.rem(x - i + 4, 4), zl]
        remote(share_in.at[x, zl], block, xs.at[0, i], xr.at[0, i], other).wait()
        for d in range(1, 4):
            remote(block, block, xs.at[d, i], xr.at[d, i], line(2 * d)).start()

    def forward(chunk):
        def step(i, carry):
            src = source(i)
            block = arrived.at[chunk, c, src]
            remote(packed.at[chunk, src], block, ds.at[chunk, i], dr.at[chunk, i], other).wait()
            remote(block, block, fs.at[chunk, i], fr.at[chunk, i], other).start()
            return carry

        lax.fori_loop(1, 16, step, 0)

    def crossed(chunk):
        def step(i, carry):
            src = source(i)
            block = arrived.at[chunk, c, src]
            remote(
                block, arrived.at[chunk, 1 - c, src], fs.at[chunk, i], fr.at[chunk, i], other
            ).wait()
            return carry

        lax.fori_loop(0, 16, step, 0)

    def ffn(rows_in, both_w, gap, units, down):
        val = dot_nt(rows_in, both_w[...])
        hidden = (jax.nn.silu(val[:, :units]) * val[:, gap : gap + units]).astype(BF16)
        return dot(hidden, down[...])

    def routed_ffn(chunk):
        out = ffn(arrived[chunk].reshape(256, 2048), gate_up, GAP, ff, down_w)
        first, second = out[:128], out[128:]
        own_out[chunk] = jnp.where(c == 0, first, second)
        cross_send[chunk] = jnp.where(c == 0, second, first).astype(BF16)
        remote(
            cross_send.at[chunk], cross_recv.at[chunk], os_.at[chunk], or_.at[chunk], other
        ).start()

    def give(chunk):
        remote(
            cross_send.at[chunk], cross_recv.at[chunk], os_.at[chunk], or_.at[chunk], other
        ).wait()
        ret_send[chunk] = (
            (own_out[chunk] + cross_recv[chunk].astype(F32)).astype(BF16).reshape(16, 8, 2048)
        )

        for dx, dy in OFFSETS:
            to_x, to_y = lax.rem(x + dx, 4), lax.rem(y + dy, 4)
            remote(
                ret_send.at[chunk, to_x * 4 + to_y],
                ret_recv.at[chunk, mine],
                rs.at[chunk, dx * 4 + dy],
                rr.at[chunk, dx * 4 + dy],
                dev(to_x, to_y, zl, zh, c),
            ).start()
        ret_recv[chunk, mine] = ret_send[chunk, mine]

    forward(0)
    for load in loads[6:9]:
        load.wait()
    crossed(0)
    routed_ffn(0)
    give(0)
    forward(1)
    crossed(1)
    routed_ffn(1)

    give(1)

    for load in loads[9:]:
        load.wait()
    for i in (1, 3, 2):
        src = lax.rem(x - i + 4, 4)
        for d in range(1, 4):
            remote(
                share_in.at[src, zl], share_in.at[src, lines[d]], xs.at[d, i], xr.at[d, i], other
            ).wait()
    shared = ffn(share_in[...].reshape(128, 2048), sgate_up, SGAP, sff, sdown_w)
    share_out[...] = shared.reshape(4, 4, 8, 2048)
    for n in range(4):
        share_near[n] = share_out[n, lines[1]].astype(BF16)
        share_send[n] = share_out[n, pl.ds(pairs[1] * 2, 2)].astype(BF16)
    remote(share_near, near_recv, bs.at[0], br.at[0], line(2)).start()
    for i in (2, 1, 3):
        peer = lax.rem(x + i, 4)
        remote(
            share_send.at[peer], share_recv.at[i], bs.at[i], br.at[i], dev(peer, y, zl, zh, c)
        ).start()

    combines = [weigh(chunk) for chunk in range(2)]

    is_own = lax.broadcasted_iota(jnp.int32, (2, 2, 8, 2048), 1) == zh

    def take(chunk):
        def step(i, carry):
            src = source(i)
            remote(
                ret_send.at[chunk, src],
                ret_recv.at[chunk, src],
                rs.at[chunk, i],
                rr.at[chunk, i],
                other,
            ).wait()
            return carry

        lax.fori_loop(1, 16, step, 0)
        back = ret_recv[chunk].reshape(128, 2048)
        w_hi = combines[chunk].astype(BF16)
        w_low = (combines[chunk] - w_hi.astype(F32)).astype(BF16)
        routed = (dot(w_hi, back) + dot(w_low, back)).reshape(2, 2, 8, 2048)
        if chunk == 1:
            shared_far = share_out[x, pl.ds(pairs[1] * 2, 2)]
            for i in (1, 3, 2):
                remote(share_send.at[0], share_recv.at[i], bs.at[i], br.at[i], other).wait()
                shared_far = shared_far + share_recv[i].astype(F32)
            routed = routed + jnp.where(is_own, shared_far[:, None], 0.0)
        first = pl.ds(pairs[chunk] * 2, 2)
        part[first] = routed
        lsend[first] = routed.astype(BF16)

    def hand(d):
        block = lsend.at[lines[d // 2], halves[d % 2]]
        return remote(block, lrecv.at[d], ls.at[d], lr.at[d], line(d))

    take(0)
    for d in (1, 3, 2):
        hand(d).start()
    remote(share_near, near_recv, bs.at[0], br.at[0], other).wait()
    for n in range(4):
        both = share_out[n, zl] + near_recv[n].astype(F32)
        share_sum[n] = both
        share_x[n] = both.astype(BF16)
    for i in (2, 1, 3):
        peer = lax.rem(x + i, 4)
        remote(
            share_x.at[peer], share_back.at[i], us.at[i], ur.at[i], dev(peer, y, zl, zh, c)
        ).start()
    take(1)
    for d in (5, 7, 4, 6):
        hand(d).start()
    result = hidden_s[zh] + part[zl, zh] + share_sum[x]
    for d in (2, 1, 3, 4, 6, 5, 7):
        hand(d).wait()
        result = result + lrecv[d].astype(F32)
    for i in (1, 3, 2):
        remote(share_x.at[lax.rem(x + i, 4)], share_back.at[i], us.at[i], ur.at[i], other).wait()
        result = result + share_back[i].astype(F32)
    out_ref[...] = result.astype(BF16)


def layer(vmem_args, more, weights):
    gate, up, down, sgate, sup, sdown = weights
    width = gate.shape[1]
    return pl.pallas_call(
        layer_kernel,
        name="layer",
        out_shape=jax.ShapeDtypeStruct((8, width), BF16),
        in_specs=[vmem_spec()] * len(vmem_args) + [hbm_spec()] * (len(more) + 6),
        out_specs=vmem_spec(),
        scratch_shapes=[VMEM(m.shape, BF16) for m in more]
        + [
            VMEM((GAP + gate.shape[0], width), BF16),
            VMEM(down.shape, BF16),
            VMEM((SGAP + sgate.shape[0], width), BF16),
            VMEM(sdown.shape, BF16),
            VMEM((4, 4, REQ, MSG), BF16),
            VMEM((3, REQ, MSG), BF16),
            VMEM((3, REQ, MSG), BF16),
            VMEM((2, 64, 128), BF16),
            VMEM((2, 64, width // 2), BF16),
            VMEM((2, 64, width // 2), BF16),
            VMEM((2, 4, 16, width // 2), F32),
            VMEM((2, 4, 16, width // 2), BF16),
            VMEM((2, 4, 16, width // 2), BF16),
            VMEM((2, 16, width // 2), BF16),
            VMEM((8, 2, 16, width // 2), BF16),
            VMEM((2, 8, width), F32),
            VMEM((4, 16, width), BF16),
            VMEM((2, 16, 8, width), BF16),
            VMEM((2, 2, 16, 8, width), BF16),
            VMEM((2, 128, width), F32),
            VMEM((2, 128, width), BF16),
            VMEM((2, 128, width), BF16),
            VMEM((2, 16, 8, width), BF16),
            VMEM((2, 16, 8, width), BF16),
            VMEM((4, 4, 8, width), BF16),
            VMEM((4, 4, 8, width), F32),
            VMEM((4, 8, width), BF16),
            VMEM((4, 8, width), BF16),
            VMEM((4, 2, 8, width), BF16),
            VMEM((4, 2, 8, width), BF16),
            VMEM((4, 8, width), F32),
            VMEM((4, 8, width), BF16),
            VMEM((4, 8, width), BF16),
            VMEM((4, 2, 8, width), F32),
            VMEM((4, 2, 8, width), BF16),
            VMEM((8, 8, width), BF16),
            DMA((12,)),
            DMA((4, 4)),
            DMA((4, 4)),
            DMA((3,)),
            DMA((3,)),
            DMA((2,)),
            DMA((2,)),
            DMA((2, 4)),
            DMA((2, 4)),
            DMA((8, 2)),
            DMA((8, 2)),
            DMA((2, 16)),
            DMA((2, 16)),
            DMA((2, 16)),
            DMA((2, 16)),
            DMA((2,)),
            DMA((2,)),
            DMA((2, 16)),
            DMA((2, 16)),
            DMA((4, 4)),
            DMA((4, 4)),
            DMA((4,)),
            DMA((4,)),
            DMA((4,)),
            DMA((4,)),
            DMA((8,)),
            DMA((8,)),
        ],
        compiler_params=pltpu.CompilerParams(
            collective_id=1, has_side_effects=True, vmem_limit_bytes=44 << 20
        ),
    )(*vmem_args, *map(stay, more), *map(stay, weights))


def on_device(
    query_nope,
    query_rope,
    absorb_weight,
    value_weight,
    output_weight,
    cache_latent,
    cache_rope,
    node_length,
    new_latent,
    new_rope,
    parent_node,
    leaf_node,
    residual,
    norm_gain,
    router_weight,
    routes,
    expert_gate,
    expert_up,
    expert_down,
    shared_gate,
    shared_up,
    shared_down,
):
    q_all, routes8, pick, place, lat, krope, absorb, value = gather(
        query_nope[:, 0, :],
        query_rope[:, 0, :].T,
        routes,
        leaf_node,
        parent_node,
        cache_latent,
        jnp.swapaxes(cache_rope, 1, 2),
        absorb_weight[0],
        value_weight[0],
    )
    msg = attend(
        node_length, q_all.reshape(16 * REQ, -1), pick, place, absorb, value, lat, krope
    )
    return layer(
        (msg.reshape(16, REQ, MSG), q_all, routes8, absorb, value),
        (norm_gain, new_latent, new_rope.T, residual, router_weight.T, output_weight),
        (
            expert_gate[0].T,
            expert_up[0].T,
            expert_down[0],
            shared_gate.T,
            shared_up.T,
            shared_down,
        ),
    )


def solution(mesh):
    in_specs = (
        P("group", "expert", None),
        P("group", "expert", None),
        P("expert", None, None),
        P("expert", None, None),
        P("expert", None),
        P("group", None, None),
        P("group", None, None),
        P("group"),
        P("group", None),
        P("group", None),
        P(),
        P(),
        P(("group", "expert"), None),
        P(),
        P(),
        P(("group", "expert"), None),
        P(("group", "expert"), None, None),
        P(("group", "expert"), None, None),
        P(("group", "expert"), None, None),
        P(None, "group"),
        P(None, "group"),
        P("group", None),
    )
    out_specs = P(("group", "expert"), None)
    return jax.shard_map(
        on_device, mesh=mesh, in_specs=in_specs, out_specs=out_specs, check_vma=False
    )
```
